32 devices in a mesh: dp: 4 (over x, core), seq: 8 (over z, y).
Axes of the slice: x: 2, y: 2, z: 4, core: 2. Of those that a mesh axis runs over, the one named last changes fastest.
Arguments:
- inputs: bfloat16 [16, 1024, 768], P('dp', 'seq'), may hold values from -6 to 6
- memory: bfloat16 [16, 64, 768], P('dp', 'seq'), may hold values from -6 to 6
- patch_count: int32 [16], P('dp'), may hold values from 16 to 64, as said below
- cotangent: bfloat16 [16, 1024, 768], P('dp', 'seq'), may hold values from -6 to 6
- norm_self: float32 [768], replicated, may hold values from 0.5 to 1.5
- w_query: bfloat16 [768, 768], replicated, may hold values from -0.21875 to 0.21875
- w_key: bfloat16 [768, 768], replicated, may hold values from -0.21875 to 0.21875
- w_value: bfloat16 [768, 768], replicated, may hold values from -0.21875 to 0.21875
- w_out: bfloat16 [768, 768], replicated, may hold values from -3.0625 to 3.0625
- norm_cross: float32 [768], replicated, may hold values from 0.5 to 1.5
- c_query: bfloat16 [768, 768], replicated, may hold values from -0.21875 to 0.21875
- c_key: bfloat16 [768, 768], replicated, may hold values from -0.21875 to 0.21875
- c_value: bfloat16 [768, 768], replicated, may hold values from -0.21875 to 0.21875
- c_out: bfloat16 [768, 768], replicated, may hold values from -0.8125 to 0.8125
- norm_ffn: float32 [768], replicated, may hold values from 0.5 to 1.5
- w_gate: bfloat16 [768, 2048], replicated, may hold values from -0.21875 to 0.21875
- w_up: bfloat16 [768, 2048], replicated, may hold values from -0.21875 to 0.21875
- w_down: bfloat16 [2048, 768], replicated, may hold values from -0.125 to 0.125
Outputs:
- block_output: float32 [16, 1024, 768], P('dp', 'seq')
- input_grad: float32 [16, 1024, 768], P('dp', 'seq')
- memory_grad: float32 [16, 64, 768], P('dp', 'seq')
- grad_norm_self: float32 [768], P('seq')
- grad_w_query: float32 [768, 768], P('seq', 'dp')
- grad_w_key: float32 [768, 768], P('seq', 'dp')
- grad_w_value: float32 [768, 768], P('seq', 'dp')
- grad_w_out: float32 [768, 768], P('seq', 'dp')
- grad_norm_cross: float32 [768], P('seq')
- grad_c_query: float32 [768, 768], P('seq', 'dp')
- grad_c_key: float32 [768, 768], P('seq', 'dp')
- grad_c_value: float32 [768, 768], P('seq', 'dp')
- grad_c_out: float32 [768, 768], P('seq', 'dp')
- grad_norm_ffn: float32 [768], P('seq')
- grad_w_gate: float32 [768, 2048], P('seq', 'dp')
- grad_w_up: float32 [768, 2048], P('seq', 'dp')
- grad_w_down: float32 [2048, 768], P('seq', 'dp')
The draws below stay inside these ranges and needn't reach their ends.
Inputs may be any that keep to these rules, and one draw needn't show every extreme that they name: Patches 0 to patch_count - 1 of a chart are valid, the others masked; some chart has all 64 valid and some has 16.
All inputs are finite; a program needn't handle non-finite values.
Results may differ from the reference program's by a relative error of at most 0.02.
Values may be sent and summed in bfloat16 or wider, within the bound.
No kernel may reach another device: no remote copies, remote signals or barrier semaphores. Data moves between devices by JAX's collectives and lax.ppermute only.
A program may use at most 896 MiB of HBM per device.

```python
import math
import jax
import jax.numpy as jnp
from jax import lax

D = 768
H = 12
HD = 64
FF = 2048
SEQ_LEN = 1024
PATCHES = 64
CHARTS = 16


def draw_patch_count(key, part):
    first, second = jax.random.split(jax.random.fold_in(key, 7))
    counts = jax.random.randint(first, (CHARTS,), PATCHES // 4, PATCHES + 1, dtype=jnp.int32)
    order = jax.random.permutation(second, CHARTS)
    counts = counts.at[order[0]].set(PATCHES)
    counts = counts.at[order[1]].set(PATCHES // 4)
    return counts


def block_levels(key, extent, pieces, smallest, high):
    def one(position, parts):
        draws = jax.random.uniform(jax.random.fold_in(jax.random.fold_in(key, 6), position), (parts,), jnp.float32, smallest / len(pieces), high / len(pieces))
        return jnp.repeat(jnp.exp(draws), extent[position] // parts).reshape((-1,) + (1,) * (len(extent) - position - 1))

    level = one(*pieces[0])
    for cut in pieces[1:]:
        level = level * one(*cut)
    return level


def scatter_about(rng, dims, deviation, reach, cuts=(), held_as=jnp.bfloat16):
    values = jax.random.normal(rng, dims, jnp.float32) * deviation
    if len(cuts) > 0:
        values = block_levels(rng, dims, cuts, -0.22, 0.18) * values
    return jnp.clip(values, min=-reach, max=reach).astype(held_as)


def setup_inputs(seed: int = 0) -> dict:
    seeds = jax.random.split(jax.random.key(seed), 19)
    return {
        "inputs": scatter_about(seeds[0], (CHARTS, SEQ_LEN, D), 1.0, 6.0, ((0, 4), (1, 8))),
        "memory": scatter_about(seeds[1], (CHARTS, PATCHES, D), 1.0, 6.0, ((0, 4), (1, 8))),
        "patch_count": draw_patch_count(jax.random.fold_in(seeds[18], 71), 0),
        "cotangent": scatter_about(seeds[3], (CHARTS, SEQ_LEN, D), 1.0, 6.0, ((0, 4), (1, 8))),
        "norm_self": jnp.clip(1.0 + 0.1 * jax.random.normal(seeds[4], (D,), jnp.float32), 0.5, 1.5),
        "w_query": scatter_about(seeds[5], (D, D), D ** -0.5, 0.21875),
        "w_key": scatter_about(seeds[6], (D, D), D ** -0.5, 0.21875),
        "w_value": scatter_about(seeds[7], (D, D), D ** -0.5, 0.21875),
        "w_out": scatter_about(seeds[8], (D, D), (0.016 * SEQ_LEN ** 0.5), 3.0625),
        "norm_cross": jnp.clip(1.0 + 0.1 * jax.random.normal(seeds[9], (D,), jnp.float32), 0.5, 1.5),
        "c_query": scatter_about(seeds[10], (D, D), D ** -0.5, 0.21875),
        "c_key": scatter_about(seeds[11], (D, D), D ** -0.5, 0.21875),
        "c_value": scatter_about(seeds[12], (D, D), D ** -0.5, 0.21875),
        "c_out": scatter_about(seeds[13], (D, D), (0.017 * PATCHES ** 0.5), 0.8125),
        "norm_ffn": jnp.clip(1.0 + 0.1 * jax.random.normal(seeds[14], (D,), jnp.float32), 0.5, 1.5),
        "w_gate": scatter_about(seeds[15], (D, FF), D ** -0.5, 0.21875),
        "w_up": scatter_about(seeds[16], (D, FF), D ** -0.5, 0.21875),
        "w_down": scatter_about(seeds[17], (FF, D), FF ** -0.5, 0.125),
    }


@jax.custom_vjp
def low(v):
    return lax.optimization_barrier(v.astype(jnp.bfloat16)).astype(jnp.float32)

@jax.custom_vjp
def low_back(v):
    return v

def low_keep(v):
    return (low(v), None)

def low_pass(kept, grad):
    return (grad,)

def back_keep(v):
    return (v, None)

def back_low(kept, grad):
    return (low(grad),)
low.defvjp(low_keep, low_pass)
low_back.defvjp(back_keep, back_low)
HIGHEST = lax.Precision.HIGHEST
EPSILON = 1e-06
NEGATIVE = -1e+30

def product(left, right):
    return jnp.dot(left, right, precision=HIGHEST, preferred_element_type=jnp.float32)

def norm_scale(values, gain):
    return values * lax.rsqrt(lax.optimization_barrier(jnp.mean(values * values, axis=-1, keepdims=True)) + EPSILON) * gain

def gelu_tanh(values):
    return 0.5 * values * (1.0 + jnp.tanh(0.7978845608028654 * (values + 0.044715 * values * values * values)))

def split_items(array):
    groups, count, _ = array.shape
    return array.reshape(groups, count, H, HD).transpose(0, 2, 1, 3).reshape(groups * H, count, HD)

def join_items(array, groups):
    count = array.shape[1]
    return array.reshape(groups, H, count, HD).transpose(0, 2, 1, 3).reshape(groups, count, H * HD)

def attend(queries, keys, values, allow):
    total, length, head = queries.shape
    block = min(512, length)
    stacked = queries.reshape(total, length // block, block, head).transpose(1, 0, 2, 3)
    starts = jnp.arange(length // block, dtype=jnp.int32) * block
    scale = HD ** (-0.5)

    def one_block(pair):
        part, start = pair
        raw = jnp.einsum('iqd,ikd->iqk', part, keys, precision=HIGHEST)
        scores = low_back(raw * scale)
        scores = jnp.where(allow(start, block), scores, NEGATIVE)
        weights = jax.nn.softmax(scores, axis=-1)
        return jnp.einsum('iqk,ikd->iqd', low(weights), values, precision=HIGHEST)
    results = lax.map(jax.checkpoint(one_block), (stacked, starts))
    return results.transpose(1, 0, 2, 3).reshape(total, length, head)

def layer(inputs, memory, counts, norm_self, w_query, w_key, w_value, w_out, norm_cross, c_query, c_key, c_value, c_out, norm_ffn, w_gate, w_up, w_down):
    groups, length, _ = inputs.shape
    patches = memory.shape[1]
    item_counts = jnp.repeat(counts, H)

    def causal(start, block):
        places = start + jnp.arange(block, dtype=jnp.int32)
        return (places[:, None] >= jnp.arange(length, dtype=jnp.int32)[None, :])[None]

    def masked(start, block):
        return jnp.arange(patches, dtype=jnp.int32)[None, None, :] < item_counts[:, None, None]
    normed = low(norm_scale(inputs, norm_self))
    query_self = low(low_back(product(normed, w_query)))
    key_self = low(low_back(product(normed, w_key)))
    value_self = low(low_back(product(normed, w_value)))
    mixed = attend(split_items(query_self), split_items(key_self), split_items(value_self), causal)
    mixed = low(low_back(join_items(mixed, groups)))
    after_self = inputs + low_back(product(mixed, w_out))
    normed_cross = low(norm_scale(after_self, norm_cross))
    query_cross = low(low_back(product(normed_cross, c_query)))
    memory_keys = low(low_back(product(memory, c_key)))
    memory_values = low(low_back(product(memory, c_value)))
    fetched = attend(split_items(query_cross), split_items(memory_keys), split_items(memory_values), masked)
    fetched = low(low_back(join_items(fetched, groups)))
    after_cross = after_self + low_back(product(fetched, c_out))
    normed_ffn = low(norm_scale(after_cross, norm_ffn))
    gate = low_back(product(normed_ffn, w_gate))
    upward = low_back(product(normed_ffn, w_up))
    hidden = low(gelu_tanh(gate) * upward)
    return after_cross + low_back(product(hidden, w_down))

def reference(inputs, memory, patch_count, cotangent, norm_self, w_query, w_key, w_value, w_out, norm_cross, c_query, c_key, c_value, c_out, norm_ffn, w_gate, w_up, w_down):
    params = tuple((p.astype(jnp.float32) for p in (norm_self, w_query, w_key, w_value, w_out, norm_cross, c_query, c_key, c_value, c_out, norm_ffn, w_gate, w_up, w_down)))
    group = math.gcd(CHARTS, max(1, 4096 // SEQ_LEN))
    rounds = CHARTS // group

    def regroup(array):
        return array.reshape((rounds, group) + array.shape[1:])

    def one_round(totals, span_data):
        inputs_now, memory_now, counts_now, grad_now = span_data

        def forward(input_values, memory_values, *weights):
            return layer(input_values, memory_values, counts_now, *weights)
        result, pull = jax.vjp(forward, inputs_now.astype(jnp.float32), memory_now.astype(jnp.float32), *params)
        grads = pull(grad_now.astype(jnp.float32))
        totals = tuple((t + g for t, g in zip(totals, grads[2:])))
        return (totals, (result, grads[0], grads[1]))
    zeros = tuple((jnp.zeros(p.shape, jnp.float32) for p in params))
    totals, (results, input_grads, memory_grads) = lax.scan(one_round, zeros, (regroup(inputs), regroup(memory), regroup(patch_count), regroup(cotangent)))
    return (results.reshape(inputs.shape), input_grads.reshape(inputs.shape), memory_grads.reshape(memory.shape), totals[0], totals[1], totals[2], totals[3], totals[4], totals[5], totals[6], totals[7], totals[8], totals[9], totals[10], totals[11], totals[12], totals[13])
```

```python
import functools

import jax
import jax.numpy as jnp
from jax import lax
from jax.experimental import pallas as pl
from jax.experimental.pallas import tpu as pltpu
from jax.sharding import PartitionSpec as P

H = 12
EPSILON = 1e-06
NEGATIVE = -1e30
F32 = jnp.float32
BF = jnp.bfloat16
VM = pl.BlockSpec(memory_space=pltpu.VMEM)
SM = pl.BlockSpec(memory_space=pltpu.SMEM)
ROWS = 512
QB = 256


def dot(a, b):
    return lax.dot_general(a, b, (((1,), (0,)), ((), ())), preferred_element_type=F32)


def nt(a, b):
    return lax.dot_general(a, b, (((1,), (1,)), ((), ())), preferred_element_type=F32)


def lanes(width):
    return lax.broadcasted_iota(jnp.int32, (1, width), 1)


def inv_rms(v):
    return lax.rsqrt(jnp.mean(v * v, axis=-1, keepdims=True) + EPSILON)


def norm_back(e, v, gain):
    r = inv_rms(v)
    u = v * r
    eg = e * gain
    grad_v = (eg - u * jnp.mean(eg * u, axis=-1, keepdims=True)) * r
    return grad_v, jnp.sum(e * u, axis=0, keepdims=True)


def cost(flops, *arrays):
    total = sum(a.size * a.dtype.itemsize for a in arrays)
    return pl.CostEstimate(flops=int(flops), bytes_accessed=int(total), transcendentals=0)


def sds(shape, dtype):
    return jax.ShapeDtypeStruct(shape, dtype)


def project_kernel(
    charts, tokens, patches, meta, own, oth, gain, wq, wk, wv, ck, cv,
    x_nat, x_own, a1, q, k, v, mem, mk, mv, mem_scr,
):
    core, place = meta[0], meta[1]
    half = q.shape[1]
    width = a1.shape[1]
    group = max(1, min(charts, ROWS // tokens))
    cols = pl.ds(pl.multiple_of(core * half, 128), half)

    def one(ref, parity, first):
        x = ref[pl.ds(first, group), :tokens, :].reshape(group * tokens, width)
        xf = x.astype(F32)
        a = (xf * inv_rms(xf) * gain[...]).astype(BF)
        qq = (dot(a, wq[:, cols]) * 0.125).astype(BF)
        kk = dot(a, wk[:, cols]).astype(BF)
        vv = dot(a, wv[:, cols]).astype(BF)
        for i in range(group):
            chunk = lax.rem(place - (first + i) + charts, charts)
            part = slice(i * tokens, (i + 1) * tokens)
            at = pl.ds(pl.multiple_of((2 * chunk + parity) * tokens, tokens), tokens)
            x_nat[at, :] = x[part]
            a1[at, :] = a[part]
            q[at, :] = qq[part]
            k[at, :] = kk[part]
            v[at, :] = vv[part]
            few = ref[first + i, tokens:, :].astype(F32)
            spot = pl.ds(pl.multiple_of((2 * chunk + parity) * patches, patches), patches)
            mem_scr[spot, :] = few
            if ref is own:
                x_own[pl.ds(pl.multiple_of(chunk * tokens, tokens), tokens), :] = x[part]

    for ref, parity in ((own, core), (oth, 1 - core)):
        if charts == group:
            one(ref, parity, 0)
        else:
            lax.fori_loop(
                0, charts // group, lambda g, c, r=ref, p=parity: (one(r, p, g * group), c)[1], 0
            )
    whole = mem_scr[...].astype(BF)
    mem[...] = whole
    mk[...] = dot(whole, ck[...]).astype(BF)
    mv[...] = dot(whole, cv[...]).astype(BF)


def split3(value):
    hi = value.astype(BF).astype(F32)
    mid = (value - hi).astype(BF).astype(F32)
    lo = (value - hi - mid).astype(BF).astype(F32)
    return hi, mid, lo


def head_masks(h):
    lane = lanes(128)
    mine = ((lane < 64) if h == 0 else (lane >= 64)).astype(F32)
    base = 64 if h == 0 else 0
    marks = [(lane == base + i).astype(F32) for i in range(3)]
    return mine, marks


def add_marks(mine, marks, body, extra):
    hi, mid, lo = split3(extra)
    return (body * mine + hi * marks[0] + mid * marks[1] + lo * marks[2]).astype(BF)


def attend_kernel(tokens, meta, q, k, v, o_keep, o_send, o_nat, q_aug):
    core = meta[0]
    size = q.shape[0]
    row = lax.broadcasted_iota(jnp.int32, (QB, QB), 0)
    col = lax.broadcasted_iota(jnp.int32, (QB, QB), 1)

    def one_block(i, count):
        at = pl.ds(i * QB, QB) if count is not None else pl.ds(pl.multiple_of(i * QB, QB), QB)
        qp = q[at, :]
        outs = []
        for h in (0, 1):
            mine, marks = head_masks(h)
            mb = mine.astype(BF)
            rest = (1.0 - mine).astype(BF)
            qh = qp * mb

            def scores(j):
                return nt(qh, k[pl.ds(pl.multiple_of(j * QB, QB), QB), :])

            def weigh(e, j):
                vh = v[pl.ds(pl.multiple_of(j * QB, QB), QB), :] * mb + rest
                return dot(e.astype(BF), vh)

            diag = jnp.where(row >= col, scores(i), NEGATIVE)
            if count is not None:
                parts = [scores(j) for j in range(count - 1)] + [diag]
                top = parts[0]
                for s in parts[1:]:
                    top = jnp.maximum(top, s)
                top = jnp.max(top, axis=1, keepdims=True)
                acc = weigh(jnp.exp(parts[0] - top), 0)
                for j, s in enumerate(parts[1:]):
                    acc = acc + weigh(jnp.exp(s - top), j + 1)
            else:
                top = jnp.max(diag, axis=1, keepdims=True)
                acc = weigh(jnp.exp(diag - top), i)

                def step(j, state):
                    top, acc = state
                    s = scores(j)
                    new = jnp.maximum(top, jnp.max(s, axis=1, keepdims=True))
                    return new, acc * jnp.exp(top - new) + weigh(jnp.exp(s - new), j)

                top, acc = lax.fori_loop(0, i, step, (top, acc))
            total = pltpu.roll(acc, 64, 1)
            outs.append(acc / (total * mine + (1.0 - mine)) * mine)
            lse = top + jnp.log(acc * (1.0 - mine) + mine)
            q_aug[h, at, :] = add_marks(mine, marks, qp.astype(F32), -lse)
        o = (outs[0] + outs[1]).astype(BF)
        o_nat[at, :] = o
        per = QB // (2 * tokens)
        for c in range(per):
            even = o[2 * c * tokens : (2 * c + 1) * tokens]
            odd = o[(2 * c + 1) * tokens : (2 * c + 2) * tokens]
            spot = pl.ds(pl.multiple_of((i * per + c) * tokens, tokens), tokens)
            flag = jnp.full(even.shape, core, jnp.int32).astype(F32)
            ef, of = even.astype(F32), odd.astype(F32)
            o_keep[spot, :] = jnp.where(flag == 0, ef, of).astype(BF)
            o_send[spot, :] = jnp.where(flag == 0, of, ef).astype(BF)

    if size <= 1024:
        for i in range(size // QB):
            one_block(i, i + 1)
    else:
        lax.fori_loop(0, size // QB, lambda i, c: (one_block(i, None), c)[1], 0)


def attend_back_kernel(
    tokens, meta, q_aug, k, v, o_nat, do_own, do_oth, dq, dk, dv, k_aug, v_aug, kt, dk_acc, dv_acc
):
    core = meta[0]
    size = k.shape[0]
    krow = lax.broadcasted_iota(jnp.int32, (QB, QB), 0)
    qcol = lax.broadcasted_iota(jnp.int32, (QB, QB), 1)
    kt[...] = k[...].astype(F32).T.astype(BF)
    for h in (0, 1):
        mine, marks = head_masks(h)
        ones = (marks[0] + marks[1] + marks[2]).astype(BF)
        k_aug[h] = k[...] * mine.astype(BF) + ones
        v_aug[h] = v[...] * mine.astype(BF) + ones
    dk_acc[...] = jnp.zeros_like(dk_acc)
    dv_acc[...] = jnp.zeros_like(dv_acc)

    def one_block(i, count):
        at = pl.ds(pl.multiple_of(i * QB, QB), QB)
        per = QB // (2 * tokens)
        pieces = []
        for c in range(per):
            spot = pl.ds(pl.multiple_of((i * per + c) * tokens, tokens), tokens)
            a, b = do_own[spot, :].astype(F32), do_oth[spot, :].astype(F32)
            flag = jnp.full(a.shape, core, jnp.int32)
            pieces += [jnp.where(flag == 0, a, b), jnp.where(flag == 0, b, a)]
        do = jnp.concatenate(pieces, 0)
        prod = do * o_nat[at, :].astype(F32)
        turned = []
        for h in (0, 1):
            mine, marks = head_masks(h)
            delta = jnp.sum(prod * mine, axis=1, keepdims=True)
            doa = add_marks(mine, marks, do, -delta)
            qa = q_aug[h, at, :]

            def one(j, dqt, diagonal):
                kat = pl.ds(pl.multiple_of(j * QB, QB), QB)
                s = nt(k_aug[h, kat, :], qa)
                if diagonal:
                    s = jnp.where(qcol >= krow, s, NEGATIVE)
                p = jnp.exp(s)
                ds = (p * nt(v_aug[h, kat, :], doa)).astype(BF)
                dv_acc[h, kat, :] += dot(p.astype(BF), doa)
                dk_acc[h, kat, :] += dot(ds, qa)
                return dqt + dot(kt[64 * h : 64 * h + 64, kat], ds)

            dqt = jnp.zeros((64, QB), F32)
            if count is not None:
                for j in range(count - 1):
                    dqt = one(j, dqt, False)
            else:
                dqt = lax.fori_loop(0, i, lambda j, c: one(j, c, False), dqt)
            turned.append(one(i, dqt, True))
        dq[at, :] = (jnp.concatenate(turned, 0).T * 0.125).astype(BF)

    if size <= 1024:
        for i in range(size // QB):
            one_block(i, i + 1)
    else:
        lax.fori_loop(0, size // QB, lambda i, c: (one_block(i, None), c)[1], 0)
    m0, m1 = head_masks(0)[0], head_masks(1)[0]
    dk[...] = (dk_acc[0] * m0 + dk_acc[1] * m1).astype(BF)
    dv[...] = (dv_acc[0] * m0 + dv_acc[1] * m1).astype(BF)


def cross_pair(ref, p):
    lane = lanes(128)
    piece = ref[:, 128 * p : 128 * p + 128]
    low = (lane < 64).astype(BF)
    high = (lane >= 64).astype(BF)
    return jnp.concatenate([piece * low, piece * high], 0)


def cross_kernel(
    meta, x, o_own, o_oth, w_out, g_cross, c_query, mk, mv, c_out, g_ffn,
    o1, y1, a2, cq, p2, o2, y2, a3,
):
    core, count = meta[0], meta[2]
    half = o_own.shape[1]
    mine = pl.ds(pl.multiple_of(core * half, 128), half)
    other = pl.ds(pl.multiple_of((1 - core) * half, 128), half)
    o1[:, mine] = o_own[...]
    o1[:, other] = o_oth[...]
    first = x[...].astype(F32) + dot(o1[...], w_out[...])
    y1[...] = first
    n2 = (first * inv_rms(first) * g_cross[...]).astype(BF)
    a2[...] = n2
    query = dot(n2, c_query[...]).astype(BF)
    cq[...] = query
    patches = mk.shape[0]
    lane = lanes(2 * patches)
    low = lane < patches
    valid = jnp.where(low, lane, lane - patches) < count
    for p in range(H // 2):
        keys = cross_pair(mk, p)
        values = cross_pair(mv, p)
        s = nt(query[:, 128 * p : 128 * p + 128], keys) * 0.125
        s = jnp.where(valid, s, NEGATIVE)
        m0 = jnp.max(jnp.where(low, s, NEGATIVE), axis=1, keepdims=True)
        m1 = jnp.max(jnp.where(low, NEGATIVE, s), axis=1, keepdims=True)
        e = jnp.exp(s - jnp.where(low, m0, m1))
        l0 = jnp.sum(jnp.where(low, e, 0.0), axis=1, keepdims=True)
        l1 = jnp.sum(jnp.where(low, 0.0, e), axis=1, keepdims=True)
        w = e / jnp.where(low, l0, l1)
        p2[p] = w
        o2[:, 128 * p : 128 * p + 128] = dot(w.astype(BF), values).astype(BF)
    second = first + dot(o2[...], c_out[...])
    y2[...] = second
    a3[...] = (second * inv_rms(second) * g_ffn[...]).astype(BF)


def ffn_kernel(
    row_blocks, meta, a3, cot, y2, g_ffn, wg, wu, wd,
    out, dy2, dy2b, gain, send, keep, acc, err, a3t, cott, dw,
):
    core = meta[0]
    i, r = pl.program_id(0), pl.program_id(1)
    rows = pl.ds(pl.multiple_of(r * ROWS, ROWS), ROWS)
    first, last = i == 0, i == pl.num_programs(0) - 1

    @pl.when(first)
    def _():
        a3t[:, rows] = a3[...].astype(F32).T.astype(BF)
        cott[:, rows] = cot[...].astype(F32).T.astype(BF)
        acc[rows, :] = y2[...]
        err[rows, :] = jnp.zeros((ROWS, err.shape[1]), F32)

    gate = dot(a3[...], wg[...])
    up = dot(a3[...], wu[...])
    square = gate * gate
    th = jnp.tanh(0.7978845608028654 * gate * (1.0 + 0.044715 * square))
    more = 0.5 * (1.0 + th)
    act = gate * more
    slope = more + 0.5 * gate * (1.0 - th * th) * (
        0.7978845608028654 * (1.0 + 3 * 0.044715 * square)
    )
    hidden = (act * up).astype(BF)
    dh = nt(cot[...], wd[...])
    d_gate = (dh * up * slope).astype(BF)
    d_up = (dh * act).astype(BF)
    acc[rows, :] += dot(hidden, wd[...])
    err[rows, :] += nt(d_gate, wg[...]) + nt(d_up, wu[...])
    terms = (dot(a3t[:, rows], d_gate), dot(a3t[:, rows], d_up), dot(cott[:, rows], hidden))
    if row_blocks > 1:
        for n, term in enumerate(terms):
            dw[n] = jnp.where(r == 0, 0.0, dw[n]) + term
        terms = (dw[0], dw[1], dw[2])

    def put():
        side = i // 2
        which = lax.rem(i, 2)
        width = terms[0].shape[1]
        for n in (0, 1):
            block = terms[n].astype(BF).reshape(8, terms[n].shape[0] // 8, width)

            @pl.when(which == core)
            def _(n=n, block=block):
                keep[side, n] = block

            @pl.when(which != core)
            def _(n=n, block=block):
                send[side, n] = block

        down = terms[2].astype(BF)
        per, part, wide = down.shape[0] // 4, down.shape[0] // 8, width // 2
        for b in range(4):
            for y in range(2):
                piece = down[b * per : (b + 1) * per, y * wide : (y + 1) * wide]
                packed = jnp.concatenate([piece[:part], piece[part:]], 1)

                @pl.when(core == b % 2)
                def _(b=b, y=y, packed=packed):
                    keep[b // 2, 2, 2 * i + y] = packed

                @pl.when(core != b % 2)
                def _(b=b, y=y, packed=packed):
                    send[b // 2, 2, 2 * i + y] = packed

    if row_blocks > 1:
        pl.when(r == row_blocks - 1)(put)
    else:
        put()

    @pl.when(last)
    def _():
        out[...] = acc[rows, :].astype(BF)
        back, gsum = norm_back(err[rows, :], y2[...], g_ffn[...])
        total = cot[...].astype(F32) + back
        dy2[...] = total
        dy2b[...] = total.astype(BF)
        gain[...] = jnp.where(r == 0, 0.0, gain[...]) + gsum


def cross_back_kernel(
    charts, patches_each, meta, dy2, dy2b, c_out, p2, mk, mv, cq, y1, g_cross, c_query, w_out,
    c_key, c_value,
    dcq, dmk, dmv, dy1, dy1b, do_keep, do_send, memg, gain, mk_acc, mv_acc, mem_scr,
):
    core = meta[0]
    r = pl.program_id(0)
    half = do_keep.shape[1]
    patches = mk.shape[0]
    lane = lanes(2 * patches)
    low = lane < patches
    left = (lanes(128) < 64).astype(F32)
    do2 = nt(dy2b[...], c_out[...]).astype(BF)
    fresh = r == 0
    for p in range(H // 2):
        at = slice(128 * p, 128 * p + 128)
        keys = cross_pair(mk, p)
        values = cross_pair(mv, p)
        w = p2[p]
        dp = nt(do2[:, at], values)
        prod = w * dp
        r0 = jnp.sum(jnp.where(low, prod, 0.0), axis=1, keepdims=True)
        r1 = jnp.sum(jnp.where(low, 0.0, prod), axis=1, keepdims=True)
        ds = w * (dp - jnp.where(low, r0, r1))
        dcq[:, at] = (dot(ds.astype(BF), keys) * 0.125).astype(BF)
        gk = dot(ds.T.astype(BF), cq[:, at]) * 0.125
        gv = dot(w.T.astype(BF), do2[:, at])
        gk = gk[:patches] * left + gk[patches:] * (1.0 - left)
        gv = gv[:patches] * left + gv[patches:] * (1.0 - left)
        mk_acc[:, at] = jnp.where(fresh, 0.0, mk_acc[:, at]) + gk
        mv_acc[:, at] = jnp.where(fresh, 0.0, mv_acc[:, at]) + gv
    err = nt(dcq[...], c_query[...])
    back, gsum = norm_back(err, y1[...], g_cross[...])
    total = dy2[...] + back
    dy1[...] = total
    tb = total.astype(BF)
    dy1b[...] = tb
    gain[...] = jnp.where(fresh, 0.0, gain[...]) + gsum
    do_keep[...] = nt(tb, w_out[pl.ds(pl.multiple_of(core * half, half), half), :]).astype(BF)
    do_send[...] = nt(tb, w_out[pl.ds(pl.multiple_of((1 - core) * half, half), half), :]).astype(BF)

    @pl.when(r == pl.num_programs(0) - 1)
    def _():
        gk, gv = mk_acc[...].astype(BF), mv_acc[...].astype(BF)
        dmk[...] = gk
        dmv[...] = gv
        mem_scr[...] = nt(gk, c_key[...]) + nt(gv, c_value[...])
        for a in range(charts):
            for parity in range(2):
                memg[parity, a] = mem_scr[pl.ds((2 * a + parity) * patches_each, patches_each), :]


def square_kernel(meta, o2, dy2b, a2, dcq, mem, dmk, dmv, o1, dy1b, send, keep):
    core = meta[0]
    half = keep.shape[2]
    mine = pl.ds(pl.multiple_of(core * half, 128), half)
    other = pl.ds(pl.multiple_of((1 - core) * half, 128), half)
    memt = mem[...].astype(F32).T.astype(BF)
    pairs = ((o2, dy2b), (a2, dcq), (None, dmk), (None, dmv), (o1, dy1b))
    for n, (left, right) in enumerate(pairs):
        turned = memt if left is None else left[...].astype(F32).T.astype(BF)
        send[n] = dot(turned, right[:, other]).astype(BF)
        keep[n] = dot(turned, right[:, mine]).astype(BF)


def entry_kernel(charts, tokens, meta, dq, dk, dv, wq, wk, wv, x_nat, e_keep, e_send, gain, scr):
    core = meta[0]
    half = dq.shape[1]
    cols = pl.ds(pl.multiple_of(core * half, 128), half)
    size = dq.shape[0]
    step = min(size, 2 * ROWS)
    gain[...] = jnp.zeros_like(gain)
    per = step // (2 * tokens)

    def one(first):
        at = pl.ds(pl.multiple_of(first * step, step), step)
        e = nt(dq[at, :], wq[:, cols]) + nt(dk[at, :], wk[:, cols]) + nt(dv[at, :], wv[:, cols])
        scr[...] = e
        x = x_nat[at, :].astype(F32)
        gain[...] += jnp.sum(e * (x * inv_rms(x)), axis=0, keepdims=True)
        for c in range(per):
            spot = pl.ds(pl.multiple_of((first * per + c) * tokens, tokens), tokens)
            e_keep[spot, :] = scr[pl.ds(pl.multiple_of((2 * c + core) * tokens, tokens), tokens), :]
            e_send[spot, :] = scr[
                pl.ds(pl.multiple_of((2 * c + 1 - core) * tokens, tokens), tokens), :
            ].astype(BF)

    if size == step:
        one(0)
    else:
        lax.fori_loop(0, size // step, lambda g, c: (one(g), c)[1], 0)


def triple_kernel(a1, dq, dk, dv, g_self, g_cross, g_ffn, out):
    half = dq.shape[1]
    turned = a1[...].astype(F32).T.astype(BF)
    for n, right in enumerate((dq, dk, dv)):
        out[:, n * half : (n + 1) * half] = dot(turned, right[...]).astype(BF)
    width = g_self.shape[1]
    stack = jnp.concatenate(
        [g_self[...], g_cross[...], g_ffn[...], jnp.zeros((125, width), F32)], 0
    )
    out[:, 3 * half :] = stack.T.astype(BF)


def input_grad_kernel(e_keep, e_recv, x, gain, dy1, out):
    err = e_keep[...] + e_recv[...].astype(F32)
    back, _ = norm_back(err, x[...].astype(F32), gain[...])
    out[...] = (dy1[...] + back).astype(BF)


def place_kernel(charts, meta, *refs):
    place = meta[1]
    out = refs[-1]
    for d in range(charts):
        out[lax.rem(place - d + charts, charts)] = refs[d][...].astype(F32)


def local(
    nseq, inputs, memory, patch_count, cotangent, norm_self, w_query, w_key, w_value, w_out,
    norm_cross, c_query, c_key, c_value, c_out, norm_ffn, w_gate, w_up, w_down,
):
    charts, tokens, width = inputs.shape
    patches_each = memory.shape[1]
    size = charts * 2 * tokens
    own = charts * tokens
    patches = patches_each * nseq
    half = width // 2
    hidden = w_gate.shape[1]
    blocks = own // ROWS
    dp = lax.axis_index("dp")
    seq = lax.axis_index("seq")
    side, core = dp // 2, lax.rem(dp, 2)
    place, parity = seq // 2, lax.rem(seq, 2)

    def shift(d):
        return [
            ((2 * x + k) * nseq + 2 * a + b, (2 * x + b) * nseq + 2 * ((a + d) % charts) + k)
            for x in range(2)
            for k in range(2)
            for a in range(charts)
            for b in range(2)
        ]

    def dp_perm(rule):
        return [(2 * x + k, 2 * rule(x, k)[0] + rule(x, k)[1]) for x in range(2) for k in range(2)]

    swap_core = dp_perm(lambda x, k: (x, 1 - k))
    swap_side = dp_perm(lambda x, k: (1 - x, k))

    def across(value):
        return lax.ppermute(value, "dp", swap_core)

    def travel(value, d):
        return lax.ppermute(value, ("dp", "seq"), shift(d))

    def pick(value, d):
        return lax.dynamic_index_in_dim(value, lax.rem(place + d, charts), 0, keepdims=False)

    gain_self, gain_cross, gain_ffn = (g.reshape(1, width) for g in (norm_self, norm_cross, norm_ffn))
    other_counts = across(patch_count)
    counts = jnp.where(core == parity, patch_count, other_counts)
    count = lax.dynamic_index_in_dim(counts, place, 0, keepdims=False)
    meta = jnp.stack([core, place, count, side]).astype(jnp.int32)

    mine = jnp.stack(
        [
            travel(jnp.concatenate([pick(inputs, d), pick(memory, d)], 0), d)
            for d in range(charts)
        ]
    )
    theirs = across(mine)
    x_nat, x_own, a1, q, k, v, mem, mk, mv = pl.pallas_call(
        functools.partial(project_kernel, charts, tokens, patches_each),
        out_shape=(
            sds((size, width), BF), sds((own, width), BF), sds((size, width), BF),
            sds((size, half), BF), sds((size, half), BF), sds((size, half), BF),
            sds((patches, width), BF), sds((patches, width), BF), sds((patches, width), BF),
        ),
        in_specs=[SM] + [VM] * 8,
        out_specs=[VM] * 9,
        scratch_shapes=[pltpu.VMEM((patches, width), F32)],
        cost_estimate=cost(2 * size * width * 3 * half, mine, theirs, w_query, w_key, w_value),
    )(meta, mine, theirs, gain_self, w_query, w_key, w_value, c_key, c_value)

    cot_parts = [travel(pick(cotangent, d), d) for d in range(charts)]

    pairs = half // 128
    pair_spec = pl.BlockSpec((size, 128), lambda p, m: (0, p))
    own_spec = pl.BlockSpec((own, 128), lambda p, m: (0, p))
    aug_spec = pl.BlockSpec((2, size, 128), lambda p, m: (p, 0, 0))
    o_keep, o_send, o_nat, q_aug = pl.pallas_call(
        functools.partial(attend_kernel, tokens),
        out_shape=(
            sds((own, half), BF), sds((own, half), BF), sds((size, half), BF),
            sds((2 * pairs, size, 128), BF),
        ),
        grid_spec=pltpu.PrefetchScalarGridSpec(
            num_scalar_prefetch=1,
            grid=(pairs,),
            in_specs=[pair_spec] * 3,
            out_specs=[own_spec, own_spec, pair_spec, aug_spec],
        ),
        cost_estimate=cost(4 * size * size * half, q, k, v),
    )(meta, q, k, v)
    o_recv = across(o_send)

    row_spec = pl.BlockSpec((ROWS, width), lambda r: (r, 0))
    half_spec = pl.BlockSpec((ROWS, half), lambda r: (r, 0))
    p2_spec = pl.BlockSpec((H // 2, ROWS, 2 * patches), lambda r: (0, r, 0))

    def fixed(shape, spaces=1):
        if spaces == 1:
            return pl.BlockSpec(shape, lambda r: (0,) * len(shape))
        return pl.BlockSpec(shape, lambda i, r: (0,) * len(shape))

    square = fixed((width, width))
    one_row = fixed((1, width))
    patch_spec = fixed((patches, width))
    rows_f = sds((own, width), F32)
    rows_b = sds((own, width), BF)
    o1, y1, a2, cq, p2, o2, y2, a3 = pl.pallas_call(
        cross_kernel,
        out_shape=(
            rows_b, rows_f, rows_b, rows_b, sds((H // 2, own, 2 * patches), F32), rows_b, rows_f,
            rows_b,
        ),
        grid=(blocks,),
        in_specs=[
            SM, row_spec, half_spec, half_spec, square, one_row, square, patch_spec, patch_spec,
            square, one_row,
        ],
        out_specs=[row_spec] * 4 + [p2_spec] + [row_spec] * 3,
        cost_estimate=cost(6 * own * width * width, w_out, c_query, c_out, rows_f, rows_f),
    )(meta, x_own, o_keep, o_recv, w_out, gain_cross, c_query, mk, mv, c_out, gain_ffn)

    cot = lax.dynamic_slice_in_dim(
        jnp.concatenate(cot_parts[::-1] + cot_parts[::-1], 0),
        (charts - 1 - place) * tokens,
        own,
        0,
    )
    wide = hidden // 4
    last = 3
    pack = (2, 3, 8, width // 8, wide)
    frow = pl.BlockSpec((ROWS, width), lambda i, r: (r, 0))
    lrow = pl.BlockSpec((ROWS, width), lambda i, r: (r * (i // last), 0))
    out_b, dy2, dy2b, ffn_gain, f_send, f_keep = pl.pallas_call(
        functools.partial(ffn_kernel, blocks),
        out_shape=(rows_b, rows_f, rows_b, sds((1, width), F32), sds(pack, BF), sds(pack, BF)),
        grid=(4, blocks),
        in_specs=[
            SM, frow, frow, frow, fixed((1, width), 2),
            pl.BlockSpec((width, wide), lambda i, r: (0, i)),
            pl.BlockSpec((width, wide), lambda i, r: (0, i)),
            pl.BlockSpec((wide, width), lambda i, r: (i, 0)),
        ],
        out_specs=[lrow, lrow, lrow, fixed((1, width), 2), fixed(pack, 2), fixed(pack, 2)],
        scratch_shapes=[
            pltpu.VMEM((own, width), F32), pltpu.VMEM((own, width), F32),
            pltpu.VMEM((width, own), BF), pltpu.VMEM((width, own), BF),
            pltpu.VMEM((3, width, wide) if blocks > 1 else (3, 8, 128), F32),
        ],
        cost_estimate=cost(18 * own * width * hidden, w_gate, w_up, w_down, rows_f, rows_f),
    )(meta, a3, cot, y2, gain_ffn, w_gate, w_up, w_down)
    f_recv = across(f_send)

    dcq, dmk, dmv, dy1, dy1b, do_keep, do_send, memg, cross_gain = pl.pallas_call(
        functools.partial(cross_back_kernel, charts, patches_each),
        out_shape=(
            rows_b, sds((patches, width), BF), sds((patches, width), BF), rows_f, rows_b,
            sds((own, half), BF), sds((own, half), BF),
            sds((2, charts, patches_each, width), F32), sds((1, width), F32),
        ),
        grid=(blocks,),
        in_specs=[
            SM, row_spec, row_spec, square, p2_spec, patch_spec, patch_spec, row_spec, row_spec,
            one_row, square, square, square, square,
        ],
        out_specs=[
            row_spec, patch_spec, patch_spec, row_spec, row_spec, half_spec, half_spec,
            fixed((2, charts, patches_each, width)), one_row,
        ],
        scratch_shapes=[pltpu.VMEM((patches, width), F32)] * 3,
        cost_estimate=cost(6 * own * width * width, w_out, c_query, c_out, rows_f, rows_f),
    )(meta, dy2, dy2b, c_out, p2, mk, mv, cq, y1, gain_cross, c_query, w_out, c_key, c_value)
    do_recv = across(do_send)

    s_send, s_keep = pl.pallas_call(
        square_kernel,
        out_shape=(sds((5, width, half), BF), sds((5, width, half), BF)),
        in_specs=[SM] + [VM] * 9,
        out_specs=[VM] * 2,
        cost_estimate=cost(6 * own * width * width, o1, o2, a2, dcq, dy2b, dy1b),
    )(meta, o2, dy2b, a2, dcq, mem, dmk, dmv, o1, dy1b)
    s_recv = across(s_send)

    memg_send = lax.dynamic_index_in_dim(memg, 1 - core, 0, keepdims=False).astype(BF)
    memg_keep = lax.dynamic_index_in_dim(memg, core, 0, keepdims=False)
    memg_own = (memg_keep + across(memg_send).astype(F32)).astype(BF)
    out_rows = jnp.concatenate([out_b.reshape(charts, tokens, width), memg_own], 1)
    out_parts = [travel(pick(out_rows, d), d) for d in range(charts)]

    dq, dk, dv = pl.pallas_call(
        functools.partial(attend_back_kernel, tokens),
        out_shape=(sds((size, half), BF),) * 3,
        grid_spec=pltpu.PrefetchScalarGridSpec(
            num_scalar_prefetch=1,
            grid=(pairs,),
            in_specs=[aug_spec, pair_spec, pair_spec, pair_spec, own_spec, own_spec],
            out_specs=[pair_spec] * 3,
            scratch_shapes=[
                pltpu.VMEM((2, size, 128), BF), pltpu.VMEM((2, size, 128), BF),
                pltpu.VMEM((128, size), BF),
                pltpu.VMEM((2, size, 128), F32), pltpu.VMEM((2, size, 128), F32),
            ],
        ),
        cost_estimate=cost(10 * size * size * half, q, k, v, q_aug),
    )(meta, q_aug, k, v, o_nat, do_keep, do_recv)

    e_keep, e_send, self_gain = pl.pallas_call(
        functools.partial(entry_kernel, charts, tokens),
        out_shape=(rows_f, rows_b, sds((1, width), F32)),
        in_specs=[SM] + [VM] * 7,
        out_specs=[VM] * 3,
        scratch_shapes=[pltpu.VMEM((min(size, 2 * ROWS), width), F32)],
        cost_estimate=cost(2 * size * width * 3 * half, dq, dk, dv, rows_f),
    )(meta, dq, dk, dv, w_query, w_key, w_value, x_nat)
    e_recv = across(e_send)

    t_keep = pl.pallas_call(
        triple_kernel,
        out_shape=sds((width, 3 * half + 128), BF),
        in_specs=[VM] * 7,
        out_specs=VM,
        cost_estimate=cost(2 * size * width * 3 * half, dq, dk, dv, a1),
    )(a1, dq, dk, dv, self_gain, cross_gain, ffn_gain)

    in_grad = pl.pallas_call(
        input_grad_kernel,
        out_shape=rows_b,
        in_specs=[VM] * 5,
        out_specs=VM,
        cost_estimate=cost(20 * own * width, e_keep, e_send, x_own, dy1),
    )(e_keep, e_recv, x_own, gain_self, dy1)
    in_rows = in_grad.reshape(charts, tokens, width)
    in_parts = [travel(pick(in_rows, d), d) for d in range(charts)]

    def total(parts):
        result = parts[0].astype(F32)
        for part in parts[1:]:
            result = result + part.astype(F32)
        return result

    def halve(parts, axis, index, name, perm):
        send = total(
            [lax.dynamic_index_in_dim(p, 1 - index, axis, keepdims=False) for p in parts]
        ).astype(BF)
        kept = [lax.dynamic_index_in_dim(p, index, axis, keepdims=False) for p in parts]
        return kept + [lax.ppermute(send, name, perm)]

    f_parts = halve([f_keep, f_recv], 0, side, "dp", swap_side)
    s_parts = [s_keep, s_recv]
    if nseq == 8:
        bits = (parity, lax.rem(place, 2), place // 2)
        perms = [[(s, s ^ (1 << b)) for s in range(8)] for b in range(3)]

        def over_seq(parts, axis):
            shape = parts[0].shape
            parts = [
                p.reshape(shape[:axis] + (2, 2, 2, shape[axis] // 8) + shape[axis + 1 :])
                for p in parts
            ]
            for b in range(3):
                parts = halve(parts, axis + 2 - b, bits[b], "seq", perms[b])
            return total(parts)

        f_sum = over_seq([p.reshape(3, width, wide) for p in f_parts], 1)
        s_sum = over_seq(s_parts, 1)
        t_sum = over_seq([t_keep], 0)
        g_gate, g_up = f_sum[0], f_sum[1]
        g_down = f_sum[2].reshape(width // 8, 2, wide // 2).transpose(2, 1, 0).reshape(wide // 2, width // 4)
    else:

        def over_seq(value, axis):
            return lax.psum_scatter(
                value.astype(BF), "seq", scatter_dimension=axis, tiled=True
            ).astype(F32)

        f_all = total(f_parts)
        g_two = over_seq(f_all[:2].reshape(2, width, wide), 1)
        g_gate, g_up = g_two[0], g_two[1]
        down = f_all[2].reshape(8, width // 8, 2, wide // 2).transpose(0, 3, 2, 1)
        g_down = over_seq(down.reshape(hidden, width // 4), 0)
        s_sum = over_seq(total(s_parts), 1)
        t_sum = over_seq(t_keep, 0)

    rows = t_sum.shape[0]
    quarter = half // 2
    t_sum = t_sum.astype(BF)
    squares = jnp.concatenate(
        [t_sum[:, : 3 * half].reshape(rows, 3, half).transpose(1, 0, 2), s_sum.astype(BF)], 0
    ).reshape(8, rows, 2, quarter)
    gains = t_sum[:, 3 * half :]
    padded = jnp.pad(gains, ((0, 0), (0, quarter - 128)))[None]

    def deliver(block, rule):
        part = lax.dynamic_index_in_dim(squares, block, 2, keepdims=False)
        return lax.ppermute(jnp.concatenate([part, padded], 0), "dp", dp_perm(rule)).astype(F32)

    done = deliver(side, lambda x, k: (k, x)) + deliver(1 - side, lambda x, k: (k, 1 - x))
    rest = lax.ppermute(gains, "dp", dp_perm(lambda x, k: (1 - k, x))).astype(F32) + lax.ppermute(
        gains, "dp", dp_perm(lambda x, k: (1 - k, 1 - x))
    ).astype(F32)
    gain_sum = done[8, :, :128] + rest

    def placed(parts):
        return pl.pallas_call(
            functools.partial(place_kernel, charts),
            out_shape=sds((charts,) + parts[0].shape, F32),
            in_specs=[SM] + [VM] * charts,
            out_specs=VM,
        )(meta, *parts)

    out_all = placed(out_parts)
    return (
        out_all[:, :tokens],
        placed(in_parts),
        out_all[:, tokens:],
        gain_sum[:, 0],
        done[0],
        done[1],
        done[2],
        done[7],
        gain_sum[:, 1],
        done[4],
        done[5],
        done[6],
        done[3],
        gain_sum[:, 2],
        g_gate,
        g_up,
        g_down,
    )


def solution(mesh):
    tok = P("dp", "seq", None)
    cut = P("seq", "dp")
    in_specs = (tok, tok, P("dp"), tok) + (P(),) * 14
    out_specs = (tok, tok, tok, P("seq"), cut, cut, cut, cut, P("seq"), cut, cut, cut, cut)
    out_specs += (P("seq"), cut, cut, cut)
    return jax.shard_map(
        functools.partial(local, mesh.shape["seq"]),
        mesh=mesh,
        in_specs=in_specs,
        out_specs=out_specs,
        check_vma=False,
    )
```

```python
import functools

import jax
import jax.numpy as jnp
from jax import lax
from jax.experimental import pallas as pl
from jax.experimental.pallas import tpu as pltpu
from jax.sharding import PartitionSpec as P

H = 12
EPSILON = 1e-06
NEGATIVE = -1e30
F32 = jnp.float32
BF = jnp.bfloat16
VM = pl.BlockSpec(memory_space=pltpu.VMEM)
SM = pl.BlockSpec(memory_space=pltpu.SMEM)
ROWS = 512
QB = 256


def dot(a, b):
    return lax.dot_general(a, b, (((1,), (0,)), ((), ())), preferred_element_type=F32)


def nt(a, b):
    return lax.dot_general(a, b, (((1,), (1,)), ((), ())), preferred_element_type=F32)


def lanes(width):
    return lax.broadcasted_iota(jnp.int32, (1, width), 1)


def inv_rms(v):
    return lax.rsqrt(jnp.mean(v * v, axis=-1, keepdims=True) + EPSILON)


def norm_back(e, v, gain):
    r = inv_rms(v)
    u = v * r
    eg = e * gain
    grad_v = (eg - u * jnp.mean(eg * u, axis=-1, keepdims=True)) * r
    return grad_v, jnp.sum(e * u, axis=0, keepdims=True)


def cost(flops, *arrays):
    total = sum(a.size * a.dtype.itemsize for a in arrays)
    return pl.CostEstimate(flops=int(flops), bytes_accessed=int(total), transcendentals=0)


def room(small, mib):
    return pltpu.CompilerParams(vmem_limit_bytes=mib << 20) if small else None


def sds(shape, dtype):
    return jax.ShapeDtypeStruct(shape, dtype)


def split3(value):
    hi = value.astype(BF).astype(F32)
    mid = (value - hi).astype(BF).astype(F32)
    lo = (value - hi - mid).astype(BF).astype(F32)
    return hi, mid, lo


def head_masks(h):
    lane = lanes(128)
    mine = ((lane < 64) if h == 0 else (lane >= 64)).astype(F32)
    base = 64 if h == 0 else 0
    marks = [(lane == base + i).astype(F32) for i in range(3)]
    return mine, marks


def add_marks(mine, marks, body, extra):
    hi, mid, lo = split3(extra)
    return (body * mine + hi * marks[0] + mid * marks[1] + lo * marks[2]).astype(BF)


def enter_kernel(
    charts, tokens, patches, meta, own, oth, gain, wq_hbm, wk_hbm, wv_hbm, ck_hbm, cv_hbm,
    x_own, a1, k, v, mem, mk, mv, o_keep, o_send, o_nat, q_aug,
    mem_scr, q, wq, wk, wv, ck, cv, sems,
):
    core, place = meta[0], meta[1]
    half = q.shape[1]
    width = a1.shape[1]
    size = q.shape[0]
    group = max(1, min(charts, ROWS // tokens))
    cols = pl.ds(pl.multiple_of(core * half, 128), half)
    copies = [
        pltpu.make_async_copy(src.at[:, cols], dst, sems.at[n])
        for n, (src, dst) in enumerate(((wq_hbm, wq), (wk_hbm, wk), (wv_hbm, wv)))
    ] + [
        pltpu.make_async_copy(src, dst, sems.at[3 + n])
        for n, (src, dst) in enumerate(((ck_hbm, ck), (cv_hbm, cv)))
    ]
    for copy in copies:
        copy.start()

    def one(ref, parity, first, fresh):
        x = ref[pl.ds(first, group), :tokens, :].reshape(group * tokens, width)
        xf = x.astype(F32)
        a = (xf * inv_rms(xf) * gain[...]).astype(BF)
        if fresh:
            for copy in copies[:3]:
                copy.wait()
        qq = (dot(a, wq[...]) * 0.125).astype(BF)
        kk = dot(a, wk[...]).astype(BF)
        vv = dot(a, wv[...]).astype(BF)
        for i in range(group):
            chunk = lax.rem(place - (first + i) + charts, charts)
            part = slice(i * tokens, (i + 1) * tokens)
            at = pl.ds(pl.multiple_of((2 * chunk + parity) * tokens, tokens), tokens)
            a1[at, :] = a[part]
            q[at, :] = qq[part]
            k[at, :] = kk[part]
            v[at, :] = vv[part]
            few = ref[first + i, tokens:, :].astype(F32)
            spot = pl.ds(pl.multiple_of((2 * chunk + parity) * patches, patches), patches)
            mem_scr[spot, :] = few
            if ref is own:
                x_own[pl.ds(pl.multiple_of(chunk * tokens, tokens), tokens), :] = x[part]

    for ref, parity in ((own, core), (oth, 1 - core)):
        if charts == group:
            one(ref, parity, 0, ref is own)
        else:
            if ref is own:
                for copy in copies[:3]:
                    copy.wait()
            lax.fori_loop(
                0, charts // group,
                lambda g, c, r=ref, p=parity: (one(r, p, g * group, False), c)[1], 0,
            )
    whole = mem_scr[...].astype(BF)
    mem[...] = whole
    for copy in copies[3:]:
        copy.wait()
    mk[...] = dot(whole, ck[...]).astype(BF)
    mv[...] = dot(whole, cv[...]).astype(BF)
    row = lax.broadcasted_iota(jnp.int32, (QB, QB), 0)
    col = lax.broadcasted_iota(jnp.int32, (QB, QB), 1)

    def pair(n):
        wide = pl.ds(pl.multiple_of(n * 128, 128), 128)

        def one_block(i, count):
            at = pl.ds(i * QB, QB) if count is not None else pl.ds(pl.multiple_of(i * QB, QB), QB)
            qp = q[at, wide]
            outs = []
            for h in (0, 1):
                mine, marks = head_masks(h)
                mb = mine.astype(BF)
                rest = (1.0 - mine).astype(BF)
                qh = qp * mb

                def scores(j):
                    return nt(qh, k[pl.ds(pl.multiple_of(j * QB, QB), QB), wide])

                def weigh(e, j):
                    vh = v[pl.ds(pl.multiple_of(j * QB, QB), QB), wide] * mb + rest
                    return dot(e.astype(BF), vh)

                diag = jnp.where(row >= col, scores(i), NEGATIVE)
                if count is not None:
                    parts = [scores(j) for j in range(count - 1)] + [diag]
                    top = parts[0]
                    for s in parts[1:]:
                        top = jnp.maximum(top, s)
                    top = jnp.max(top, axis=1, keepdims=True)
                    acc = weigh(jnp.exp(parts[0] - top), 0)
                    for j, s in enumerate(parts[1:]):
                        acc = acc + weigh(jnp.exp(s - top), j + 1)
                else:
                    top = jnp.max(diag, axis=1, keepdims=True)
                    acc = weigh(jnp.exp(diag - top), i)

                    def step(j, state):
                        top, acc = state
                        s = scores(j)
                        new = jnp.maximum(top, jnp.max(s, axis=1, keepdims=True))
                        return new, acc * jnp.exp(top - new) + weigh(jnp.exp(s - new), j)

                    top, acc = lax.fori_loop(0, i, step, (top, acc))
                total = pltpu.roll(acc, 64, 1)
                outs.append(acc / (total * mine + (1.0 - mine)) * mine)
                lse = top + jnp.log(acc * (1.0 - mine) + mine)
                q_aug[2 * n + h, at, :] = add_marks(mine, marks, qp.astype(F32), -lse)
            o = (outs[0] + outs[1]).astype(BF)
            o_nat[at, wide] = o
            per = QB // (2 * tokens)
            for c in range(per):
                even = o[2 * c * tokens : (2 * c + 1) * tokens]
                odd = o[(2 * c + 1) * tokens : (2 * c + 2) * tokens]
                spot = pl.ds(pl.multiple_of((i * per + c) * tokens, tokens), tokens)
                flag = jnp.full(even.shape, core, jnp.int32).astype(F32)
                ef, of = even.astype(F32), odd.astype(F32)
                o_keep[spot, wide] = jnp.where(flag == 0, ef, of).astype(BF)
                o_send[spot, wide] = jnp.where(flag == 0, of, ef).astype(BF)

        if size <= 1024:
            for i in range(size // QB):
                one_block(i, i + 1)
        else:
            lax.fori_loop(0, size // QB, lambda i, c: (one_block(i, None), c)[1], 0)

    lax.fori_loop(0, half // 128, lambda n, c: (pair(n), c)[1], 0)
    info = jnp.full((16, 128), meta[2], jnp.int32)
    o_send[size // 2 :, :128] = (info // 16).astype(F32).astype(BF)
    o_send[size // 2 :, 128:256] = lax.rem(info, 16).astype(F32).astype(BF)
    o_send[size // 2 :, 256:] = jnp.zeros((16, half - 256), BF)


def attend_back_kernel(
    tokens, meta, q_aug, k, v, o_nat, do_own, do_oth, dq, dk, dv, k_aug, v_aug, kt, dk_acc, dv_acc
):
    core = meta[0]
    size = k.shape[0]
    krow = lax.broadcasted_iota(jnp.int32, (QB, QB), 0)
    qcol = lax.broadcasted_iota(jnp.int32, (QB, QB), 1)
    kt[...] = k[...].astype(F32).T.astype(BF)
    for h in (0, 1):
        mine, marks = head_masks(h)
        ones = (marks[0] + marks[1] + marks[2]).astype(BF)
        k_aug[h] = k[...] * mine.astype(BF) + ones
        v_aug[h] = v[...] * mine.astype(BF) + ones
    dk_acc[...] = jnp.zeros_like(dk_acc)
    dv_acc[...] = jnp.zeros_like(dv_acc)

    def one_block(i, count):
        at = pl.ds(pl.multiple_of(i * QB, QB), QB)
        per = QB // (2 * tokens)
        pieces = []
        for c in range(per):
            spot = pl.ds(pl.multiple_of((i * per + c) * tokens, tokens), tokens)
            a, b = do_own[spot, :].astype(F32), do_oth[spot, :].astype(F32)
            flag = jnp.full(a.shape, core, jnp.int32)
            pieces += [jnp.where(flag == 0, a, b), jnp.where(flag == 0, b, a)]
        do = jnp.concatenate(pieces, 0)
        prod = do * o_nat[at, :].astype(F32)
        turned = []
        for h in (0, 1):
            mine, marks = head_masks(h)
            delta = jnp.sum(prod * mine, axis=1, keepdims=True)
            doa = add_marks(mine, marks, do, -delta)
            qa = q_aug[h, at, :]

            def one(j, dqt, diagonal):
                kat = pl.ds(pl.multiple_of(j * QB, QB), QB)
                s = nt(k_aug[h, kat, :], qa)
                if diagonal:
                    s = jnp.where(qcol >= krow, s, NEGATIVE)
                p = jnp.exp(s)
                ds = (p * nt(v_aug[h, kat, :], doa)).astype(BF)
                dv_acc[h, kat, :] += dot(p.astype(BF), doa)
                dk_acc[h, kat, :] += dot(ds, qa)
                return dqt + dot(kt[64 * h : 64 * h + 64, kat], ds)

            dqt = jnp.zeros((64, QB), F32)
            if count is not None:
                for j in range(count - 1):
                    dqt = one(j, dqt, False)
            else:
                dqt = lax.fori_loop(0, i, lambda j, c: one(j, c, False), dqt)
            turned.append(one(i, dqt, True))
        dq[at, :] = (jnp.concatenate(turned, 0).T * 0.125).astype(BF)

    if size <= 1024:
        for i in range(size // QB):
            one_block(i, i + 1)
    else:
        lax.fori_loop(0, size // QB, lambda i, c: (one_block(i, None), c)[1], 0)
    m0, m1 = head_masks(0)[0], head_masks(1)[0]
    dk[...] = (dk_acc[0] * m0 + dk_acc[1] * m1).astype(BF)
    dv[...] = (dv_acc[0] * m0 + dv_acc[1] * m1).astype(BF)


def cross_pair(ref, p):
    lane = lanes(128)
    piece = ref[:, 128 * p : 128 * p + 128]
    low = (lane < 64).astype(BF)
    high = (lane >= 64).astype(BF)
    return jnp.concatenate([piece * low, piece * high], 0)


def cross_kernel(
    meta, x, o_own, o_oth, info, w_out, g_cross, c_query, mk, mv, c_out, g_ffn,
    o1, y1, a2, cq, p2, o2, y2, a3,
):
    core = meta[0]
    half = o_own.shape[1]
    mine = pl.ds(pl.multiple_of(core * half, 128), half)
    other = pl.ds(pl.multiple_of((1 - core) * half, 128), half)
    o1[:, mine] = o_own[...]
    o1[:, other] = o_oth[...]
    first = x[...].astype(F32) + dot(o1[...], w_out[...])
    y1[...] = first
    n2 = (first * inv_rms(first) * g_cross[...]).astype(BF)
    a2[...] = n2
    query = dot(n2, c_query[...]).astype(BF)
    cq[...] = query
    patches = mk.shape[0]
    lane = lanes(2 * patches)
    low = lane < patches
    sent = info[0:1, 0:1].astype(F32) * 16.0 + info[0:1, 128:129].astype(F32)
    known = jnp.full((1, 1), meta[2], jnp.int32).astype(F32)
    same = jnp.full((1, 1), meta[0] - meta[4], jnp.int32) == 0
    count = jnp.where(same, known, sent)
    valid = jnp.where(low, lane, lane - patches).astype(F32) < count
    for p in range(H // 2):
        keys = cross_pair(mk, p)
        values = cross_pair(mv, p)
        s = nt(query[:, 128 * p : 128 * p + 128], keys) * 0.125
        s = jnp.where(valid, s, NEGATIVE)
        m0 = jnp.max(jnp.where(low, s, NEGATIVE), axis=1, keepdims=True)
        m1 = jnp.max(jnp.where(low, NEGATIVE, s), axis=1, keepdims=True)
        e = jnp.exp(s - jnp.where(low, m0, m1))
        l0 = jnp.sum(jnp.where(low, e, 0.0), axis=1, keepdims=True)
        l1 = jnp.sum(jnp.where(low, 0.0, e), axis=1, keepdims=True)
        w = e / jnp.where(low, l0, l1)
        p2[p] = w
        o2[:, 128 * p : 128 * p + 128] = dot(w.astype(BF), values).astype(BF)
    second = first + dot(o2[...], c_out[...])
    y2[...] = second
    a3[...] = (second * inv_rms(second) * g_ffn[...]).astype(BF)


def ffn_kernel(
    row_blocks, meta, a3, cot, y2, g_ffn, wg, wu, wd,
    out, dy2, dy2b, gain, gu_send, gu_keep, wd_send, wd_keep, acc, err, a3t, cott, dw,
):
    core = meta[0]
    i, r = pl.program_id(0), pl.program_id(1)
    rows = pl.ds(pl.multiple_of(r * ROWS, ROWS), ROWS)
    first, last = i == 0, i == pl.num_programs(0) - 1

    @pl.when(first)
    def _():
        a3t[:, rows] = a3[...].astype(F32).T.astype(BF)
        cott[:, rows] = cot[...].astype(F32).T.astype(BF)
        acc[rows, :] = y2[...]
        err[rows, :] = jnp.zeros((ROWS, err.shape[1]), F32)

    gate = dot(a3[...], wg[...])
    up = dot(a3[...], wu[...])
    square = gate * gate
    th = jnp.tanh(0.7978845608028654 * gate * (1.0 + 0.044715 * square))
    more = 0.5 * (1.0 + th)
    act = gate * more
    slope = more + 0.5 * gate * (1.0 - th * th) * (
        0.7978845608028654 * (1.0 + 3 * 0.044715 * square)
    )
    hidden = (act * up).astype(BF)
    dh = nt(cot[...], wd[...])
    d_gate = (dh * up * slope).astype(BF)
    d_up = (dh * act).astype(BF)
    acc[rows, :] += dot(hidden, wd[...])
    err[rows, :] += nt(d_gate, wg[...]) + nt(d_up, wu[...])
    terms = (dot(a3t[:, rows], d_gate), dot(a3t[:, rows], d_up), dot(cott[:, rows], hidden))
    if row_blocks > 1:
        for n, term in enumerate(terms):
            dw[n] = jnp.where(r == 0, 0.0, dw[n]) + term
        terms = (dw[0], dw[1], dw[2])

    def put():
        which = lax.rem(i, 2)
        width = terms[0].shape[1]
        for n in (0, 1):
            block = terms[n].astype(BF).reshape(8, terms[n].shape[0] // 8, width)

            @pl.when(which == core)
            def _(n=n, block=block):
                gu_keep[0, n] = block

            @pl.when(which != core)
            def _(n=n, block=block):
                gu_send[0, n] = block

        down = terms[2].astype(BF)
        per, part, wide = down.shape[0] // 4, down.shape[0] // 8, width // 2
        for b in range(4):
            for y in range(2):
                piece = down[b * per : (b + 1) * per, y * wide : (y + 1) * wide]
                packed = jnp.concatenate([piece[:part], piece[part:]], 1)

                @pl.when(core == b % 2)
                def _(b=b, y=y, packed=packed):
                    wd_keep[b // 2, y] = packed

                @pl.when(core != b % 2)
                def _(b=b, y=y, packed=packed):
                    wd_send[b // 2, y] = packed

    if row_blocks > 1:
        pl.when(r == row_blocks - 1)(put)
    else:
        put()

    @pl.when(last)
    def _():
        out[...] = acc[rows, :].astype(BF)
        back, gsum = norm_back(err[rows, :], y2[...], g_ffn[...])
        total = cot[...].astype(F32) + back
        dy2[...] = total
        dy2b[...] = total.astype(BF)
        gain[...] = jnp.where(r == 0, 0.0, gain[...]) + gsum


def cross_back_kernel(
    charts, patches_each, meta, dy2, dy2b, c_out, p2, mk, mv, cq, y1, g_cross, c_query, w_out,
    c_key, c_value,
    dcq, dmk, dmv, dy1, dy1b, do_keep, do_send, memg, gain, mk_acc, mv_acc, mem_scr,
):
    core = meta[0]
    r = pl.program_id(0)
    half = do_keep.shape[1]
    patches = mk.shape[0]
    lane = lanes(2 * patches)
    low = lane < patches
    left = (lanes(128) < 64).astype(F32)
    do2 = nt(dy2b[...], c_out[...]).astype(BF)
    fresh = r == 0
    for p in range(H // 2):
        at = slice(128 * p, 128 * p + 128)
        keys = cross_pair(mk, p)
        values = cross_pair(mv, p)
        w = p2[p]
        dp = nt(do2[:, at], values)
        prod = w * dp
        r0 = jnp.sum(jnp.where(low, prod, 0.0), axis=1, keepdims=True)
        r1 = jnp.sum(jnp.where(low, 0.0, prod), axis=1, keepdims=True)
        ds = w * (dp - jnp.where(low, r0, r1))
        dcq[:, at] = (dot(ds.astype(BF), keys) * 0.125).astype(BF)
        gk = dot(ds.T.astype(BF), cq[:, at]) * 0.125
        gv = dot(w.T.astype(BF), do2[:, at])
        gk = gk[:patches] * left + gk[patches:] * (1.0 - left)
        gv = gv[:patches] * left + gv[patches:] * (1.0 - left)
        mk_acc[:, at] = jnp.where(fresh, 0.0, mk_acc[:, at]) + gk
        mv_acc[:, at] = jnp.where(fresh, 0.0, mv_acc[:, at]) + gv
    err = nt(dcq[...], c_query[...])
    back, gsum = norm_back(err, y1[...], g_cross[...])
    total = dy2[...] + back
    dy1[...] = total
    tb = total.astype(BF)
    dy1b[...] = tb
    gain[...] = jnp.where(fresh, 0.0, gain[...]) + gsum
    do_keep[...] = nt(tb, w_out[pl.ds(pl.multiple_of(core * half, half), half), :]).astype(BF)
    rows = tb.shape[0]
    do_send[pl.ds(pl.multiple_of(r * rows, rows), rows), :] = nt(
        tb, w_out[pl.ds(pl.multiple_of((1 - core) * half, half), half), :]
    ).astype(BF)

    @pl.when(r == pl.num_programs(0) - 1)
    def _():
        gk, gv = mk_acc[...].astype(BF), mv_acc[...].astype(BF)
        dmk[...] = gk
        dmv[...] = gv
        mem_scr[...] = nt(gk, c_key[...]) + nt(gv, c_value[...])

        def gather(parity):
            return jnp.concatenate(
                [
                    mem_scr[pl.ds(pl.multiple_of((2 * a + parity) * patches_each, 8), patches_each), :]
                    for a in range(charts)
                ],
                0,
            )

        memg[...] = gather(core)
        away = gather(1 - core).astype(BF)
        extra = away.shape[0]
        base = do_send.shape[0] - 2 * extra
        do_send[base : base + extra, :] = away[:, :half]
        do_send[base + extra :, :] = away[:, half:]


def square_kernel(meta, o2, dy2b, a2, dcq, mem, dmk, dmv, o1, dy1b, send, keep):
    core = meta[0]
    half = keep.shape[2]
    mine = pl.ds(pl.multiple_of(core * half, 128), half)
    other = pl.ds(pl.multiple_of((1 - core) * half, 128), half)
    memt = mem[...].astype(F32).T.astype(BF)
    pairs = ((o2, dy2b), (a2, dcq), (None, dmk), (None, dmv), (o1, dy1b))
    for n, (left, right) in enumerate(pairs):
        turned = memt if left is None else left[...].astype(F32).T.astype(BF)
        send[n] = dot(turned, right[:, other]).astype(BF)
        keep[n] = dot(turned, right[:, mine]).astype(BF)


def entry_kernel(charts, tokens, meta, dq, dk, dv, wq, wk, wv, e_keep, e_send, scr):
    core = meta[0]
    half = dq.shape[1]
    cols = pl.ds(pl.multiple_of(core * half, 128), half)
    size = dq.shape[0]
    step = min(size, 2 * ROWS)
    per = step // (2 * tokens)

    def one(first):
        at = pl.ds(pl.multiple_of(first * step, step), step)
        e = nt(dq[at, :], wq[:, cols]) + nt(dk[at, :], wk[:, cols]) + nt(dv[at, :], wv[:, cols])
        scr[...] = e
        for c in range(per):
            spot = pl.ds(pl.multiple_of((first * per + c) * tokens, tokens), tokens)
            e_keep[spot, :] = scr[pl.ds(pl.multiple_of((2 * c + core) * tokens, tokens), tokens), :]
            e_send[spot, :] = scr[
                pl.ds(pl.multiple_of((2 * c + 1 - core) * tokens, tokens), tokens), :
            ].astype(BF)

    if size == step:
        one(0)
    else:
        lax.fori_loop(0, size // step, lambda g, c: (one(g), c)[1], 0)


def triple_kernel(split, meta, a1, dq, dk, dv, wq, wk, wv, column, g_cross, g_ffn, *outs):
    half = dq.shape[1]
    width = g_ffn.shape[1]
    core, parity = meta[0], meta[4]
    cols = pl.ds(pl.multiple_of(core * half, 128), half)
    turned = a1[...].astype(F32).T.astype(BF)
    out = outs[-1]
    gain = jnp.zeros((width, 1), F32)
    for n, (right, weight) in enumerate(((dq, wq), (dk, wk), (dv, wv))):
        block = dot(turned, right[...])
        gain += jnp.sum(block * weight[:, cols].astype(F32), axis=1, keepdims=True)
        out[:, n * half : (n + 1) * half] = block.astype(BF)
    gain = gain / column[...]
    stack = jnp.concatenate([g_cross[...], g_ffn[...], jnp.zeros((126, width), F32)], 0).T
    out[:, 3 * half :] = (jnp.where(lanes(128) == 2, gain, stack)).astype(BF)
    if split:
        send, keep = outs[0], outs[1]
        part = width // 8
        for n in range(4):
            keep[n] = out[pl.ds(pl.multiple_of((2 * n + parity) * part, part), part), :]
            send[n] = out[pl.ds(pl.multiple_of((2 * n + 1 - parity) * part, part), part), :]


def halve_kernel(which, meta, keep, recv, send, kept):
    i = meta[which]
    for o in range(keep.shape[0]):
        send[o] = (keep[o, 1 - i].astype(F32) + recv[o, 1 - i].astype(F32)).astype(BF)
        kept[o] = (keep[o, i].astype(F32) + recv[o, i].astype(F32)).astype(BF)


def mix_kernel(meta, gu_keep, gu_recv, wd_keep, wd_recv, send1, kept1, send2, kept2):
    side, parity = meta[3], meta[4]
    rows = gu_keep.shape[3]
    low = rows // 2

    def gu(x, w, s):
        return (gu_keep[x, w, s].astype(F32) + gu_recv[x, w, s].astype(F32)).astype(BF)

    def wd(x, s, part):
        return (wd_keep[x, s, part, :].astype(F32) + wd_recv[x, s, part, :].astype(F32)).astype(BF)

    for s in range(8):
        for x, to in ((1 - side, send1), (side, kept1)):
            to[s, :rows, :] = gu(x, 0, s)
            to[s, rows:, :] = wd(x, s, slice(0, low))
    for n in range(4):
        for x in range(2):
            for y, to in ((1 - parity, send2), (parity, kept2)):
                to[x, n, :rows, :] = gu(x, 1, 2 * n + y)
                to[x, n, rows:, :] = wd(x, 2 * n + y, slice(low, rows))


def input_grad_kernel(e_keep, e_recv, x, gain, dy1, out):
    err = e_keep[...] + e_recv[...].astype(F32)
    back, _ = norm_back(err, x[...].astype(F32), gain[...])
    out[...] = (dy1[...] + back).astype(BF)


def total(parts):
    result = parts[0].astype(F32)
    for part in parts[1:]:
        result = result + part.astype(F32)
    return result


def tie(value, *deps):
    return lax.optimization_barrier((value, deps))[0]


def turn_kernel(meta, base, recv, send, keep):
    v, z = meta[5], meta[6]
    send[v] = base[1 - z, v]
    send[1 - v] = recv[1 - z]
    keep[v] = base[z, v]
    keep[1 - v] = recv[z]


def turn_in_kernel(meta, base, recv, send, keep):
    v, z = meta[5], meta[6]
    send[z] = base[z, 1 - v]
    send[1 - z] = recv[1 - v]
    keep[z] = base[z, v]
    keep[1 - z] = recv[v]


def gather_kernel(meta, keep, recv, out):
    v = meta[5]
    for n in range(2):
        out[n, v] = keep[n]
        out[n, 1 - v] = recv[n]


def finish_kernel(meta, keep, recv, out):
    z = meta[6]
    out[z] = keep[...].astype(F32)
    out[1 - z] = recv[...].astype(F32)


def place_kernel(charts, meta, *refs):
    place = meta[1]
    out = refs[-1]
    for d in range(charts):
        out[lax.rem(place - d + charts, charts)] = refs[d][...].astype(out.dtype)


def local(
    nseq, inputs, memory, patch_count, cotangent, norm_self, w_query, w_key, w_value, w_out,
    norm_cross, c_query, c_key, c_value, c_out, norm_ffn, w_gate, w_up, w_down,
):
    charts, tokens, width = inputs.shape
    patches_each = memory.shape[1]
    size = charts * 2 * tokens
    own = charts * tokens
    patches = patches_each * nseq
    half = width // 2
    small = size <= 1024
    hidden = w_gate.shape[1]
    blocks = own // ROWS
    dp = lax.axis_index("dp")
    seq = lax.axis_index("seq")
    side, core = dp // 2, lax.rem(dp, 2)
    place, parity = seq // 2, lax.rem(seq, 2)

    def shift(d):
        return [
            ((2 * x + k) * nseq + 2 * a + b, (2 * x + b) * nseq + 2 * ((a + d) % charts) + k)
            for x in range(2)
            for k in range(2)
            for a in range(charts)
            for b in range(2)
        ]

    def dp_perm(rule):
        return [(2 * x + k, 2 * rule(x, k)[0] + rule(x, k)[1]) for x in range(2) for k in range(2)]

    swap_core = dp_perm(lambda x, k: (x, 1 - k))
    swap_side = dp_perm(lambda x, k: (1 - x, k))

    def across(value):
        return lax.ppermute(value, "dp", swap_core)

    def travel(value, d):
        return lax.ppermute(value, ("dp", "seq"), shift(d))

    def pick(value, d):
        return lax.dynamic_index_in_dim(value, lax.rem(place + d, charts), 0, keepdims=False)

    gain_self, gain_cross, gain_ffn = (g.reshape(1, width) for g in (norm_self, norm_cross, norm_ffn))
    count = lax.dynamic_index_in_dim(patch_count, place, 0, keepdims=False)
    meta = jnp.stack(
        [core, place, count, side, parity, lax.rem(place, 2), place // 2]
    ).astype(jnp.int32)

    trade = [
        ((2 * x + k) * nseq + 2 * a + b, (2 * x + b) * nseq + 2 * a + k)
        for x in range(2)
        for k in range(2)
        for a in range(charts)
        for b in range(2)
    ]
    flips = {
        name: [(s, s ^ (1 << bit)) for s in range(nseq)] for bit, name in enumerate("yvz")
    }
    low_bit, high_bit = lax.rem(place, 2), place // 2

    mine = jnp.stack(
        [
            travel(jnp.concatenate([pick(inputs, d), pick(memory, d)], 0), d)
            for d in range(charts)
        ]
    )
    theirs = across(mine)
    if small:
        cot_base = lax.ppermute(cotangent, ("dp", "seq"), trade)
        cot_base = cot_base.reshape(2, 2, tokens, width)
        cot_away = lax.dynamic_index_in_dim(cot_base, 1 - high_bit, 0, keepdims=False)
        cot_got = lax.ppermute(cot_away, "seq", flips["z"])
        theirs = tie(theirs, cot_away)
    else:
        cot_parts = [travel(pick(cotangent, d), d) for d in range(charts)]
    pairs = half // 128
    pair_spec = pl.BlockSpec((size, 128), lambda p, m: (0, p))
    own_spec = pl.BlockSpec((own, 128), lambda p, m: (0, p))
    aug_spec = pl.BlockSpec((2, size, 128), lambda p, m: (p, 0, 0))
    x_own, a1, k, v, mem, mk, mv, o_keep, o_send, o_nat, q_aug = pl.pallas_call(
        functools.partial(enter_kernel, charts, tokens, patches_each),
        compiler_params=room(small, 20),
        out_shape=(
            sds((own, width), BF), sds((size, width), BF), sds((size, half), BF),
            sds((size, half), BF), sds((patches, width), BF), sds((patches, width), BF),
            sds((patches, width), BF), sds((own, half), BF), sds((own + 16, half), BF),
            sds((size, half), BF), sds((2 * pairs, size, 128), BF),
        ),
        in_specs=[SM] + [VM] * 3 + [pl.BlockSpec(memory_space=pltpu.HBM)] * 5,
        out_specs=[VM] * 11,
        scratch_shapes=[
            pltpu.VMEM((patches, width), F32), pltpu.VMEM((size, half), BF),
            pltpu.VMEM((width, half), BF), pltpu.VMEM((width, half), BF),
            pltpu.VMEM((width, half), BF), pltpu.VMEM((width, width), BF),
            pltpu.VMEM((width, width), BF), pltpu.SemaphoreType.DMA((5,)),
        ],
        cost_estimate=cost(2 * size * width * 3 * half, mine, theirs, w_query, w_key, w_value),
    )(meta, mine, theirs, gain_self, w_query, w_key, w_value, c_key, c_value)
    if small:
        part = sds((2, tokens, width), BF)
        cot_send, cot_keep = pl.pallas_call(
            turn_in_kernel,
            compiler_params=room(small, 6),
            out_shape=(part, part),
            in_specs=[SM, VM, VM],
            out_specs=[VM] * 2,
        )(meta, cot_base, cot_got)
        cot_got = lax.ppermute(cot_send, "seq", flips["v"])
        o_recv = tie(across(o_send), cot_send)
    else:
        o_recv = across(o_send)

    row_spec = pl.BlockSpec((ROWS, width), lambda r: (r, 0))
    half_spec = pl.BlockSpec((ROWS, half), lambda r: (r, 0))
    p2_spec = pl.BlockSpec((H // 2, ROWS, 2 * patches), lambda r: (0, r, 0))

    def fixed(shape, spaces=1):
        if spaces == 1:
            return pl.BlockSpec(shape, lambda r: (0,) * len(shape))
        return pl.BlockSpec(shape, lambda i, r: (0,) * len(shape))

    square = fixed((width, width))
    one_row = fixed((1, width))
    patch_spec = fixed((patches, width))
    rows_f = sds((own, width), F32)
    rows_b = sds((own, width), BF)
    o1, y1, a2, cq, p2, o2, y2, a3 = pl.pallas_call(
        cross_kernel,
        compiler_params=room(small, 16),
        out_shape=(
            rows_b, rows_f, rows_b, rows_b, sds((H // 2, own, 2 * patches), F32), rows_b, rows_f,
            rows_b,
        ),
        grid=(blocks,),
        in_specs=[
            SM, row_spec, half_spec, half_spec, pl.BlockSpec((16, half), lambda r: (own // 16, 0)),
            square, one_row, square, patch_spec, patch_spec, square, one_row,
        ],
        out_specs=[row_spec] * 4 + [p2_spec] + [row_spec] * 3,
        cost_estimate=cost(6 * own * width * width, w_out, c_query, c_out, rows_f, rows_f),
    )(meta, x_own, o_keep, o_recv, o_recv, w_out, gain_cross, c_query, mk, mv, c_out, gain_ffn)

    def placed(parts, dtype):
        return pl.pallas_call(
            functools.partial(place_kernel, charts),
            compiler_params=room(small, 6),
            out_shape=sds((charts,) + parts[0].shape, dtype),
            in_specs=[SM] + [VM] * charts,
            out_specs=VM,
        )(meta, *parts)

    if small:
        cot = pl.pallas_call(
            gather_kernel,
            compiler_params=room(small, 6),
            out_shape=sds((2, 2, tokens, width), BF),
            in_specs=[SM, VM, VM],
            out_specs=VM,
        )(meta, cot_keep, tie(cot_got, y2)).reshape(own, width)
    else:
        cot = placed(cot_parts, BF).reshape(own, width)
    wide = hidden // 4
    last = 3
    gu_pack = sds((2, 2, 8, width // 8, wide), BF)
    wd_pack = sds((2, 8, width // 8, wide), BF)
    gu_spec = pl.BlockSpec((1, 2, 8, width // 8, wide), lambda i, r: (i // 2, 0, 0, 0, 0))
    wd_spec = pl.BlockSpec((2, 2, width // 8, wide), lambda i, r: (0, i, 0, 0))
    frow = pl.BlockSpec((ROWS, width), lambda i, r: (r, 0))
    lrow = pl.BlockSpec((ROWS, width), lambda i, r: (r * (i // last), 0))
    out_b, dy2, dy2b, ffn_gain, gu_send, gu_keep, wd_send, wd_keep = pl.pallas_call(
        functools.partial(ffn_kernel, blocks),
        compiler_params=room(small, 30),
        out_shape=(rows_b, rows_f, rows_b, sds((1, width), F32)) + (gu_pack,) * 2 + (wd_pack,) * 2,
        grid=(4, blocks),
        in_specs=[
            SM, frow, frow, frow, fixed((1, width), 2),
            pl.BlockSpec((width, wide), lambda i, r: (0, i)),
            pl.BlockSpec((width, wide), lambda i, r: (0, i)),
            pl.BlockSpec((wide, width), lambda i, r: (i, 0)),
        ],
        out_specs=[lrow, lrow, lrow, fixed((1, width), 2), gu_spec, gu_spec, wd_spec, wd_spec],
        scratch_shapes=[
            pltpu.VMEM((own, width), F32), pltpu.VMEM((own, width), F32),
            pltpu.VMEM((width, own), BF), pltpu.VMEM((width, own), BF),
            pltpu.VMEM((3, width, wide) if blocks > 1 else (3, 8, 128), F32),
        ],
        cost_estimate=cost(18 * own * width * hidden, w_gate, w_up, w_down, rows_f, rows_f),
    )(meta, a3, cot, y2, gain_ffn, w_gate, w_up, w_down)
    gu_recv, wd_recv = across(gu_send), across(wd_send)

    def back_first(rows):
        return lax.ppermute(rows, ("dp", "seq"), trade)

    def back_second(rows):
        rows = rows.reshape((2, 2) + rows.shape[1:])
        send = lax.dynamic_index_in_dim(rows, 1 - low_bit, 1, keepdims=False)
        return rows, lax.ppermute(send, "seq", flips["v"])

    def back_third(rows, got):
        shape = sds(got.shape, BF)
        send, keep = pl.pallas_call(
            turn_kernel,
            compiler_params=room(small, 6),
            out_shape=(shape, shape),
            in_specs=[SM, VM, VM],
            out_specs=[VM] * 2,
        )(meta, rows, got)
        return keep, lax.ppermute(send, "seq", flips["z"])

    def back_last(keep, got):
        return pl.pallas_call(
            finish_kernel,
            compiler_params=room(small, 8),
            out_shape=sds((2,) + got.shape, F32),
            in_specs=[SM, VM, VM],
            out_specs=VM,
        )(meta, keep, got).reshape((charts,) + got.shape[1:])

    out_rows = out_b.reshape(charts, tokens, width)
    if small:
        out_rows = back_first(out_rows)
    else:
        out_parts = [travel(pick(out_rows, d), d) for d in range(charts)]

    dcq, dmk, dmv, dy1, dy1b, do_keep, do_send, memg, cross_gain = pl.pallas_call(
        functools.partial(cross_back_kernel, charts, patches_each),
        compiler_params=room(small, 16),
        out_shape=(
            rows_b, sds((patches, width), BF), sds((patches, width), BF), rows_f, rows_b,
            sds((own, half), BF), sds((own + patches, half), BF),
            sds((patches // 2, width), F32), sds((1, width), F32),
        ),
        grid=(blocks,),
        in_specs=[
            SM, row_spec, row_spec, square, p2_spec, patch_spec, patch_spec, row_spec, row_spec,
            one_row, square, square, square, square,
        ],
        out_specs=[
            row_spec, patch_spec, patch_spec, row_spec, row_spec, half_spec,
            fixed((own + patches, half)), fixed((patches // 2, width)), one_row,
        ],
        scratch_shapes=[pltpu.VMEM((patches, width), F32)] * 3,
        cost_estimate=cost(6 * own * width * width, w_out, c_query, c_out, rows_f, rows_f),
    )(meta, dy2, dy2b, c_out, p2, mk, mv, cq, y1, gain_cross, c_query, w_out, c_key, c_value)
    do_recv = across(do_send)

    def halve(which, keep, recv, outer):
        shape = (outer, 2, keep.size // (outer * 2 * keep.shape[-1]), keep.shape[-1])
        piece = sds((outer,) + shape[2:], BF)
        return pl.pallas_call(
            functools.partial(halve_kernel, which),
            compiler_params=room(small, 10),
            out_shape=(piece, piece),
            in_specs=[SM, VM, VM],
            out_specs=[VM] * 2,
        )(meta, keep.reshape(shape), recv.reshape(shape))

    def over(name, value):
        if name == "x":
            return lax.ppermute(value, "dp", swap_side)
        return lax.ppermute(value, "seq", flips[name])

    s_send, s_keep = pl.pallas_call(
        square_kernel,
        compiler_params=room(small, 16),
        out_shape=(sds((5, width, half), BF), sds((5, width, half), BF)),
        in_specs=[SM] + [VM] * 9,
        out_specs=[VM] * 2,
        cost_estimate=cost(6 * own * width * width, o1, o2, a2, dcq, dy2b, dy1b),
    )(meta, o2, dy2b, a2, dcq, mem, dmk, dmv, o1, dy1b)
    s_recv = across(s_send)

    few = patches // 2
    memg_recv = jnp.concatenate([do_recv[own : own + few], do_recv[own + few :]], 1)
    memg_own = (memg + memg_recv.astype(F32)).astype(BF).reshape(charts, patches_each, width)
    if small:
        out_rows, out_got = back_second(tie(out_rows, dy1b))
        gu_keep = tie(gu_keep, gu_recv, wd_recv, out_rows)
        f1 = sds((8, 3 * width // 16, wide), BF)
        f2 = sds((2, 4, 3 * width // 16, wide), BF)
        f1_send, f1_keep, f2_send, f2_keep = pl.pallas_call(
            mix_kernel,
            compiler_params=room(small, 16),
            out_shape=(f1, f1, f2, f2),
            in_specs=[SM] + [VM] * 4,
            out_specs=[VM] * 4,
        )(meta, gu_keep, gu_recv, wd_keep, wd_recv)
        f1_recv, f2_recv = over("x", f1_send), over("y", f2_send)
        s_send, s_keep = halve(5, s_keep, tie(s_recv, f1_send), 10)
        s_recv = over("v", s_send)
        out_keep, out_got = back_third(out_rows, tie(out_got, s_send))
        do_recv = tie(do_recv, s_send, out_keep)

    dq, dk, dv = pl.pallas_call(
        functools.partial(attend_back_kernel, tokens),
        compiler_params=room(small, 14),
        out_shape=(sds((size, half), BF),) * 3,
        grid_spec=pltpu.PrefetchScalarGridSpec(
            num_scalar_prefetch=1,
            grid=(pairs,),
            in_specs=[aug_spec, pair_spec, pair_spec, pair_spec, own_spec, own_spec],
            out_specs=[pair_spec] * 3,
            scratch_shapes=[
                pltpu.VMEM((2, size, 128), BF), pltpu.VMEM((2, size, 128), BF),
                pltpu.VMEM((128, size), BF),
                pltpu.VMEM((2, size, 128), F32), pltpu.VMEM((2, size, 128), F32),
            ],
        ),
        cost_estimate=cost(10 * size * size * half, k, v, q_aug),
    )(meta, q_aug, k, v, o_nat, do_keep, do_recv)

    if small:
        dq = tie(dq, f1_recv, f2_recv, out_got)
    t_whole = sds((width, 3 * half + 128), BF)
    t_piece = sds((4, width // 8, 3 * half + 128), BF)
    t_out = pl.pallas_call(
        functools.partial(triple_kernel, small),
        compiler_params=room(small, 14),
        out_shape=(t_piece, t_piece) if small else t_whole,
        in_specs=[SM] + [VM] * 10,
        out_specs=[VM] * 2 if small else VM,
        scratch_shapes=[pltpu.VMEM((width, 3 * half + 128), BF)] if small else [],
        cost_estimate=cost(2 * size * width * 3 * half, dq, dk, dv, a1),
    )(
        meta, a1, dq, dk, dv, w_query, w_key, w_value, norm_self.reshape(width, 1), cross_gain,
        ffn_gain,
    )
    if small:
        t_send, t_keep = t_out
        t_recv = over("y", t_send)
        dq = tie(dq, t_send)

    e_keep, e_send = pl.pallas_call(
        functools.partial(entry_kernel, charts, tokens),
        compiler_params=room(small, 14),
        out_shape=(rows_f, rows_b),
        in_specs=[SM] + [VM] * 6,
        out_specs=[VM] * 2,
        scratch_shapes=[pltpu.VMEM((min(size, 2 * ROWS), width), F32)],
        cost_estimate=cost(2 * size * width * 3 * half, dq, dk, dv, rows_f),
    )(meta, dq, dk, dv, w_query, w_key, w_value)
    e_recv = across(e_send)
    if small:
        f2_send, f2_keep = halve(3, f2_keep, tie(f2_recv, e_send), 1)
        f2_recv = over("x", f2_send)
        e_recv = tie(e_recv, f2_send)

    in_grad = pl.pallas_call(
        input_grad_kernel,
        compiler_params=room(small, 8),
        out_shape=rows_b,
        in_specs=[VM] * 5,
        out_specs=VM,
        cost_estimate=cost(20 * own * width, e_keep, e_send, x_own, dy1),
    )(e_keep, e_recv, x_own, gain_self, dy1)
    in_rows = jnp.concatenate([in_grad.reshape(charts, tokens, width), memg_own], 1)
    if small:
        in_rows = back_first(in_rows)
        s_send, s_keep = halve(3, s_keep, tie(s_recv, in_grad), 20)
        s_recv = over("x", s_send)
        f2_send, f2_keep = halve(5, f2_keep, tie(f2_recv, s_send), 2)
        f2_recv = over("v", f2_send)
        t_send, t_keep = halve(5, t_keep, tie(t_recv, f2_send), 2)
        t_recv = over("v", t_send)
        f1_send, f1_keep = halve(4, f1_keep, tie(f1_recv, t_send), 4)
        f1_recv = over("y", f1_send)
        in_rows, in_got = back_second(tie(in_rows, f1_send))
        f2_send, f2_keep = halve(6, f2_keep, tie(f2_recv, in_rows), 1)
        f2_recv = over("z", f2_send)
        t_send, t_keep = halve(6, t_keep, tie(t_recv, f2_send), 1)
        t_recv = over("z", t_send)
        s_send, s_keep = halve(4, s_keep, tie(s_recv, t_send), 10)
        s_recv = over("y", s_send)
        f1_send, f1_keep = halve(5, f1_keep, tie(f1_recv, s_send), 2)
        f1_recv = over("v", f1_send)
        s_send, s_keep = halve(6, s_keep, tie(s_recv, f1_send), 5)
        s_recv = over("z", s_send)
        f1_send, f1_keep = halve(6, f1_keep, tie(f1_recv, s_send), 1)
        f1_recv = over("z", f1_send)
        in_keep, in_got = back_third(in_rows, tie(in_got, f1_send))
    else:
        in_parts = [travel(pick(in_rows, d), d) for d in range(charts)]

    if small:
        f1_sum = total([f1_keep, f1_recv]).reshape(3 * width // 16, wide)
        f2_sum = total([f2_keep, f2_recv]).reshape(3 * width // 16, wide)
        t_sum = total([t_keep, t_recv]).reshape(width // 8, 3 * half + 128)
        s_part = total([s_keep, s_recv])
        s_zero = jnp.zeros_like(s_part)
        s_sum = jnp.concatenate(
            [jnp.where(side == 0, s_part, s_zero), jnp.where(side == 0, s_zero, s_part)], 1
        )
        g_gate, g_up = f1_sum[: width // 8], f2_sum[: width // 8]
        g_down = jnp.concatenate([f1_sum[width // 8 :], f2_sum[width // 8 :]], 0)
        g_down = g_down.reshape(width // 8, 2, wide // 2).transpose(2, 1, 0)
        g_down = g_down.reshape(wide // 2, width // 4)
    else:

        def over_seq(value, axis):
            return lax.psum_scatter(
                value.astype(BF), "seq", scatter_dimension=axis, tiled=True
            ).astype(F32)

        def over_side(parts):
            sends = [lax.dynamic_index_in_dim(p, 1 - side, 0, keepdims=False) for p in parts]
            kept = [lax.dynamic_index_in_dim(p, side, 0, keepdims=False) for p in parts]
            return total(kept + [lax.ppermute(total(sends).astype(BF), "dp", swap_side)])

        g_two = over_seq(over_side([gu_keep, gu_recv]).reshape(2, width, wide), 1)
        g_gate, g_up = g_two[0], g_two[1]
        down = over_side([wd_keep, wd_recv]).reshape(8, width // 8, 2, wide // 2)
        g_down = over_seq(down.transpose(0, 3, 2, 1).reshape(hidden, width // 4), 0)
        s_sum = over_seq(total([s_keep, s_recv]), 1)
        t_sum = over_seq(t_out, 0)

    rows = t_sum.shape[0]
    quarter = half // 2
    t_sum = t_sum.astype(BF)
    squares = jnp.concatenate(
        [t_sum[:, : 3 * half].reshape(rows, 3, half).transpose(1, 0, 2), s_sum.astype(BF)], 0
    ).reshape(8, rows, 2, quarter)
    gains = t_sum[:, 3 * half :]
    padded = jnp.pad(gains, ((0, 0), (0, quarter - 128)))[None]

    def deliver(block, rule):
        part = lax.dynamic_index_in_dim(squares, block, 2, keepdims=False)
        return lax.ppermute(jnp.concatenate([part, padded], 0), "dp", dp_perm(rule)).astype(F32)

    done = deliver(side, lambda x, k: (k, x)) + deliver(1 - side, lambda x, k: (k, 1 - x))
    rest = lax.ppermute(gains, "dp", dp_perm(lambda x, k: (1 - k, x))).astype(F32) + lax.ppermute(
        gains, "dp", dp_perm(lambda x, k: (1 - k, 1 - x))
    ).astype(F32)
    gain_sum = done[8, :, :128] + rest

    if small:
        out_all, in_all = back_last(out_keep, out_got), back_last(in_keep, in_got)
    else:
        out_all, in_all = placed(out_parts, F32), placed(in_parts, F32)
    return (
        out_all,
        in_all[:, :tokens],
        in_all[:, tokens:],
        gain_sum[:, 2],
        done[0],
        done[1],
        done[2],
        done[7],
        gain_sum[:, 0],
        done[4],
        done[5],
        done[6],
        done[3],
        gain_sum[:, 1],
        g_gate,
        g_up,
        g_down,
    )


def solution(mesh):
    tok = P("dp", "seq", None)
    cut = P("seq", "dp")
    in_specs = (tok, tok, P("dp"), tok) + (P(),) * 14
    out_specs = (tok, tok, tok, P("seq"), cut, cut, cut, cut, P("seq"), cut, cut, cut, cut)
    out_specs += (P("seq"), cut, cut, cut)
    return jax.shard_map(
        functools.partial(local, mesh.shape["seq"]),
        mesh=mesh,
        in_specs=in_specs,
        out_specs=out_specs,
        check_vma=False,
    )
```

```python
import functools

import jax
import jax.numpy as jnp
from jax import lax
from jax.experimental import pallas as pl
from jax.experimental.pallas import tpu as pltpu
from jax.sharding import PartitionSpec as P

H = 12
EPSILON = 1e-06
NEGATIVE = -1e30
F32 = jnp.float32
BF = jnp.bfloat16
VM = pl.BlockSpec(memory_space=pltpu.VMEM)
SM = pl.BlockSpec(memory_space=pltpu.SMEM)
ROWS = 512
QB = 256


def dot(a, b):
    return lax.dot_general(a, b, (((1,), (0,)), ((), ())), preferred_element_type=F32)


def nt(a, b):
    return lax.dot_general(a, b, (((1,), (1,)), ((), ())), preferred_element_type=F32)


def lanes(width):
    return lax.broadcasted_iota(jnp.int32, (1, width), 1)


def inv_rms(v):
    return lax.rsqrt(jnp.mean(v * v, axis=-1, keepdims=True) + EPSILON)


def norm_back(e, v, gain):
    r = inv_rms(v)
    u = v * r
    eg = e * gain
    grad_v = (eg - u * jnp.mean(eg * u, axis=-1, keepdims=True)) * r
    return grad_v, jnp.sum(e * u, axis=0, keepdims=True)


def cost(flops, *arrays):
    total = sum(a.size * a.dtype.itemsize for a in arrays)
    return pl.CostEstimate(flops=int(flops), bytes_accessed=int(total), transcendentals=0)


def room(small, mib):
    return pltpu.CompilerParams(vmem_limit_bytes=mib << 20) if small else None


def sds(shape, dtype):
    return jax.ShapeDtypeStruct(shape, dtype)


def split3(value):
    hi = value.astype(BF).astype(F32)
    mid = (value - hi).astype(BF).astype(F32)
    lo = (value - hi - mid).astype(BF).astype(F32)
    return hi, mid, lo


def head_masks(h):
    lane = lanes(128)
    mine = ((lane < 64) if h == 0 else (lane >= 64)).astype(F32)
    base = 64 if h == 0 else 0
    marks = [(lane == base + i).astype(F32) for i in range(3)]
    return mine, marks


def add_marks(mine, marks, body, extra):
    hi, mid, lo = split3(extra)
    return (body * mine + hi * marks[0] + mid * marks[1] + lo * marks[2]).astype(BF)


def enter_kernel(
    charts, tokens, patches, meta, own, oth, gain, wq_hbm, wk_hbm, wv_hbm, ck_hbm, cv_hbm,
    x_own, a1, k, v, mem, mk, mv, o_keep, o_send, o_nat, q_aug,
    mem_scr, q, wq, wk, wv, ck, cv, sems,
):
    core, place = meta[0], meta[1]
    half = q.shape[1]
    width = a1.shape[1]
    size = q.shape[0]
    group = max(1, min(charts, ROWS // tokens))
    cols = pl.ds(pl.multiple_of(core * half, 128), half)
    copies = [
        pltpu.make_async_copy(src.at[:, cols], dst, sems.at[n])
        for n, (src, dst) in enumerate(((wq_hbm, wq), (wk_hbm, wk), (wv_hbm, wv)))
    ] + [
        pltpu.make_async_copy(src, dst, sems.at[3 + n])
        for n, (src, dst) in enumerate(((ck_hbm, ck), (cv_hbm, cv)))
    ]
    for copy in copies:
        copy.start()

    def one(ref, parity, first, fresh):
        x = ref[pl.ds(first, group), :tokens, :].reshape(group * tokens, width)
        xf = x.astype(F32)
        a = (xf * inv_rms(xf) * gain[...]).astype(BF)
        if fresh:
            for copy in copies[:3]:
                copy.wait()
        qq = (dot(a, wq[...]) * 0.125).astype(BF)
        kk = dot(a, wk[...]).astype(BF)
        vv = dot(a, wv[...]).astype(BF)
        for i in range(group):
            chunk = lax.rem(place - (first + i) + charts, charts)
            part = slice(i * tokens, (i + 1) * tokens)
            at = pl.ds(pl.multiple_of((2 * chunk + parity) * tokens, tokens), tokens)
            a1[at, :] = a[part]
            q[at, :] = qq[part]
            k[at, :] = kk[part]
            v[at, :] = vv[part]
            few = ref[first + i, tokens:, :].astype(F32)
            spot = pl.ds(pl.multiple_of((2 * chunk + parity) * patches, patches), patches)
            mem_scr[spot, :] = few
            if ref is own:
                x_own[pl.ds(pl.multiple_of(chunk * tokens, tokens), tokens), :] = x[part]

    for ref, parity in ((own, core), (oth, 1 - core)):
        if charts == group:
            one(ref, parity, 0, ref is own)
        else:
            if ref is own:
                for copy in copies[:3]:
                    copy.wait()
            lax.fori_loop(
                0, charts // group,
                lambda g, c, r=ref, p=parity: (one(r, p, g * group, False), c)[1], 0,
            )
    whole = mem_scr[...].astype(BF)
    mem[...] = whole
    for copy in copies[3:]:
        copy.wait()
    mk[...] = dot(whole, ck[...]).astype(BF)
    mv[...] = dot(whole, cv[...]).astype(BF)
    row = lax.broadcasted_iota(jnp.int32, (QB, QB), 0)
    col = lax.broadcasted_iota(jnp.int32, (QB, QB), 1)

    def pair(n):
        wide = pl.ds(pl.multiple_of(n * 128, 128), 128)

        def one_block(i, count):
            at = pl.ds(i * QB, QB) if count is not None else pl.ds(pl.multiple_of(i * QB, QB), QB)
            qp = q[at, wide]
            outs = []
            for h in (0, 1):
                mine, marks = head_masks(h)
                mb = mine.astype(BF)
                rest = (1.0 - mine).astype(BF)
                qh = qp * mb

                def scores(j):
                    return nt(qh, k[pl.ds(pl.multiple_of(j * QB, QB), QB), wide])

                def weigh(e, j):
                    vh = v[pl.ds(pl.multiple_of(j * QB, QB), QB), wide] * mb + rest
                    return dot(e.astype(BF), vh)

                diag = jnp.where(row >= col, scores(i), NEGATIVE)
                if count is not None:
                    parts = [scores(j) for j in range(count - 1)] + [diag]
                    top = parts[0]
                    for s in parts[1:]:
                        top = jnp.maximum(top, s)
                    top = jnp.max(top, axis=1, keepdims=True)
                    acc = weigh(jnp.exp(parts[0] - top), 0)
                    for j, s in enumerate(parts[1:]):
                        acc = acc + weigh(jnp.exp(s - top), j + 1)
                else:
                    top = jnp.max(diag, axis=1, keepdims=True)
                    acc = weigh(jnp.exp(diag - top), i)

                    def step(j, state):
                        top, acc = state
                        s = scores(j)
                        new = jnp.maximum(top, jnp.max(s, axis=1, keepdims=True))
                        return new, acc * jnp.exp(top - new) + weigh(jnp.exp(s - new), j)

                    top, acc = lax.fori_loop(0, i, step, (top, acc))
                total = pltpu.roll(acc, 64, 1)
                outs.append(acc / (total * mine + (1.0 - mine)) * mine)
                lse = top + jnp.log(acc * (1.0 - mine) + mine)
                q_aug[2 * n + h, at, :] = add_marks(mine, marks, qp.astype(F32), -lse)
            o = (outs[0] + outs[1]).astype(BF)
            o_nat[at, wide] = o
            per = QB // (2 * tokens)
            for c in range(per):
                even = o[2 * c * tokens : (2 * c + 1) * tokens]
                odd = o[(2 * c + 1) * tokens : (2 * c + 2) * tokens]
                spot = pl.ds(pl.multiple_of((i * per + c) * tokens, tokens), tokens)
                flag = jnp.full(even.shape, core, jnp.int32).astype(F32)
                ef, of = even.astype(F32), odd.astype(F32)
                o_keep[spot, wide] = jnp.where(flag == 0, ef, of).astype(BF)
                o_send[spot, wide] = jnp.where(flag == 0, of, ef).astype(BF)

        if size <= 1024:
            for i in range(size // QB):
                one_block(i, i + 1)
        else:
            lax.fori_loop(0, size // QB, lambda i, c: (one_block(i, None), c)[1], 0)

    lax.fori_loop(0, half // 128, lambda n, c: (pair(n), c)[1], 0)
    info = jnp.full((16, 128), meta[2], jnp.int32)
    o_send[size // 2 :, :128] = (info // 16).astype(F32).astype(BF)
    o_send[size // 2 :, 128:256] = lax.rem(info, 16).astype(F32).astype(BF)
    o_send[size // 2 :, 256:] = jnp.zeros((16, half - 256), BF)


def attend_back_kernel(
    tokens, meta, q_aug, k, v, o_nat, do_own, do_oth, dq, dk, dv, k_aug, v_aug, kt, dk_acc, dv_acc
):
    core = meta[0]
    size = k.shape[0]
    krow = lax.broadcasted_iota(jnp.int32, (QB, QB), 0)
    qcol = lax.broadcasted_iota(jnp.int32, (QB, QB), 1)
    kt[...] = k[...].astype(F32).T.astype(BF)
    for h in (0, 1):
        mine, marks = head_masks(h)
        ones = (marks[0] + marks[1] + marks[2]).astype(BF)
        k_aug[h] = k[...] * mine.astype(BF) + ones
        v_aug[h] = v[...] * mine.astype(BF) + ones
    dk_acc[...] = jnp.zeros_like(dk_acc)
    dv_acc[...] = jnp.zeros_like(dv_acc)

    def one_block(i, count):
        at = pl.ds(pl.multiple_of(i * QB, QB), QB)
        per = QB // (2 * tokens)
        pieces = []
        for c in range(per):
            spot = pl.ds(pl.multiple_of((i * per + c) * tokens, tokens), tokens)
            a, b = do_own[spot, :].astype(F32), do_oth[spot, :].astype(F32)
            flag = jnp.full(a.shape, core, jnp.int32)
            pieces += [jnp.where(flag == 0, a, b), jnp.where(flag == 0, b, a)]
        do = jnp.concatenate(pieces, 0)
        prod = do * o_nat[at, :].astype(F32)
        turned = []
        for h in (0, 1):
            mine, marks = head_masks(h)
            delta = jnp.sum(prod * mine, axis=1, keepdims=True)
            doa = add_marks(mine, marks, do, -delta)
            qa = q_aug[h, at, :]

            def one(j, dqt, diagonal):
                kat = pl.ds(pl.multiple_of(j * QB, QB), QB)
                s = nt(k_aug[h, kat, :], qa)
                if diagonal:
                    s = jnp.where(qcol >= krow, s, NEGATIVE)
                p = jnp.exp(s)
                ds = (p * nt(v_aug[h, kat, :], doa)).astype(BF)
                dv_acc[h, kat, :] += dot(p.astype(BF), doa)
                dk_acc[h, kat, :] += dot(ds, qa)
                return dqt + dot(kt[64 * h : 64 * h + 64, kat], ds)

            dqt = jnp.zeros((64, QB), F32)
            if count is not None:
                for j in range(count - 1):
                    dqt = one(j, dqt, False)
            else:
                dqt = lax.fori_loop(0, i, lambda j, c: one(j, c, False), dqt)
            turned.append(one(i, dqt, True))
        dq[at, :] = (jnp.concatenate(turned, 0).T * 0.125).astype(BF)

    if size <= 1024:
        for i in range(size // QB):
            one_block(i, i + 1)
    else:
        lax.fori_loop(0, size // QB, lambda i, c: (one_block(i, None), c)[1], 0)
    m0, m1 = head_masks(0)[0], head_masks(1)[0]
    dk[...] = (dk_acc[0] * m0 + dk_acc[1] * m1).astype(BF)
    dv[...] = (dv_acc[0] * m0 + dv_acc[1] * m1).astype(BF)


def cross_pair(ref, p):
    lane = lanes(128)
    piece = ref[:, 128 * p : 128 * p + 128]
    low = (lane < 64).astype(BF)
    high = (lane >= 64).astype(BF)
    return jnp.concatenate([piece * low, piece * high], 0)


def cross_kernel(
    meta, x, o_own, o_oth, info, w_out, g_cross, c_query, mk, mv, c_out, g_ffn,
    o1, y1, a2, cq, p2, o2, y2, a3,
):
    core = meta[0]
    half = o_own.shape[1]
    mine = pl.ds(pl.multiple_of(core * half, 128), half)
    other = pl.ds(pl.multiple_of((1 - core) * half, 128), half)
    o1[:, mine] = o_own[...]
    o1[:, other] = o_oth[...]
    first = x[...].astype(F32) + dot(o1[...], w_out[...])
    y1[...] = first
    n2 = (first * inv_rms(first) * g_cross[...]).astype(BF)
    a2[...] = n2
    query = dot(n2, c_query[...]).astype(BF)
    cq[...] = query
    patches = mk.shape[0]
    lane = lanes(2 * patches)
    low = lane < patches
    sent = info[0:1, 0:1].astype(F32) * 16.0 + info[0:1, 128:129].astype(F32)
    known = jnp.full((1, 1), meta[2], jnp.int32).astype(F32)
    same = jnp.full((1, 1), meta[0] - meta[4], jnp.int32) == 0
    count = jnp.where(same, known, sent)
    valid = jnp.where(low, lane, lane - patches).astype(F32) < count
    for p in range(H // 2):
        keys = cross_pair(mk, p)
        values = cross_pair(mv, p)
        s = nt(query[:, 128 * p : 128 * p + 128], keys) * 0.125
        s = jnp.where(valid, s, NEGATIVE)
        m0 = jnp.max(jnp.where(low, s, NEGATIVE), axis=1, keepdims=True)
        m1 = jnp.max(jnp.where(low, NEGATIVE, s), axis=1, keepdims=True)
        e = jnp.exp(s - jnp.where(low, m0, m1))
        l0 = jnp.sum(jnp.where(low, e, 0.0), axis=1, keepdims=True)
        l1 = jnp.sum(jnp.where(low, 0.0, e), axis=1, keepdims=True)
        w = e / jnp.where(low, l0, l1)
        p2[p] = w
        o2[:, 128 * p : 128 * p + 128] = dot(w.astype(BF), values).astype(BF)
    second = first + dot(o2[...], c_out[...])
    y2[...] = second
    a3[...] = (second * inv_rms(second) * g_ffn[...]).astype(BF)


def ffn_kernel(
    row_blocks, meta, a3, cot, y2, g_ffn, wg, wu, wd,
    out, dy2, dy2b, gain, send, keep, acc, err, a3t, cott, dw, gu_buf, wd_buf, sems,
):
    core = meta[0]
    i, r = pl.program_id(0), pl.program_id(1)
    rows = pl.ds(pl.multiple_of(r * ROWS, ROWS), ROWS)
    first, last = i == 0, i == pl.num_programs(0) - 1

    @pl.when(first)
    def _():
        a3t[:, rows] = a3[...].astype(F32).T.astype(BF)
        cott[:, rows] = cot[...].astype(F32).T.astype(BF)
        acc[rows, :] = y2[...]
        err[rows, :] = jnp.zeros((ROWS, err.shape[1]), F32)

    gate = dot(a3[...], wg[...])
    up = dot(a3[...], wu[...])
    square = gate * gate
    th = jnp.tanh(0.7978845608028654 * gate * (1.0 + 0.044715 * square))
    more = 0.5 * (1.0 + th)
    act = gate * more
    slope = more + 0.5 * gate * (1.0 - th * th) * (
        0.7978845608028654 * (1.0 + 3 * 0.044715 * square)
    )
    hidden = (act * up).astype(BF)
    dh = nt(cot[...], wd[...])
    d_gate = (dh * up * slope).astype(BF)
    d_up = (dh * act).astype(BF)
    acc[rows, :] += dot(hidden, wd[...])
    err[rows, :] += nt(d_gate, wg[...]) + nt(d_up, wu[...])
    terms = (dot(a3t[:, rows], d_gate), dot(a3t[:, rows], d_up), dot(cott[:, rows], hidden))
    if row_blocks > 1:
        for n, term in enumerate(terms):
            dw[n] = jnp.where(r == 0, 0.0, dw[n]) + term
        terms = (dw[0], dw[1], dw[2])

    slot = lax.rem(i, 2)
    side = i // 2

    def gu_copy(dst):
        return pltpu.make_async_copy(gu_buf.at[slot], dst.at[side, pl.ds(0, 2)], sems.at[0, slot])

    def wd_copy(n, dst):
        return pltpu.make_async_copy(
            wd_buf.at[slot, n], dst.at[:, 2, pl.ds(2 * i, 2)], sems.at[1 + n, slot]
        )

    def drain(at):
        pltpu.make_async_copy(gu_buf.at[at], keep.at[0, pl.ds(0, 2)], sems.at[0, at]).wait()
        for n, dst in enumerate((send, keep)):
            pltpu.make_async_copy(
                wd_buf.at[at, n], dst.at[:, 2, pl.ds(0, 2)], sems.at[1 + n, at]
            ).wait()

    def put():
        pl.when(i >= 2)(lambda: drain(slot))
        width = terms[0].shape[1]
        for n in (0, 1):
            gu_buf[slot, n] = terms[n].astype(BF).reshape(8, terms[n].shape[0] // 8, width)
        down = terms[2].astype(BF)
        per, part, wide = down.shape[0] // 4, down.shape[0] // 8, width // 2
        for b in range(4):
            kept = jnp.where(core == b % 2, 1, 0)
            for y in range(2):
                piece = down[b * per : (b + 1) * per, y * wide : (y + 1) * wide]
                packed = jnp.concatenate([piece[:part], piece[part:]], 1)
                wd_buf[slot, kept, b // 2, y] = packed
        pl.when(slot == core)(lambda: gu_copy(keep).start())
        pl.when(slot != core)(lambda: gu_copy(send).start())
        wd_copy(0, send).start()
        wd_copy(1, keep).start()

        @pl.when(last)
        def _():
            drain(1 - slot)
            drain(slot)

    if row_blocks > 1:
        pl.when(r == row_blocks - 1)(put)
    else:
        put()

    @pl.when(last)
    def _():
        out[...] = acc[rows, :].astype(BF)
        back, gsum = norm_back(err[rows, :], y2[...], g_ffn[...])
        total = cot[...].astype(F32) + back
        dy2[...] = total
        dy2b[...] = total.astype(BF)
        gain[...] = jnp.where(r == 0, 0.0, gain[...]) + gsum


def cross_back_kernel(
    charts, patches_each, meta, dy2, dy2b, c_out, p2, mk, mv, cq, y1, g_cross, c_query, w_out,
    c_key, c_value,
    dcq, dmk, dmv, dy1, dy1b, do_keep, do_send, memg, gain, mk_acc, mv_acc, mem_scr,
):
    core = meta[0]
    r = pl.program_id(0)
    half = do_keep.shape[1]
    patches = mk.shape[0]
    lane = lanes(2 * patches)
    low = lane < patches
    left = (lanes(128) < 64).astype(F32)
    do2 = nt(dy2b[...], c_out[...]).astype(BF)
    fresh = r == 0
    for p in range(H // 2):
        at = slice(128 * p, 128 * p + 128)
        keys = cross_pair(mk, p)
        values = cross_pair(mv, p)
        w = p2[p]
        dp = nt(do2[:, at], values)
        prod = w * dp
        r0 = jnp.sum(jnp.where(low, prod, 0.0), axis=1, keepdims=True)
        r1 = jnp.sum(jnp.where(low, 0.0, prod), axis=1, keepdims=True)
        ds = w * (dp - jnp.where(low, r0, r1))
        dcq[:, at] = (dot(ds.astype(BF), keys) * 0.125).astype(BF)
        gk = dot(ds.T.astype(BF), cq[:, at]) * 0.125
        gv = dot(w.T.astype(BF), do2[:, at])
        gk = gk[:patches] * left + gk[patches:] * (1.0 - left)
        gv = gv[:patches] * left + gv[patches:] * (1.0 - left)
        mk_acc[:, at] = jnp.where(fresh, 0.0, mk_acc[:, at]) + gk
        mv_acc[:, at] = jnp.where(fresh, 0.0, mv_acc[:, at]) + gv
    err = nt(dcq[...], c_query[...])
    back, gsum = norm_back(err, y1[...], g_cross[...])
    total = dy2[...] + back
    dy1[...] = total
    tb = total.astype(BF)
    dy1b[...] = tb
    gain[...] = jnp.where(fresh, 0.0, gain[...]) + gsum
    do_keep[...] = nt(tb, w_out[pl.ds(pl.multiple_of(core * half, half), half), :]).astype(BF)
    rows = tb.shape[0]
    do_send[pl.ds(pl.multiple_of(r * rows, rows), rows), :] = nt(
        tb, w_out[pl.ds(pl.multiple_of((1 - core) * half, half), half), :]
    ).astype(BF)

    @pl.when(r == pl.num_programs(0) - 1)
    def _():
        gk, gv = mk_acc[...].astype(BF), mv_acc[...].astype(BF)
        dmk[...] = gk
        dmv[...] = gv
        mem_scr[...] = nt(gk, c_key[...]) + nt(gv, c_value[...])

        def gather(parity):
            return jnp.concatenate(
                [
                    mem_scr[pl.ds(pl.multiple_of((2 * a + parity) * patches_each, 8), patches_each), :]
                    for a in range(charts)
                ],
                0,
            )

        memg[...] = gather(core)
        away = gather(1 - core).astype(BF)
        extra = away.shape[0]
        base = do_send.shape[0] - 2 * extra
        do_send[base : base + extra, :] = away[:, :half]
        do_send[base + extra :, :] = away[:, half:]


def square_kernel(meta, o2, dy2b, a2, dcq, mem, dmk, dmv, o1, dy1b, send, keep):
    core = meta[0]
    half = keep.shape[2]
    mine = pl.ds(pl.multiple_of(core * half, 128), half)
    other = pl.ds(pl.multiple_of((1 - core) * half, 128), half)
    memt = mem[...].astype(F32).T.astype(BF)
    pairs = ((o2, dy2b), (a2, dcq), (None, dmk), (None, dmv), (o1, dy1b))
    for n, (left, right) in enumerate(pairs):
        turned = memt if left is None else left[...].astype(F32).T.astype(BF)
        send[n] = dot(turned, right[:, other]).astype(BF)
        keep[n] = dot(turned, right[:, mine]).astype(BF)


def leave_kernel(
    split, charts, tokens, meta, a1, dq, dk, dv, wq, wk, wv, column, g_cross, g_ffn, *outs,
):
    half = dq.shape[1]
    size = dq.shape[0]
    width = g_ffn.shape[1]
    core, parity = meta[0], meta[4]
    cols = pl.ds(pl.multiple_of(core * half, 128), half)
    e_keep, e_send = outs[0], outs[1]
    out, scr = (outs[4], outs[5]) if split else (outs[2], outs[3])
    third = width // 3

    def rows_of(n):
        at = pl.ds(pl.multiple_of(n * third, third), third)
        turned = a1[:, at].astype(F32).T.astype(BF)
        gain = jnp.zeros((third, 1), F32)
        for m, (right, weight) in enumerate(((dq, wq), (dk, wk), (dv, wv))):
            block = dot(turned, right[...])
            gain += jnp.sum(block * weight[at, cols].astype(F32), axis=1, keepdims=True)
            out[at, m * half : (m + 1) * half] = block.astype(BF)
        gain = gain / column[at, :]
        stack = jnp.concatenate(
            [g_cross[:, at], g_ffn[:, at], jnp.zeros((126, third), F32)], 0
        ).T
        out[at, 3 * half :] = (jnp.where(lanes(128) == 2, gain, stack)).astype(BF)

    lax.fori_loop(0, 3, lambda n, c: (rows_of(n), c)[1], 0)
    if split:
        send, keep = outs[2], outs[3]
        part = width // 8
        for n in range(4):
            keep[n] = out[pl.ds(pl.multiple_of((2 * n + parity) * part, part), part), :]
            send[n] = out[pl.ds(pl.multiple_of((2 * n + 1 - parity) * part, part), part), :]
    step = scr.shape[0]
    per = step // (2 * tokens)

    def one(first):
        at = pl.ds(pl.multiple_of(first * step, step), step)
        scr[...] = (
            nt(dq[at, :], wq[:, cols]) + nt(dk[at, :], wk[:, cols]) + nt(dv[at, :], wv[:, cols])
        )
        for c in range(per):
            spot = pl.ds(pl.multiple_of((first * per + c) * tokens, tokens), tokens)
            e_keep[spot, :] = scr[pl.ds(pl.multiple_of((2 * c + core) * tokens, tokens), tokens), :]
            e_send[spot, :] = scr[
                pl.ds(pl.multiple_of((2 * c + 1 - core) * tokens, tokens), tokens), :
            ].astype(BF)

    lax.fori_loop(0, size // step, lambda g, c: (one(g), c)[1], 0)


def mix_kernel(meta, keep, recv, send1, kept1, send2, kept2):
    side, parity = meta[3], meta[4]
    rows = keep.shape[3]
    low = rows // 2

    def gu(x, w, s):
        return (keep[x, w, s].astype(F32) + recv[x, w, s].astype(F32)).astype(BF)

    def wd(x, s, part):
        return (keep[x, 2, s, part, :].astype(F32) + recv[x, 2, s, part, :].astype(F32)).astype(BF)

    for s in range(8):
        for x, to in ((1 - side, send1), (side, kept1)):
            to[s, :rows, :] = gu(x, 0, s)
            to[s, rows:, :] = wd(x, s, slice(0, low))
    for n in range(4):
        for x in range(2):
            for y, to in ((1 - parity, send2), (parity, kept2)):
                to[x, n, :rows, :] = gu(x, 1, 2 * n + y)
                to[x, n, rows:, :] = wd(x, 2 * n + y, slice(low, rows))


def input_grad_kernel(e_keep, e_recv, x, gain, dy1, out):
    err = e_keep[...] + e_recv[...].astype(F32)
    back, _ = norm_back(err, x[...].astype(F32), gain[...])
    out[...] = (dy1[...] + back).astype(BF)


def total(parts):
    result = parts[0].astype(F32)
    for part in parts[1:]:
        result = result + part.reshape(result.shape).astype(F32)
    return result


def tie(value, *deps):
    return lax.optimization_barrier((value, deps))[0]


def turn_in_kernel(meta, base, recv, send, keep):
    v, z = meta[5], meta[6]
    send[z] = base[z, 1 - v]
    send[1 - z] = recv[1 - v]
    keep[z] = base[z, v]
    keep[1 - z] = recv[v]


def gather_kernel(meta, keep, recv, out):
    v = meta[5]
    for n in range(2):
        out[n, v] = keep[n]
        out[n, 1 - v] = recv[n]


def finish_kernel(tokens, got, first, few):
    for n in range(got.shape[0]):
        first[n] = got[n, :tokens, :].astype(F32)
        few[n] = got[n, tokens:, :].astype(F32)


def place_kernel(charts, meta, *refs):
    place = meta[1]
    out = refs[-1]
    for d in range(charts):
        out[lax.rem(place - d + charts, charts)] = refs[d][...].astype(out.dtype)


def local(
    nseq, inputs, memory, patch_count, cotangent, norm_self, w_query, w_key, w_value, w_out,
    norm_cross, c_query, c_key, c_value, c_out, norm_ffn, w_gate, w_up, w_down,
):
    charts, tokens, width = inputs.shape
    patches_each = memory.shape[1]
    size = charts * 2 * tokens
    own = charts * tokens
    patches = patches_each * nseq
    half = width // 2
    small = size <= 1024
    hidden = w_gate.shape[1]
    blocks = own // ROWS
    dp = lax.axis_index("dp")
    seq = lax.axis_index("seq")
    side, core = dp // 2, lax.rem(dp, 2)
    place, parity = seq // 2, lax.rem(seq, 2)

    def shift(d):
        return [
            ((2 * x + k) * nseq + 2 * a + b, (2 * x + b) * nseq + 2 * ((a + d) % charts) + k)
            for x in range(2)
            for k in range(2)
            for a in range(charts)
            for b in range(2)
        ]

    def dp_perm(rule):
        return [(2 * x + k, 2 * rule(x, k)[0] + rule(x, k)[1]) for x in range(2) for k in range(2)]

    swap_core = dp_perm(lambda x, k: (x, 1 - k))
    swap_side = dp_perm(lambda x, k: (1 - x, k))

    def across(value):
        return lax.ppermute(value, "dp", swap_core)

    def travel(value, d):
        return lax.ppermute(value, ("dp", "seq"), shift(d))

    def pick(value, d):
        return lax.dynamic_index_in_dim(value, lax.rem(place + d, charts), 0, keepdims=False)

    gain_self, gain_cross, gain_ffn = (g.reshape(1, width) for g in (norm_self, norm_cross, norm_ffn))
    count = lax.dynamic_index_in_dim(patch_count, place, 0, keepdims=False)
    meta = jnp.stack(
        [core, place, count, side, parity, lax.rem(place, 2), place // 2]
    ).astype(jnp.int32)

    trade = [
        ((2 * x + k) * nseq + 2 * a + b, (2 * x + b) * nseq + 2 * a + k)
        for x in range(2)
        for k in range(2)
        for a in range(charts)
        for b in range(2)
    ]
    flips = {
        name: [(s, s ^ (1 << bit)) for s in range(nseq)] for bit, name in enumerate("yvz")
    }
    low_bit, high_bit = lax.rem(place, 2), place // 2

    mine = jnp.stack(
        [
            travel(jnp.concatenate([pick(inputs, d), pick(memory, d)], 0), d)
            for d in range(charts)
        ]
    )
    theirs = across(mine)
    if small:
        cot_base = lax.ppermute(cotangent, ("dp", "seq"), trade)
        cot_base = cot_base.reshape(2, 2, tokens, width)
        cot_away = lax.dynamic_index_in_dim(cot_base, 1 - high_bit, 0, keepdims=False)
        cot_got = lax.ppermute(cot_away, "seq", flips["z"])
        theirs = tie(theirs, cot_away)
    else:
        cot_parts = [travel(pick(cotangent, d), d) for d in range(charts)]
    pairs = half // 128
    pair_spec = pl.BlockSpec((size, 128), lambda p, m: (0, p))
    own_spec = pl.BlockSpec((own, 128), lambda p, m: (0, p))
    aug_spec = pl.BlockSpec((2, size, 128), lambda p, m: (p, 0, 0))
    x_own, a1, k, v, mem, mk, mv, o_keep, o_send, o_nat, q_aug = pl.pallas_call(
        functools.partial(enter_kernel, charts, tokens, patches_each),
        compiler_params=room(small, 20),
        out_shape=(
            sds((own, width), BF), sds((size, width), BF), sds((size, half), BF),
            sds((size, half), BF), sds((patches, width), BF), sds((patches, width), BF),
            sds((patches, width), BF), sds((own, half), BF), sds((own + 16, half), BF),
            sds((size, half), BF), sds((2 * pairs, size, 128), BF),
        ),
        in_specs=[SM] + [VM] * 3 + [pl.BlockSpec(memory_space=pltpu.HBM)] * 5,
        out_specs=[VM] * 11,
        scratch_shapes=[
            pltpu.VMEM((patches, width), F32), pltpu.VMEM((size, half), BF),
            pltpu.VMEM((width, half), BF), pltpu.VMEM((width, half), BF),
            pltpu.VMEM((width, half), BF), pltpu.VMEM((width, width), BF),
            pltpu.VMEM((width, width), BF), pltpu.SemaphoreType.DMA((5,)),
        ],
        cost_estimate=cost(2 * size * width * 3 * half, mine, theirs, w_query, w_key, w_value),
    )(meta, mine, theirs, gain_self, w_query, w_key, w_value, c_key, c_value)
    if small:
        part = sds((2, tokens, width), BF)
        cot_send, cot_keep = pl.pallas_call(
            turn_in_kernel,
            compiler_params=room(small, 6),
            out_shape=(part, part),
            in_specs=[SM, VM, VM],
            out_specs=[VM] * 2,
        )(meta, cot_base, cot_got)
        cot_got = lax.ppermute(cot_send, "seq", flips["v"])
        o_recv = tie(across(o_send), cot_send)
    else:
        o_recv = across(o_send)

    row_spec = pl.BlockSpec((ROWS, width), lambda r: (r, 0))
    half_spec = pl.BlockSpec((ROWS, half), lambda r: (r, 0))
    p2_spec = pl.BlockSpec((H // 2, ROWS, 2 * patches), lambda r: (0, r, 0))

    def fixed(shape, spaces=1):
        if spaces == 1:
            return pl.BlockSpec(shape, lambda r: (0,) * len(shape))
        return pl.BlockSpec(shape, lambda i, r: (0,) * len(shape))

    square = fixed((width, width))
    one_row = fixed((1, width))
    patch_spec = fixed((patches, width))
    rows_f = sds((own, width), F32)
    rows_b = sds((own, width), BF)
    o1, y1, a2, cq, p2, o2, y2, a3 = pl.pallas_call(
        cross_kernel,
        compiler_params=room(small, 16),
        out_shape=(
            rows_b, rows_f, rows_b, rows_b, sds((H // 2, own, 2 * patches), F32), rows_b, rows_f,
            rows_b,
        ),
        grid=(blocks,),
        in_specs=[
            SM, row_spec, half_spec, half_spec, pl.BlockSpec((16, half), lambda r: (own // 16, 0)),
            square, one_row, square, patch_spec, patch_spec, square, one_row,
        ],
        out_specs=[row_spec] * 4 + [p2_spec] + [row_spec] * 3,
        cost_estimate=cost(6 * own * width * width, w_out, c_query, c_out, rows_f, rows_f),
    )(meta, x_own, o_keep, o_recv, o_recv, w_out, gain_cross, c_query, mk, mv, c_out, gain_ffn)

    def placed(parts, dtype):
        return pl.pallas_call(
            functools.partial(place_kernel, charts),
            compiler_params=room(small, 6),
            out_shape=sds((charts,) + parts[0].shape, dtype),
            in_specs=[SM] + [VM] * charts,
            out_specs=VM,
        )(meta, *parts)

    if small:
        cot = pl.pallas_call(
            gather_kernel,
            compiler_params=room(small, 6),
            out_shape=sds((2, 2, tokens, width), BF),
            in_specs=[SM, VM, VM],
            out_specs=VM,
        )(meta, cot_keep, tie(cot_got, y2)).reshape(own, width)
    else:
        cot = placed(cot_parts, BF).reshape(own, width)
    wide = hidden // 4
    last = 3
    f_pack = sds((2, 3, 8, width // 8, wide), BF)
    anywhere = pl.BlockSpec(memory_space=pl.ANY)
    frow = pl.BlockSpec((ROWS, width), lambda i, r: (r, 0))
    lrow = pl.BlockSpec((ROWS, width), lambda i, r: (r * (i // last), 0))
    out_b, dy2, dy2b, ffn_gain, f_send, f_keep = pl.pallas_call(
        functools.partial(ffn_kernel, blocks),
        compiler_params=room(small, 30),
        out_shape=(rows_b, rows_f, rows_b, sds((1, width), F32), f_pack, f_pack),
        grid=(4, blocks),
        in_specs=[
            SM, frow, frow, frow, fixed((1, width), 2),
            pl.BlockSpec((width, wide), lambda i, r: (0, i)),
            pl.BlockSpec((width, wide), lambda i, r: (0, i)),
            pl.BlockSpec((wide, width), lambda i, r: (i, 0)),
        ],
        out_specs=[lrow, lrow, lrow, fixed((1, width), 2), anywhere, anywhere],
        scratch_shapes=[
            pltpu.VMEM((own, width), F32), pltpu.VMEM((own, width), F32),
            pltpu.VMEM((width, own), BF), pltpu.VMEM((width, own), BF),
            pltpu.VMEM((3, width, wide) if blocks > 1 else (3, 8, 128), F32),
            pltpu.VMEM((2, 2, 8, width // 8, wide), BF),
            pltpu.VMEM((2, 2, 2, 2, width // 8, wide), BF), pltpu.SemaphoreType.DMA((3, 2)),
        ],
        cost_estimate=cost(18 * own * width * hidden, w_gate, w_up, w_down, rows_f, rows_f),
    )(meta, a3, cot, y2, gain_ffn, w_gate, w_up, w_down)
    f_recv = across(f_send)

    def back_first(rows):
        return lax.ppermute(rows, ("dp", "seq"), trade)

    def back_second(rows):
        base = rows.reshape((2, 2) + rows.shape[1:])
        away = lax.dynamic_index_in_dim(base, 1 - high_bit, 0, keepdims=False)
        return base, lax.ppermute(away, "seq", flips["z"])

    def back_turn(base, got):
        return pl.pallas_call(
            turn_in_kernel,
            compiler_params=room(small, 6),
            out_shape=(sds(got.shape, BF), sds(got.shape, BF)),
            in_specs=[SM, VM, VM],
            out_specs=[VM] * 2,
        )(meta, base, got)

    def gathered(keep, got):
        return pl.pallas_call(
            gather_kernel,
            compiler_params=room(small, 6),
            out_shape=sds((2, 2) + got.shape[1:], BF),
            in_specs=[SM, VM, VM],
            out_specs=VM,
        )(meta, keep, got).reshape((charts,) + got.shape[1:])

    def back_last(got):
        return pl.pallas_call(
            functools.partial(finish_kernel, tokens),
            compiler_params=room(small, 8),
            out_shape=(
                sds((charts, tokens, width), F32), sds((charts, patches_each, width), F32),
            ),
            in_specs=[VM],
            out_specs=[VM] * 2,
        )(got)

    def halve(which, keep, recv, outer):
        parts = (keep if isinstance(keep, list) else [keep]) + [recv]
        size_now, wide_now = parts[0].size, parts[0].shape[-1]
        shape = (outer, 2, size_now // (outer * 2 * wide_now), wide_now)
        parts = [p.reshape(shape) for p in parts]
        i = meta[which]
        sends = [lax.dynamic_index_in_dim(p, 1 - i, 1, keepdims=False) for p in parts]
        kept = [lax.dynamic_index_in_dim(p, i, 1, keepdims=False) for p in parts]
        return total(sends).astype(BF), kept

    def over(name, value):
        if name == "x":
            return lax.ppermute(value, "dp", swap_side)
        return lax.ppermute(value, "seq", flips[name])

    out_rows = out_b.reshape(charts, tokens, width)
    if small:
        out_base, out_got = back_second(out_rows)
    else:
        out_parts = [travel(pick(out_rows, d), d) for d in range(charts)]
    dcq, dmk, dmv, dy1, dy1b, do_keep, do_send, memg, cross_gain = pl.pallas_call(
        functools.partial(cross_back_kernel, charts, patches_each),
        compiler_params=room(small, 16),
        out_shape=(
            rows_b, sds((patches, width), BF), sds((patches, width), BF), rows_f, rows_b,
            sds((own, half), BF), sds((own + patches, half), BF),
            sds((patches // 2, width), F32), sds((1, width), F32),
        ),
        grid=(blocks,),
        in_specs=[
            SM, row_spec, row_spec, square, p2_spec, patch_spec, patch_spec, row_spec, row_spec,
            one_row, square, square, square, square,
        ],
        out_specs=[
            row_spec, patch_spec, patch_spec, row_spec, row_spec, half_spec,
            fixed((own + patches, half)), fixed((patches // 2, width)), one_row,
        ],
        scratch_shapes=[pltpu.VMEM((patches, width), F32)] * 3,
        cost_estimate=cost(6 * own * width * width, w_out, c_query, c_out, rows_f, rows_f),
    )(meta, dy2, dy2b, c_out, p2, mk, mv, cq, y1, gain_cross, c_query, w_out, c_key, c_value)
    do_recv = across(do_send)

    if small:
        f1 = sds((8, 3 * width // 16, wide), BF)
        f2 = sds((2, 4, 3 * width // 16, wide), BF)
        f1_send, f1_keep, f2_send, f2_keep = pl.pallas_call(
            mix_kernel,
            compiler_params=room(small, 16),
            out_shape=(f1, f1, f2, f2),
            in_specs=[SM] + [VM] * 2,
            out_specs=[VM] * 4,
        )(meta, f_keep, f_recv)
        f1_recv, f2_recv = over("x", f1_send), over("y", f2_send)
        dcq = tie(dcq, f1_send)
    s_send, s_keep = pl.pallas_call(
        square_kernel,
        compiler_params=room(small, 16),
        out_shape=(sds((5, width, half), BF), sds((5, width, half), BF)),
        in_specs=[SM] + [VM] * 9,
        out_specs=[VM] * 2,
        cost_estimate=cost(6 * own * width * width, o1, o2, a2, dcq, dy2b, dy1b),
    )(meta, o2, dy2b, a2, dcq, mem, dmk, dmv, o1, dy1b)
    s_recv = across(s_send)

    few = patches // 2
    memg_recv = jnp.concatenate([do_recv[own : own + few], do_recv[own + few :]], 1)
    memg_own = (memg + memg_recv.astype(F32)).astype(BF).reshape(charts, patches_each, width)
    if small:
        s_send, s_keep = halve(5, s_keep, s_recv, 10)
        s_recv = over("v", s_send)
        do_recv = tie(do_recv, s_send)

    dq, dk, dv = pl.pallas_call(
        functools.partial(attend_back_kernel, tokens),
        compiler_params=room(small, 14),
        out_shape=(sds((size, half), BF),) * 3,
        grid_spec=pltpu.PrefetchScalarGridSpec(
            num_scalar_prefetch=1,
            grid=(pairs,),
            in_specs=[aug_spec, pair_spec, pair_spec, pair_spec, own_spec, own_spec],
            out_specs=[pair_spec] * 3,
            scratch_shapes=[
                pltpu.VMEM((2, size, 128), BF), pltpu.VMEM((2, size, 128), BF),
                pltpu.VMEM((128, size), BF),
                pltpu.VMEM((2, size, 128), F32), pltpu.VMEM((2, size, 128), F32),
            ],
        ),
        cost_estimate=cost(10 * size * size * half, k, v, q_aug),
    )(meta, q_aug, k, v, o_nat, do_keep, do_recv)

    if small:
        dq = tie(dq, f1_recv, f2_recv, out_got)
    t_whole = sds((width, 3 * half + 128), BF)
    t_piece = sds((4, width // 8, 3 * half + 128), BF)
    gone = pl.pallas_call(
        functools.partial(leave_kernel, small, charts, tokens),
        compiler_params=room(small, 14),
        out_shape=(rows_f, rows_b) + ((t_piece, t_piece) if small else (t_whole,)),
        in_specs=[SM] + [VM] * 10,
        out_specs=[VM] * (4 if small else 3),
        scratch_shapes=([pltpu.VMEM((width, 3 * half + 128), BF)] if small else [])
        + [pltpu.VMEM((256, width), F32)],
    )(
        meta, a1, dq, dk, dv, w_query, w_key, w_value, norm_self.reshape(width, 1), cross_gain,
        ffn_gain,
    )
    e_keep, e_send = gone[:2]
    e_recv = across(e_send)
    if small:
        t_send, t_keep = gone[2:]
        t_recv = over("y", t_send)
        e_recv = tie(e_recv, t_send)
    else:
        t_out = gone[2]

    in_grad = pl.pallas_call(
        input_grad_kernel,
        compiler_params=room(small, 8),
        out_shape=rows_b,
        in_specs=[VM] * 5,
        out_specs=VM,
        cost_estimate=cost(20 * own * width, e_keep, e_send, x_own, dy1),
    )(e_keep, e_recv, x_own, gain_self, dy1)
    in_rows = jnp.concatenate([in_grad.reshape(charts, tokens, width), memg_own], 1)
    if small:
        in_base, in_got = back_second(in_rows)
        f2_send, f2_keep = halve(3, f2_keep, tie(f2_recv, in_base), 1)
        f2_recv = over("x", f2_send)
        s_send, s_keep = halve(3, s_keep, tie(s_recv, f2_send), 20)
        s_recv = over("x", s_send)
        out_send, out_keep = back_turn(out_base, tie(out_got, s_send))
        out_got = lax.ppermute(out_send, "seq", flips["v"])
        t_send, t_keep = halve(5, t_keep, tie(t_recv, out_send), 2)
        t_recv = over("v", t_send)
        f2_send, f2_keep = halve(5, f2_keep, tie(f2_recv, t_send), 2)
        f2_recv = over("v", f2_send)
        f1_send, f1_keep = halve(4, f1_keep, tie(f1_recv, f2_send), 4)
        f1_recv = over("y", f1_send)
        in_send, in_keep = back_turn(in_base, tie(in_got, f1_send))
        in_got = lax.ppermute(in_send, "seq", flips["v"])
        s_send, s_keep = halve(4, s_keep, tie(s_recv, in_send), 10)
        s_recv = over("y", s_send)
        t_send, t_keep = halve(6, t_keep, tie(t_recv, s_send), 1)
        t_recv = over("z", t_send)
        f1_send, f1_keep = halve(5, f1_keep, tie(f1_recv, t_send), 2)
        f1_recv = over("v", f1_send)
        out_rows = gathered(out_keep, tie(out_got, f1_send))
        out_mid = out_rows
        out_rows = back_first(out_rows)
        f2_send, f2_keep = halve(6, f2_keep, tie(f2_recv, out_mid, s_recv), 1)
        f2_recv = over("z", f2_send)
        in_rows = gathered(in_keep, tie(in_got, f2_send))
        in_mid = in_rows
        in_rows = back_first(in_rows)
        s_send, s_keep = halve(6, s_keep, tie(s_recv, in_mid, in_rows), 5)
        s_recv = over("z", s_send)
        f1_send, f1_keep = halve(6, f1_keep, tie(f1_recv, s_send), 1)
        f1_recv = over("z", f1_send)
    else:
        in_parts = [travel(pick(in_rows, d), d) for d in range(charts)]

    if small:
        f1_sum = total(f1_keep + [f1_recv]).reshape(3 * width // 16, wide)
        f2_sum = total(f2_keep + [f2_recv]).reshape(3 * width // 16, wide)
        t_sum = total(t_keep + [t_recv]).reshape(width // 8, 3 * half + 128)
        s_part = total(s_keep + [s_recv])
        s_zero = jnp.zeros_like(s_part)
        s_sum = jnp.concatenate(
            [jnp.where(side == 0, s_part, s_zero), jnp.where(side == 0, s_zero, s_part)], 1
        )
        g_gate, g_up = f1_sum[: width // 8], f2_sum[: width // 8]
        g_down = jnp.concatenate([f1_sum[width // 8 :], f2_sum[width // 8 :]], 0)
        g_down = g_down.reshape(width // 8, 2, wide // 2).transpose(2, 1, 0)
        g_down = g_down.reshape(wide // 2, width // 4)
    else:

        def over_seq(value, axis):
            return lax.psum_scatter(
                value.astype(BF), "seq", scatter_dimension=axis, tiled=True
            ).astype(F32)

        def over_side(parts):
            sends = [lax.dynamic_index_in_dim(p, 1 - side, 0, keepdims=False) for p in parts]
            kept = [lax.dynamic_index_in_dim(p, side, 0, keepdims=False) for p in parts]
            return total(kept + [lax.ppermute(total(sends).astype(BF), "dp", swap_side)])

        f_all = over_side([f_keep, f_recv])
        g_two = over_seq(f_all[:2].reshape(2, width, wide), 1)
        g_gate, g_up = g_two[0], g_two[1]
        down = f_all[2].reshape(8, width // 8, 2, wide // 2)
        g_down = over_seq(down.transpose(0, 3, 2, 1).reshape(hidden, width // 4), 0)
        s_sum = over_seq(total([s_keep, s_recv]), 1)
        t_sum = over_seq(t_out, 0)

    rows = t_sum.shape[0]
    quarter = half // 2
    t_sum = t_sum.astype(BF)
    squares = jnp.concatenate(
        [t_sum[:, : 3 * half].reshape(rows, 3, half).transpose(1, 0, 2), s_sum.astype(BF)], 0
    ).reshape(8, rows, 2, quarter)
    gains = t_sum[:, 3 * half :]
    padded = jnp.pad(gains, ((0, 0), (0, quarter - 128)))[None]

    def deliver(block, rule):
        part = lax.dynamic_index_in_dim(squares, block, 2, keepdims=False)
        return lax.ppermute(jnp.concatenate([part, padded], 0), "dp", dp_perm(rule)).astype(F32)

    done = deliver(side, lambda x, k: (k, x)) + deliver(1 - side, lambda x, k: (k, 1 - x))
    rest = lax.ppermute(gains, "dp", dp_perm(lambda x, k: (1 - k, x))).astype(F32) + lax.ppermute(
        gains, "dp", dp_perm(lambda x, k: (1 - k, 1 - x))
    ).astype(F32)
    gain_sum = done[8, :, :128] + rest

    if small:
        in_all, few_all = back_last(in_rows)
        out_all = out_rows.astype(F32)
    else:
        out_all, in_all = placed(out_parts, F32), placed(in_parts, F32)
        in_all, few_all = in_all[:, :tokens], in_all[:, tokens:]
    return (
        out_all,
        in_all,
        few_all,
        gain_sum[:, 2],
        done[0],
        done[1],
        done[2],
        done[7],
        gain_sum[:, 0],
        done[4],
        done[5],
        done[6],
        done[3],
        gain_sum[:, 1],
        g_gate,
        g_up,
        g_down,
    )


def solution(mesh):
    tok = P("dp", "seq", None)
    cut = P("seq", "dp")
    in_specs = (tok, tok, P("dp"), tok) + (P(),) * 14
    out_specs = (tok, tok, tok, P("seq"), cut, cut, cut, cut, P("seq"), cut, cut, cut, cut)
    out_specs += (P("seq"), cut, cut, cut)
    return jax.shard_map(
        functools.partial(local, mesh.shape["seq"]),
        mesh=mesh,
        in_specs=in_specs,
        out_specs=out_specs,
        check_vma=False,
    )
```

```python
import functools

import jax
import jax.numpy as jnp
from jax import lax
from jax.experimental import pallas as pl
from jax.experimental.pallas import tpu as pltpu
from jax.sharding import PartitionSpec as P

H = 12
EPSILON = 1e-06
NEGATIVE = -1e30
F32 = jnp.float32
BF = jnp.bfloat16
VM = pl.BlockSpec(memory_space=pltpu.VMEM)
SM = pl.BlockSpec(memory_space=pltpu.SMEM)
HB = pl.BlockSpec(memory_space=pltpu.HBM)
ROWS = 512
QB = 256


def dot(a, b):
    return lax.dot_general(a, b, (((1,), (0,)), ((), ())), preferred_element_type=F32)


def nt(a, b):
    return lax.dot_general(a, b, (((1,), (1,)), ((), ())), preferred_element_type=F32)


def lanes(width):
    return lax.broadcasted_iota(jnp.int32, (1, width), 1)


def inv_rms(v):
    return lax.rsqrt(jnp.mean(v * v, axis=-1, keepdims=True) + EPSILON)


def norm_back(e, v, gain):
    r = inv_rms(v)
    u = v * r
    eg = e * gain
    grad_v = (eg - u * jnp.mean(eg * u, axis=-1, keepdims=True)) * r
    return grad_v, jnp.sum(e * u, axis=0, keepdims=True)


def cost(flops, *arrays):
    total = sum(a.size * a.dtype.itemsize for a in arrays)
    return pl.CostEstimate(flops=int(flops), bytes_accessed=int(total), transcendentals=0)


def room(small, mib):
    return pltpu.CompilerParams(vmem_limit_bytes=mib << 20) if small else None


def sds(shape, dtype):
    return jax.ShapeDtypeStruct(shape, dtype)


def split3(value):
    hi = value.astype(BF).astype(F32)
    mid = (value - hi).astype(BF).astype(F32)
    lo = (value - hi - mid).astype(BF).astype(F32)
    return hi, mid, lo


def head_masks(h):
    lane = lanes(128)
    mine = ((lane < 64) if h == 0 else (lane >= 64)).astype(F32)
    base = 64 if h == 0 else 0
    marks = [(lane == base + i).astype(F32) for i in range(3)]
    return mine, marks


def add_marks(mine, marks, body, extra):
    hi, mid, lo = split3(extra)
    return (body * mine + hi * marks[0] + mid * marks[1] + lo * marks[2]).astype(BF)


def enter_kernel(
    staged, charts, tokens, patches, meta, own, oth, gain, wq_hbm, wk_hbm, wv_hbm, ck_hbm, cv_hbm,
    x_own, a1_out, k_out, v_out, mem, mk, mv, o_keep, o_send, o_nat, q_aug_out,
    mem_scr, q, wq, wk, wv, ck, cv, sems, *stage,
):
    if staged:
        a1, k, v, q_aug, out_sems, pair_sems = stage
    else:
        a1, k, v, q_aug = a1_out, k_out, v_out, q_aug_out
    core, place = meta[0], meta[1]
    half = q.shape[1]
    width = a1.shape[1]
    size = q.shape[0]
    group = max(1, min(charts, ROWS // tokens))
    cols = pl.ds(pl.multiple_of(core * half, 128), half)
    copies = [
        pltpu.make_async_copy(src.at[:, cols], dst, sems.at[n])
        for n, (src, dst) in enumerate(((wq_hbm, wq), (wk_hbm, wk), (wv_hbm, wv)))
    ] + [
        pltpu.make_async_copy(src, dst, sems.at[3 + n])
        for n, (src, dst) in enumerate(((ck_hbm, ck), (cv_hbm, cv)))
    ]
    for copy in copies:
        copy.start()

    def one(ref, parity, first, fresh):
        x = ref[pl.ds(first, group), :tokens, :].reshape(group * tokens, width)
        xf = x.astype(F32)
        a = (xf * inv_rms(xf) * gain[...]).astype(BF)
        if fresh:
            for copy in copies[:3]:
                copy.wait()
        qq = (dot(a, wq[...]) * 0.125).astype(BF)
        kk = dot(a, wk[...]).astype(BF)
        vv = dot(a, wv[...]).astype(BF)
        for i in range(group):
            chunk = lax.rem(place - (first + i) + charts, charts)
            part = slice(i * tokens, (i + 1) * tokens)
            at = pl.ds(pl.multiple_of((2 * chunk + parity) * tokens, tokens), tokens)
            a1[at, :] = a[part]
            q[at, :] = qq[part]
            k[at, :] = kk[part]
            v[at, :] = vv[part]
            few = ref[first + i, tokens:, :].astype(F32)
            spot = pl.ds(pl.multiple_of((2 * chunk + parity) * patches, patches), patches)
            mem_scr[spot, :] = few
            if ref is own:
                x_own[pl.ds(pl.multiple_of(chunk * tokens, tokens), tokens), :] = x[part]

    for ref, parity in ((own, core), (oth, 1 - core)):
        if charts == group:
            one(ref, parity, 0, ref is own)
        else:
            if ref is own:
                for copy in copies[:3]:
                    copy.wait()
            lax.fori_loop(
                0, charts // group,
                lambda g, c, r=ref, p=parity: (one(r, p, g * group, False), c)[1], 0,
            )
    whole = mem_scr[...].astype(BF)
    mem[...] = whole
    for copy in copies[3:]:
        copy.wait()
    mk[...] = dot(whole, ck[...]).astype(BF)
    mv[...] = dot(whole, cv[...]).astype(BF)
    leaving = [
        pltpu.make_async_copy(src, dst, out_sems.at[n])
        for n, (src, dst) in enumerate(((a1, a1_out), (k, k_out), (v, v_out)))
        if staged
    ]
    for copy in leaving:
        copy.start()
    row = lax.broadcasted_iota(jnp.int32, (QB, QB), 0)
    col = lax.broadcasted_iota(jnp.int32, (QB, QB), 1)

    def pair_copy(n):
        at = pl.ds(2 * n, 2)
        return pltpu.make_async_copy(q_aug.at[at], q_aug_out.at[at], pair_sems.at[n])

    def pair(n):
        wide = pl.ds(pl.multiple_of(n * 128, 128), 128)

        def one_block(i, count):
            at = pl.ds(i * QB, QB) if count is not None else pl.ds(pl.multiple_of(i * QB, QB), QB)
            qp = q[at, wide]
            outs = []
            for h in (0, 1):
                mine, marks = head_masks(h)
                mb = mine.astype(BF)
                rest = (1.0 - mine).astype(BF)
                qh = qp * mb

                def scores(j):
                    return nt(qh, k[pl.ds(pl.multiple_of(j * QB, QB), QB), wide])

                def weigh(e, j):
                    vh = v[pl.ds(pl.multiple_of(j * QB, QB), QB), wide] * mb + rest
                    return dot(e.astype(BF), vh)

                diag = jnp.where(row >= col, scores(i), NEGATIVE)
                if count is not None:
                    parts = [scores(j) for j in range(count - 1)] + [diag]
                    top = parts[0]
                    for s in parts[1:]:
                        top = jnp.maximum(top, s)
                    top = jnp.max(top, axis=1, keepdims=True)
                    acc = weigh(jnp.exp(parts[0] - top), 0)
                    for j, s in enumerate(parts[1:]):
                        acc = acc + weigh(jnp.exp(s - top), j + 1)
                else:
                    top = jnp.max(diag, axis=1, keepdims=True)
                    acc = weigh(jnp.exp(diag - top), i)

                    def step(j, state):
                        top, acc = state
                        s = scores(j)
                        new = jnp.maximum(top, jnp.max(s, axis=1, keepdims=True))
                        return new, acc * jnp.exp(top - new) + weigh(jnp.exp(s - new), j)

                    top, acc = lax.fori_loop(0, i, step, (top, acc))
                total = pltpu.roll(acc, 64, 1)
                outs.append(acc / (total * mine + (1.0 - mine)) * mine)
                lse = top + jnp.log(acc * (1.0 - mine) + mine)
                q_aug[2 * n + h, at, :] = add_marks(mine, marks, qp.astype(F32), -lse)
            o = (outs[0] + outs[1]).astype(BF)
            o_nat[at, wide] = o
            per = QB // (2 * tokens)
            for c in range(per):
                even = o[2 * c * tokens : (2 * c + 1) * tokens]
                odd = o[(2 * c + 1) * tokens : (2 * c + 2) * tokens]
                spot = pl.ds(pl.multiple_of((i * per + c) * tokens, tokens), tokens)
                flag = jnp.full(even.shape, core, jnp.int32).astype(F32)
                ef, of = even.astype(F32), odd.astype(F32)
                o_keep[spot, wide] = jnp.where(flag == 0, ef, of).astype(BF)
                o_send[spot, wide] = jnp.where(flag == 0, of, ef).astype(BF)

        if size <= 1024:
            for i in range(size // QB):
                one_block(i, i + 1)
        else:
            lax.fori_loop(0, size // QB, lambda i, c: (one_block(i, None), c)[1], 0)

    def pair_and_copy(n, carry):
        pair(n)
        if staged:
            pair_copy(n).start()
        return carry

    lax.fori_loop(0, half // 128, pair_and_copy, 0)
    info = jnp.full((16, 128), meta[2], jnp.int32)
    o_send[size // 2 :, :128] = (info // 16).astype(F32).astype(BF)
    o_send[size // 2 :, 128:256] = lax.rem(info, 16).astype(F32).astype(BF)
    o_send[size // 2 :, 256:] = jnp.zeros((16, half - 256), BF)
    for copy in leaving:
        copy.wait()
    for n in range(half // 128 if staged else 0):
        pair_copy(n).wait()


def attend_back_kernel(
    tokens, meta, q_aug, k, v, o_nat, do_own, do_oth, dq, dk, dv, k_aug, v_aug, kt, dk_acc, dv_acc
):
    core = meta[0]
    size = k.shape[0]
    krow = lax.broadcasted_iota(jnp.int32, (QB, QB), 0)
    qcol = lax.broadcasted_iota(jnp.int32, (QB, QB), 1)
    kt[...] = k[...].astype(F32).T.astype(BF)
    for h in (0, 1):
        mine, marks = head_masks(h)
        ones = (marks[0] + marks[1] + marks[2]).astype(BF)
        k_aug[h] = k[...] * mine.astype(BF) + ones
        v_aug[h] = v[...] * mine.astype(BF) + ones
    dk_acc[...] = jnp.zeros_like(dk_acc)
    dv_acc[...] = jnp.zeros_like(dv_acc)

    def one_block(i, count):
        at = pl.ds(pl.multiple_of(i * QB, QB), QB)
        per = QB // (2 * tokens)
        pieces = []
        for c in range(per):
            spot = pl.ds(pl.multiple_of((i * per + c) * tokens, tokens), tokens)
            a, b = do_own[spot, :].astype(F32), do_oth[spot, :].astype(F32)
            flag = jnp.full(a.shape, core, jnp.int32)
            pieces += [jnp.where(flag == 0, a, b), jnp.where(flag == 0, b, a)]
        do = jnp.concatenate(pieces, 0)
        prod = do * o_nat[at, :].astype(F32)
        turned = []
        for h in (0, 1):
            mine, marks = head_masks(h)
            delta = jnp.sum(prod * mine, axis=1, keepdims=True)
            doa = add_marks(mine, marks, do, -delta)
            qa = q_aug[h, at, :]

            def one(j, dqt, diagonal):
                kat = pl.ds(pl.multiple_of(j * QB, QB), QB)
                s = nt(k_aug[h, kat, :], qa)
                if diagonal:
                    s = jnp.where(qcol >= krow, s, NEGATIVE)
                p = jnp.exp(s)
                ds = (p * nt(v_aug[h, kat, :], doa)).astype(BF)
                dv_acc[h, kat, :] += dot(p.astype(BF), doa)
                dk_acc[h, kat, :] += dot(ds, qa)
                return dqt + dot(kt[64 * h : 64 * h + 64, kat], ds)

            dqt = jnp.zeros((64, QB), F32)
            if count is not None:
                for j in range(count - 1):
                    dqt = one(j, dqt, False)
            else:
                dqt = lax.fori_loop(0, i, lambda j, c: one(j, c, False), dqt)
            turned.append(one(i, dqt, True))
        dq[at, :] = (jnp.concatenate(turned, 0).T * 0.125).astype(BF)

    if size <= 1024:
        for i in range(size // QB):
            one_block(i, i + 1)
    else:
        lax.fori_loop(0, size // QB, lambda i, c: (one_block(i, None), c)[1], 0)
    m0, m1 = head_masks(0)[0], head_masks(1)[0]
    dk[...] = (dk_acc[0] * m0 + dk_acc[1] * m1).astype(BF)
    dv[...] = (dv_acc[0] * m0 + dv_acc[1] * m1).astype(BF)


def cross_pair(ref, p):
    lane = lanes(128)
    piece = ref[:, 128 * p : 128 * p + 128]
    low = (lane < 64).astype(BF)
    high = (lane >= 64).astype(BF)
    return jnp.concatenate([piece * low, piece * high], 0)


def cross_kernel(
    meta, x, o_own, o_oth, info, w_out, g_cross, c_query, mk, mv, c_out, g_ffn,
    o1, y1, a2, cq, p2, o2, y2, a3,
):
    core = meta[0]
    half = o_own.shape[1]
    mine = pl.ds(pl.multiple_of(core * half, 128), half)
    other = pl.ds(pl.multiple_of((1 - core) * half, 128), half)
    o1[:, mine] = o_own[...]
    o1[:, other] = o_oth[...]
    first = x[...].astype(F32) + dot(o1[...], w_out[...])
    y1[...] = first
    n2 = (first * inv_rms(first) * g_cross[...]).astype(BF)
    a2[...] = n2
    query = dot(n2, c_query[...]).astype(BF)
    cq[...] = query
    patches = mk.shape[0]
    lane = lanes(2 * patches)
    low = lane < patches
    sent = info[0:1, 0:1].astype(F32) * 16.0 + info[0:1, 128:129].astype(F32)
    known = jnp.full((1, 1), meta[2], jnp.int32).astype(F32)
    same = jnp.full((1, 1), meta[0] - meta[4], jnp.int32) == 0
    count = jnp.where(same, known, sent)
    valid = jnp.where(low, lane, lane - patches).astype(F32) < count
    for p in range(H // 2):
        keys = cross_pair(mk, p)
        values = cross_pair(mv, p)
        s = nt(query[:, 128 * p : 128 * p + 128], keys) * 0.125
        s = jnp.where(valid, s, NEGATIVE)
        m0 = jnp.max(jnp.where(low, s, NEGATIVE), axis=1, keepdims=True)
        m1 = jnp.max(jnp.where(low, NEGATIVE, s), axis=1, keepdims=True)
        e = jnp.exp(s - jnp.where(low, m0, m1))
        l0 = jnp.sum(jnp.where(low, e, 0.0), axis=1, keepdims=True)
        l1 = jnp.sum(jnp.where(low, 0.0, e), axis=1, keepdims=True)
        w = e / jnp.where(low, l0, l1)
        p2[p] = w
        o2[:, 128 * p : 128 * p + 128] = dot(w.astype(BF), values).astype(BF)
    second = first + dot(o2[...], c_out[...])
    y2[...] = second
    a3[...] = (second * inv_rms(second) * g_ffn[...]).astype(BF)


def ffn_kernel(
    row_blocks, meta, a3, cot, y2, g_ffn, wg, wu, wd,
    out, dy2, dy2b, gain, send, keep, acc, err, a3t, cott, dw, gu_buf, wd_buf, sems,
):
    core = meta[0]
    i, r = pl.program_id(0), pl.program_id(1)
    rows = pl.ds(pl.multiple_of(r * ROWS, ROWS), ROWS)
    first, last = i == 0, i == pl.num_programs(0) - 1

    @pl.when(first)
    def _():
        a3t[:, rows] = a3[...].astype(F32).T.astype(BF)
        cott[:, rows] = cot[...].astype(F32).T.astype(BF)
        acc[rows, :] = y2[...]
        err[rows, :] = jnp.zeros((ROWS, err.shape[1]), F32)

    gate = dot(a3[...], wg[...])
    up = dot(a3[...], wu[...])
    square = gate * gate
    th = jnp.tanh(0.7978845608028654 * gate * (1.0 + 0.044715 * square))
    more = 0.5 * (1.0 + th)
    act = gate * more
    slope = more + 0.5 * gate * (1.0 - th * th) * (
        0.7978845608028654 * (1.0 + 3 * 0.044715 * square)
    )
    hidden = (act * up).astype(BF)
    dh = nt(cot[...], wd[...])
    d_gate = (dh * up * slope).astype(BF)
    d_up = (dh * act).astype(BF)
    acc[rows, :] += dot(hidden, wd[...])
    err[rows, :] += nt(d_gate, wg[...]) + nt(d_up, wu[...])
    terms = (dot(a3t[:, rows], d_gate), dot(a3t[:, rows], d_up), dot(cott[:, rows], hidden))
    if row_blocks > 1:
        for n, term in enumerate(terms):
            dw[n] = jnp.where(r == 0, 0.0, dw[n]) + term
        terms = (dw[0], dw[1], dw[2])

    slot = lax.rem(i, 2)
    side = i // 2

    def gu_copy(dst):
        return pltpu.make_async_copy(gu_buf.at[slot], dst.at[side, pl.ds(0, 2)], sems.at[0, slot])

    def wd_copy(n, dst):
        return pltpu.make_async_copy(
            wd_buf.at[slot, n], dst.at[:, 2, pl.ds(2 * i, 2)], sems.at[1 + n, slot]
        )

    def drain(at):
        pltpu.make_async_copy(gu_buf.at[at], keep.at[0, pl.ds(0, 2)], sems.at[0, at]).wait()
        for n, dst in enumerate((send, keep)):
            pltpu.make_async_copy(
                wd_buf.at[at, n], dst.at[:, 2, pl.ds(0, 2)], sems.at[1 + n, at]
            ).wait()

    def put():
        pl.when(i >= 2)(lambda: drain(slot))
        width = terms[0].shape[1]
        for n in (0, 1):
            gu_buf[slot, n] = terms[n].astype(BF).reshape(8, terms[n].shape[0] // 8, width)
        down = terms[2].astype(BF)
        per, part, wide = down.shape[0] // 4, down.shape[0] // 8, width // 2
        for b in range(4):
            kept = jnp.where(core == b % 2, 1, 0)
            for y in range(2):
                piece = down[b * per : (b + 1) * per, y * wide : (y + 1) * wide]
                packed = jnp.concatenate([piece[:part], piece[part:]], 1)
                wd_buf[slot, kept, b // 2, y] = packed
        pl.when(slot == core)(lambda: gu_copy(keep).start())
        pl.when(slot != core)(lambda: gu_copy(send).start())
        wd_copy(0, send).start()
        wd_copy(1, keep).start()

        @pl.when(last)
        def _():
            drain(1 - slot)
            drain(slot)

    if row_blocks > 1:
        pl.when(r == row_blocks - 1)(put)
    else:
        put()

    @pl.when(last)
    def _():
        out[...] = acc[rows, :].astype(BF)
        back, gsum = norm_back(err[rows, :], y2[...], g_ffn[...])
        total = cot[...].astype(F32) + back
        dy2[...] = total
        dy2b[...] = total.astype(BF)
        gain[...] = jnp.where(r == 0, 0.0, gain[...]) + gsum


def cross_back_kernel(
    charts, patches_each, meta, dy2, dy2b, c_out, p2, mk, mv, cq, y1, g_cross, c_query, w_out,
    c_key_hbm, c_value_hbm,
    dcq, dmk, dmv, dy1, dy1b, do_keep, do_send, memg, gain, mk_acc, mv_acc, mem_scr, c_key, c_value, sems,
):
    core = meta[0]
    r = pl.program_id(0)
    half = do_keep.shape[1]
    patches = mk.shape[0]
    lane = lanes(2 * patches)
    low = lane < patches
    left = (lanes(128) < 64).astype(F32)
    do2 = nt(dy2b[...], c_out[...]).astype(BF)
    fresh = r == 0
    copies = [
        pltpu.make_async_copy(c_key_hbm, c_key, sems.at[0]),
        pltpu.make_async_copy(c_value_hbm, c_value, sems.at[1]),
    ]

    @pl.when(fresh)
    def _():
        for copy in copies:
            copy.start()

    for p in range(H // 2):
        at = slice(128 * p, 128 * p + 128)
        keys = cross_pair(mk, p)
        values = cross_pair(mv, p)
        w = p2[p]
        dp = nt(do2[:, at], values)
        prod = w * dp
        r0 = jnp.sum(jnp.where(low, prod, 0.0), axis=1, keepdims=True)
        r1 = jnp.sum(jnp.where(low, 0.0, prod), axis=1, keepdims=True)
        ds = w * (dp - jnp.where(low, r0, r1))
        dcq[:, at] = (dot(ds.astype(BF), keys) * 0.125).astype(BF)
        gk = dot(ds.T.astype(BF), cq[:, at]) * 0.125
        gv = dot(w.T.astype(BF), do2[:, at])
        gk = gk[:patches] * left + gk[patches:] * (1.0 - left)
        gv = gv[:patches] * left + gv[patches:] * (1.0 - left)
        mk_acc[:, at] = jnp.where(fresh, 0.0, mk_acc[:, at]) + gk
        mv_acc[:, at] = jnp.where(fresh, 0.0, mv_acc[:, at]) + gv
    err = nt(dcq[...], c_query[...])
    back, gsum = norm_back(err, y1[...], g_cross[...])
    total = dy2[...] + back
    dy1[...] = total
    tb = total.astype(BF)
    dy1b[...] = tb
    gain[...] = jnp.where(fresh, 0.0, gain[...]) + gsum
    do_keep[...] = nt(tb, w_out[pl.ds(pl.multiple_of(core * half, half), half), :]).astype(BF)
    rows = tb.shape[0]
    do_send[pl.ds(pl.multiple_of(r * rows, rows), rows), :] = nt(
        tb, w_out[pl.ds(pl.multiple_of((1 - core) * half, half), half), :]
    ).astype(BF)

    @pl.when(r == pl.num_programs(0) - 1)
    def _():
        gk, gv = mk_acc[...].astype(BF), mv_acc[...].astype(BF)
        for copy in copies:
            copy.wait()
        dmk[...] = gk
        dmv[...] = gv
        mem_scr[...] = nt(gk, c_key[...]) + nt(gv, c_value[...])

        def gather(parity):
            return jnp.concatenate(
                [
                    mem_scr[pl.ds(pl.multiple_of((2 * a + parity) * patches_each, 8), patches_each), :]
                    for a in range(charts)
                ],
                0,
            )

        memg[...] = gather(core)
        away = gather(1 - core).astype(BF)
        extra = away.shape[0]
        base = do_send.shape[0] - 2 * extra
        do_send[base : base + extra, :] = away[:, :half]
        do_send[base + extra :, :] = away[:, half:]


def square_kernel(meta, o2, dy2b, a2, dcq, mem, dmk, dmv, o1, dy1b, send, keep):
    core = meta[0]
    half = keep.shape[2]
    mine = pl.ds(pl.multiple_of(core * half, 128), half)
    other = pl.ds(pl.multiple_of((1 - core) * half, 128), half)
    memt = mem[...].astype(F32).T.astype(BF)
    pairs = ((o2, dy2b), (a2, dcq), (None, dmk), (None, dmv), (o1, dy1b))
    for n, (left, right) in enumerate(pairs):
        turned = memt if left is None else left[...].astype(F32).T.astype(BF)
        send[n] = dot(turned, right[:, other]).astype(BF)
        keep[n] = dot(turned, right[:, mine]).astype(BF)


def leave_kernel(
    split, charts, tokens, meta, a1, dq, dk, dv, wq, wk, wv, column, g_cross, g_ffn, *outs,
):
    half = dq.shape[1]
    size = dq.shape[0]
    width = g_ffn.shape[1]
    core, parity = meta[0], meta[4]
    cols = pl.ds(pl.multiple_of(core * half, 128), half)
    e_keep, e_send = outs[0], outs[1]
    out, scr = (outs[4], outs[5]) if split else (outs[2], outs[3])
    third = width // 3

    def rows_of(n):
        at = pl.ds(pl.multiple_of(n * third, third), third)
        turned = a1[:, at].astype(F32).T.astype(BF)
        gain = jnp.zeros((third, 1), F32)
        for m, (right, weight) in enumerate(((dq, wq), (dk, wk), (dv, wv))):
            block = dot(turned, right[...])
            gain += jnp.sum(block * weight[at, cols].astype(F32), axis=1, keepdims=True)
            out[at, m * half : (m + 1) * half] = block.astype(BF)
        gain = gain / column[at, :]
        stack = jnp.concatenate(
            [g_cross[:, at], g_ffn[:, at], jnp.zeros((126, third), F32)], 0
        ).T
        out[at, 3 * half :] = (jnp.where(lanes(128) == 2, gain, stack)).astype(BF)

    lax.fori_loop(0, 3, lambda n, c: (rows_of(n), c)[1], 0)
    if split:
        send, keep = outs[2], outs[3]
        part = width // 8
        for n in range(4):
            keep[n] = out[pl.ds(pl.multiple_of((2 * n + parity) * part, part), part), :]
            send[n] = out[pl.ds(pl.multiple_of((2 * n + 1 - parity) * part, part), part), :]
    step = scr.shape[0]
    per = step // (2 * tokens)

    def one(first):
        at = pl.ds(pl.multiple_of(first * step, step), step)
        scr[...] = (
            nt(dq[at, :], wq[:, cols]) + nt(dk[at, :], wk[:, cols]) + nt(dv[at, :], wv[:, cols])
        )
        for c in range(per):
            spot = pl.ds(pl.multiple_of((first * per + c) * tokens, tokens), tokens)
            e_keep[spot, :] = scr[pl.ds(pl.multiple_of((2 * c + core) * tokens, tokens), tokens), :]
            e_send[spot, :] = scr[
                pl.ds(pl.multiple_of((2 * c + 1 - core) * tokens, tokens), tokens), :
            ].astype(BF)

    lax.fori_loop(0, size // step, lambda g, c: (one(g), c)[1], 0)


def mix_kernel(meta, keep, recv, send1, kept1, send2, kept2):
    side, parity = meta[3], meta[4]
    rows = keep.shape[3]
    low = rows // 2

    def gu(x, w, s):
        return (keep[x, w, s].astype(F32) + recv[x, w, s].astype(F32)).astype(BF)

    def wd(x, s, part):
        return (keep[x, 2, s, part, :].astype(F32) + recv[x, 2, s, part, :].astype(F32)).astype(BF)

    for s in range(8):
        for x, to in ((1 - side, send1), (side, kept1)):
            to[s, :rows, :] = gu(x, 0, s)
            to[s, rows:, :] = wd(x, s, slice(0, low))
    for n in range(4):
        for x in range(2):
            for y, to in ((1 - parity, send2), (parity, kept2)):
                to[x, n, :rows, :] = gu(x, 1, 2 * n + y)
                to[x, n, rows:, :] = wd(x, 2 * n + y, slice(low, rows))


def input_grad_kernel(e_keep, e_recv, x, gain, dy1, out):
    err = e_keep[...] + e_recv[...].astype(F32)
    back, _ = norm_back(err, x[...].astype(F32), gain[...])
    out[...] = (dy1[...] + back).astype(BF)


def total(parts):
    result = parts[0].astype(F32)
    for part in parts[1:]:
        result = result + part.reshape(result.shape).astype(F32)
    return result


def tie(value, *deps):
    return lax.optimization_barrier((value, deps))[0]


def turn_in_kernel(meta, base, recv, send, keep):
    v, z = meta[5], meta[6]
    send[z] = base[z, 1 - v]
    send[1 - z] = recv[1 - v]
    keep[z] = base[z, v]
    keep[1 - z] = recv[v]


def gather_kernel(meta, keep, recv, out):
    v = meta[5]
    for n in range(2):
        out[n, v] = keep[n]
        out[n, 1 - v] = recv[n]


def finish_kernel(tokens, got, first, few):
    for n in range(got.shape[0]):
        first[n] = got[n, :tokens, :].astype(F32)
        few[n] = got[n, tokens:, :].astype(F32)


def place_kernel(charts, meta, *refs):
    place = meta[1]
    out = refs[-1]
    for d in range(charts):
        out[lax.rem(place - d + charts, charts)] = refs[d][...].astype(out.dtype)


def local(
    nseq, inputs, memory, patch_count, cotangent, norm_self, w_query, w_key, w_value, w_out,
    norm_cross, c_query, c_key, c_value, c_out, norm_ffn, w_gate, w_up, w_down,
):
    charts, tokens, width = inputs.shape
    patches_each = memory.shape[1]
    size = charts * 2 * tokens
    own = charts * tokens
    patches = patches_each * nseq
    half = width // 2
    small = size <= 1024
    hidden = w_gate.shape[1]
    blocks = own // ROWS
    dp = lax.axis_index("dp")
    seq = lax.axis_index("seq")
    side, core = dp // 2, lax.rem(dp, 2)
    place, parity = seq // 2, lax.rem(seq, 2)

    def shift(d):
        return [
            ((2 * x + k) * nseq + 2 * a + b, (2 * x + b) * nseq + 2 * ((a + d) % charts) + k)
            for x in range(2)
            for k in range(2)
            for a in range(charts)
            for b in range(2)
        ]

    def dp_perm(rule):
        return [(2 * x + k, 2 * rule(x, k)[0] + rule(x, k)[1]) for x in range(2) for k in range(2)]

    swap_core = dp_perm(lambda x, k: (x, 1 - k))
    swap_side = dp_perm(lambda x, k: (1 - x, k))

    def across(value):
        return lax.ppermute(value, "dp", swap_core)

    def travel(value, d):
        return lax.ppermute(value, ("dp", "seq"), shift(d))

    def pick(value, d):
        return lax.dynamic_index_in_dim(value, lax.rem(place + d, charts), 0, keepdims=False)

    gain_self, gain_cross, gain_ffn = (g.reshape(1, width) for g in (norm_self, norm_cross, norm_ffn))
    count = lax.dynamic_index_in_dim(patch_count, place, 0, keepdims=False)
    meta = jnp.stack(
        [core, place, count, side, parity, lax.rem(place, 2), place // 2]
    ).astype(jnp.int32)

    trade = [
        ((2 * x + k) * nseq + 2 * a + b, (2 * x + b) * nseq + 2 * a + k)
        for x in range(2)
        for k in range(2)
        for a in range(charts)
        for b in range(2)
    ]
    flips = {
        name: [(s, s ^ (1 << bit)) for s in range(nseq)] for bit, name in enumerate("yvz")
    }
    low_bit, high_bit = lax.rem(place, 2), place // 2

    mine = jnp.stack(
        [
            travel(jnp.concatenate([pick(inputs, d), pick(memory, d)], 0), d)
            for d in range(charts)
        ]
    )
    theirs = across(mine)
    if small:
        cot_base = lax.ppermute(cotangent, ("dp", "seq"), trade)
        cot_base = cot_base.reshape(2, 2, tokens, width)
        cot_away = lax.dynamic_index_in_dim(cot_base, 1 - high_bit, 0, keepdims=False)
        cot_got = lax.ppermute(cot_away, "seq", flips["z"])
        theirs = tie(theirs, cot_away)
    else:
        cot_parts = [travel(pick(cotangent, d), d) for d in range(charts)]
    pairs = half // 128
    pair_spec = pl.BlockSpec((size, 128), lambda p, m: (0, p))
    own_spec = pl.BlockSpec((own, 128), lambda p, m: (0, p))
    aug_spec = pl.BlockSpec((2, size, 128), lambda p, m: (p, 0, 0))
    far = pltpu.HBM if small else sds
    x_own, a1, k, v, mem, mk, mv, o_keep, o_send, o_nat, q_aug = pl.pallas_call(
        functools.partial(enter_kernel, small, charts, tokens, patches_each),
        compiler_params=room(small, 24),
        out_shape=(
            sds((own, width), BF), far((size, width), BF), far((size, half), BF),
            far((size, half), BF), sds((patches, width), BF), sds((patches, width), BF),
            sds((patches, width), BF), sds((own, half), BF), sds((own + 16, half), BF),
            far((size, half), BF), far((2 * pairs, size, 128), BF),
        ),
        in_specs=[SM] + [VM] * 3 + [pl.BlockSpec(memory_space=pltpu.HBM)] * 5,
        out_specs=([VM] + [HB] * 3 + [VM] * 6 + [HB]) if small else [VM] * 11,
        scratch_shapes=[
            pltpu.VMEM((patches, width), F32), pltpu.VMEM((size, half), BF),
            pltpu.VMEM((width, half), BF), pltpu.VMEM((width, half), BF),
            pltpu.VMEM((width, half), BF), pltpu.VMEM((width, width), BF),
            pltpu.VMEM((width, width), BF), pltpu.SemaphoreType.DMA((5,)),
        ]
        + (
            [
                pltpu.VMEM((size, width), BF), pltpu.VMEM((size, half), BF),
                pltpu.VMEM((size, half), BF), pltpu.VMEM((2 * pairs, size, 128), BF),
                pltpu.SemaphoreType.DMA((3,)), pltpu.SemaphoreType.DMA((pairs,)),
            ]
            if small
            else []
        ),
        cost_estimate=cost(2 * size * width * 3 * half, mine, theirs, w_query, w_key, w_value),
    )(
        meta, mine, theirs, gain_self,
        *(
            pltpu.with_memory_space_constraint(w, pltpu.HBM)
            for w in (w_query, w_key, w_value, c_key, c_value)
        ),
    )
    if small:
        part = sds((2, tokens, width), BF)
        cot_send, cot_keep = pl.pallas_call(
            turn_in_kernel,
            compiler_params=room(small, 6),
            out_shape=(part, part),
            in_specs=[SM, VM, VM],
            out_specs=[VM] * 2,
        )(meta, cot_base, cot_got)
        cot_got = lax.ppermute(cot_send, "seq", flips["v"])
        o_recv = tie(across(o_send), cot_send)
    else:
        o_recv = across(o_send)

    each = ROWS if small else QB
    row_spec = pl.BlockSpec((each, width), lambda r: (r, 0))
    half_spec = pl.BlockSpec((each, half), lambda r: (r, 0))
    p2_spec = pl.BlockSpec((H // 2, each, 2 * patches), lambda r: (0, r, 0))

    def fixed(shape, spaces=1):
        if spaces == 1:
            return pl.BlockSpec(shape, lambda r: (0,) * len(shape))
        return pl.BlockSpec(shape, lambda i, r: (0,) * len(shape))

    square = fixed((width, width))
    one_row = fixed((1, width))
    patch_spec = fixed((patches, width))
    rows_f = sds((own, width), F32)
    rows_b = sds((own, width), BF)
    o1, y1, a2, cq, p2, o2, y2, a3 = pl.pallas_call(
        cross_kernel,
        compiler_params=room(small, 16),
        out_shape=(
            rows_b, rows_f, rows_b, rows_b, sds((H // 2, own, 2 * patches), F32), rows_b, rows_f,
            rows_b,
        ),
        grid=(own // each,),
        in_specs=[
            SM, row_spec, half_spec, half_spec, pl.BlockSpec((16, half), lambda r: (own // 16, 0)),
            square, one_row, square, patch_spec, patch_spec, square, one_row,
        ],
        out_specs=[row_spec] * 4 + [p2_spec] + [row_spec] * 3,
        cost_estimate=cost(6 * own * width * width, w_out, c_query, c_out, rows_f, rows_f),
    )(meta, x_own, o_keep, o_recv, o_recv, w_out, gain_cross, c_query, mk, mv, c_out, gain_ffn)

    def placed(parts, dtype):
        return pl.pallas_call(
            functools.partial(place_kernel, charts),
            compiler_params=room(small, 6),
            out_shape=sds((charts,) + parts[0].shape, dtype),
            in_specs=[SM] + [VM] * charts,
            out_specs=VM,
        )(meta, *parts)

    if small:
        cot = pl.pallas_call(
            gather_kernel,
            compiler_params=room(small, 6),
            out_shape=sds((2, 2, tokens, width), BF),
            in_specs=[SM, VM, VM],
            out_specs=VM,
        )(meta, cot_keep, tie(cot_got, y2)).reshape(own, width)
    else:
        cot = placed(cot_parts, BF).reshape(own, width)
    wide = hidden // 4
    last = 3
    f_pack = sds((2, 3, 8, width // 8, wide), BF)
    anywhere = pl.BlockSpec(memory_space=pl.ANY)
    frow = pl.BlockSpec((ROWS, width), lambda i, r: (r, 0))
    lrow = pl.BlockSpec((ROWS, width), lambda i, r: (r * (i // last), 0))
    out_b, dy2, dy2b, ffn_gain, f_send, f_keep = pl.pallas_call(
        functools.partial(ffn_kernel, blocks),
        compiler_params=room(small, 30),
        out_shape=(rows_b, rows_f, rows_b, sds((1, width), F32), f_pack, f_pack),
        grid=(4, blocks),
        in_specs=[
            SM, frow, frow, frow, fixed((1, width), 2),
            pl.BlockSpec((width, wide), lambda i, r: (0, i)),
            pl.BlockSpec((width, wide), lambda i, r: (0, i)),
            pl.BlockSpec((wide, width), lambda i, r: (i, 0)),
        ],
        out_specs=[lrow, lrow, lrow, fixed((1, width), 2), anywhere, anywhere],
        scratch_shapes=[
            pltpu.VMEM((own, width), F32), pltpu.VMEM((own, width), F32),
            pltpu.VMEM((width, own), BF), pltpu.VMEM((width, own), BF),
            pltpu.VMEM((3, width, wide) if blocks > 1 else (3, 8, 128), F32),
            pltpu.VMEM((2, 2, 8, width // 8, wide), BF),
            pltpu.VMEM((2, 2, 2, 2, width // 8, wide), BF), pltpu.SemaphoreType.DMA((3, 2)),
        ],
        cost_estimate=cost(18 * own * width * hidden, w_gate, w_up, w_down, rows_f, rows_f),
    )(meta, a3, cot, y2, gain_ffn, w_gate, w_up, w_down)
    f_recv = across(f_send)

    def back_first(rows):
        return lax.ppermute(rows, ("dp", "seq"), trade)

    def back_second(rows):
        base = rows.reshape((2, 2) + rows.shape[1:])
        away = lax.dynamic_index_in_dim(base, 1 - high_bit, 0, keepdims=False)
        return base, lax.ppermute(away, "seq", flips["z"])

    def back_turn(base, got):
        return pl.pallas_call(
            turn_in_kernel,
            compiler_params=room(small, 6),
            out_shape=(sds(got.shape, BF), sds(got.shape, BF)),
            in_specs=[SM, VM, VM],
            out_specs=[VM] * 2,
        )(meta, base, got)

    def gathered(keep, got):
        return pl.pallas_call(
            gather_kernel,
            compiler_params=room(small, 6),
            out_shape=sds((2, 2) + got.shape[1:], BF),
            in_specs=[SM, VM, VM],
            out_specs=VM,
        )(meta, keep, got).reshape((charts,) + got.shape[1:])

    def back_last(got):
        return pl.pallas_call(
            functools.partial(finish_kernel, tokens),
            compiler_params=room(small, 8),
            out_shape=(
                sds((charts, tokens, width), F32), sds((charts, patches_each, width), F32),
            ),
            in_specs=[VM],
            out_specs=[VM] * 2,
        )(got)

    def halve(which, keep, recv, outer):
        parts = (keep if isinstance(keep, list) else [keep]) + [recv]
        size_now, wide_now = parts[0].size, parts[0].shape[-1]
        shape = (outer, 2, size_now // (outer * 2 * wide_now), wide_now)
        parts = [p.reshape(shape) for p in parts]
        i = meta[which]
        sends = [lax.dynamic_index_in_dim(p, 1 - i, 1, keepdims=False) for p in parts]
        kept = [lax.dynamic_index_in_dim(p, i, 1, keepdims=False) for p in parts]
        return total(sends).astype(BF), kept

    def over(name, value):
        if name == "x":
            return lax.ppermute(value, "dp", swap_side)
        return lax.ppermute(value, "seq", flips[name])

    out_rows = out_b.reshape(charts, tokens, width)
    if small:
        out_base, out_got = back_second(out_rows)
    else:
        out_parts = [travel(pick(out_rows, d), d) for d in range(charts)]
    dcq, dmk, dmv, dy1, dy1b, do_keep, do_send, memg, cross_gain = pl.pallas_call(
        functools.partial(cross_back_kernel, charts, patches_each),
        compiler_params=room(small, 18),
        out_shape=(
            rows_b, sds((patches, width), BF), sds((patches, width), BF), rows_f, rows_b,
            sds((own, half), BF), sds((own + patches, half), BF),
            sds((patches // 2, width), F32), sds((1, width), F32),
        ),
        grid=(own // each,),
        in_specs=[
            SM, row_spec, row_spec, square, p2_spec, patch_spec, patch_spec, row_spec, row_spec,
            one_row, square, square, HB, HB,
        ],
        out_specs=[
            row_spec, patch_spec, patch_spec, row_spec, row_spec, half_spec,
            fixed((own + patches, half)), fixed((patches // 2, width)), one_row,
        ],
        scratch_shapes=[pltpu.VMEM((patches, width), F32)] * 3
        + [pltpu.VMEM((width, width), BF)] * 2
        + [pltpu.SemaphoreType.DMA((2,))],
        cost_estimate=cost(6 * own * width * width, w_out, c_query, c_out, rows_f, rows_f),
    )(meta, dy2, dy2b, c_out, p2, mk, mv, cq, y1, gain_cross, c_query, w_out, c_key, c_value)
    do_recv = across(do_send)

    if small:
        f1 = sds((8, 3 * width // 16, wide), BF)
        f2 = sds((2, 4, 3 * width // 16, wide), BF)
        f1_send, f1_keep, f2_send, f2_keep = pl.pallas_call(
            mix_kernel,
            compiler_params=room(small, 16),
            out_shape=(f1, f1, f2, f2),
            in_specs=[SM] + [VM] * 2,
            out_specs=[VM] * 4,
        )(meta, f_keep, f_recv)
        f1_recv, f2_recv = over("x", f1_send), over("y", f2_send)
        dcq = tie(dcq, f1_send)
    s_send, s_keep = pl.pallas_call(
        square_kernel,
        compiler_params=room(small, 16),
        out_shape=(sds((5, width, half), BF), sds((5, width, half), BF)),
        in_specs=[SM] + [VM] * 9,
        out_specs=[VM] * 2,
        cost_estimate=cost(6 * own * width * width, o1, o2, a2, dcq, dy2b, dy1b),
    )(meta, o2, dy2b, a2, dcq, mem, dmk, dmv, o1, dy1b)
    s_recv = across(s_send)

    few = patches // 2
    memg_recv = jnp.concatenate([do_recv[own : own + few], do_recv[own + few :]], 1)
    memg_own = (memg + memg_recv.astype(F32)).astype(BF).reshape(charts, patches_each, width)
    if small:
        s_send, s_keep = halve(5, s_keep, s_recv, 10)
        s_recv = over("v", s_send)
        do_recv = tie(do_recv, s_send)

    dq, dk, dv = pl.pallas_call(
        functools.partial(attend_back_kernel, tokens),
        compiler_params=room(small, 14),
        out_shape=(sds((size, half), BF),) * 3,
        grid_spec=pltpu.PrefetchScalarGridSpec(
            num_scalar_prefetch=1,
            grid=(pairs,),
            in_specs=[aug_spec, pair_spec, pair_spec, pair_spec, own_spec, own_spec],
            out_specs=[pair_spec] * 3,
            scratch_shapes=[
                pltpu.VMEM((2, size, 128), BF), pltpu.VMEM((2, size, 128), BF),
                pltpu.VMEM((128, size), BF),
                pltpu.VMEM((2, size, 128), F32), pltpu.VMEM((2, size, 128), F32),
            ],
        ),
        cost_estimate=cost(10 * size * size * half, k, v, q_aug),
    )(meta, q_aug, k, v, o_nat, do_keep, do_recv)

    if small:
        dq = tie(dq, f1_recv, f2_recv, out_got)
    t_whole = sds((width, 3 * half + 128), BF)
    t_piece = sds((4, width // 8, 3 * half + 128), BF)
    gone = pl.pallas_call(
        functools.partial(leave_kernel, small, charts, tokens),
        compiler_params=room(small, 14),
        out_shape=(rows_f, rows_b) + ((t_piece, t_piece) if small else (t_whole,)),
        in_specs=[SM] + [VM] * 10,
        out_specs=[VM] * (4 if small else 3),
        scratch_shapes=([pltpu.VMEM((width, 3 * half + 128), BF)] if small else [])
        + [pltpu.VMEM((256, width), F32)],
    )(
        meta, a1, dq, dk, dv, w_query, w_key, w_value, norm_self.reshape(width, 1), cross_gain,
        ffn_gain,
    )
    e_keep, e_send = gone[:2]
    e_recv = across(e_send)
    if small:
        t_send, t_keep = gone[2:]
        t_recv = over("y", t_send)
        e_recv = tie(e_recv, t_send)
    else:
        t_out = gone[2]

    in_grad = pl.pallas_call(
        input_grad_kernel,
        compiler_params=room(small, 8),
        out_shape=rows_b,
        in_specs=[VM] * 5,
        out_specs=VM,
        cost_estimate=cost(20 * own * width, e_keep, e_send, x_own, dy1),
    )(e_keep, e_recv, x_own, gain_self, dy1)
    in_rows = jnp.concatenate([in_grad.reshape(charts, tokens, width), memg_own], 1)
    if small:
        in_base, in_got = back_second(in_rows)
        f2_send, f2_keep = halve(3, f2_keep, tie(f2_recv, in_base), 1)
        f2_recv = over("x", f2_send)
        s_send, s_keep = halve(3, s_keep, tie(s_recv, f2_send), 20)
        s_recv = over("x", s_send)
        out_send, out_keep = back_turn(out_base, tie(out_got, s_send))
        out_got = lax.ppermute(out_send, "seq", flips["v"])
        t_send, t_keep = halve(5, t_keep, tie(t_recv, out_send), 2)
        t_recv = over("v", t_send)
        f2_send, f2_keep = halve(5, f2_keep, tie(f2_recv, t_send), 2)
        f2_recv = over("v", f2_send)
        f1_send, f1_keep = halve(4, f1_keep, tie(f1_recv, f2_send), 4)
        f1_recv = over("y", f1_send)
        out_rows = gathered(out_keep, tie(out_got, f1_send))
        out_mid = out_rows
        out_rows = back_first(out_rows)
        in_send, in_keep = back_turn(in_base, tie(in_got, out_mid))
        in_got = lax.ppermute(in_send, "seq", flips["v"])
        s_send, s_keep = halve(4, s_keep, tie(s_recv, in_send), 10)
        s_recv = over("y", s_send)
        t_send, t_keep = halve(6, t_keep, tie(t_recv, s_send, f2_recv, s_recv), 1)
        t_recv = over("z", t_send)
        f1_send, f1_keep = halve(5, f1_keep, tie(f1_recv, t_send), 2)
        f1_recv = over("v", f1_send)
        s_send, s_keep = halve(6, s_keep, tie(s_recv, f1_send), 5)
        s_recv = over("z", s_send)
        in_rows = gathered(in_keep, tie(in_got, s_send, s_recv))
        in_mid = in_rows
        in_rows = back_first(in_rows)
        f2_send, f2_keep = halve(6, f2_keep, tie(f2_recv, in_mid), 1)
        f2_recv = over("z", f2_send)
        f1_send, f1_keep = halve(6, f1_keep, tie(f1_recv, f2_send), 1)
        f1_recv = over("z", f1_send)
    else:
        in_parts = [travel(pick(in_rows, d), d) for d in range(charts)]

    if small:
        f1_sum = total(f1_keep + [f1_recv]).reshape(3 * width // 16, wide)
        f2_sum = total(f2_keep + [f2_recv]).reshape(3 * width // 16, wide)
        t_sum = total(t_keep + [t_recv]).reshape(width // 8, 3 * half + 128)
        s_part = total(s_keep + [s_recv])
        s_zero = jnp.zeros_like(s_part)
        s_sum = jnp.concatenate(
            [jnp.where(side == 0, s_part, s_zero), jnp.where(side == 0, s_zero, s_part)], 1
        )
        g_gate, g_up = f1_sum[: width // 8], f2_sum[: width // 8]
        g_down = jnp.concatenate([f1_sum[width // 8 :], f2_sum[width // 8 :]], 0)
        g_down = g_down.reshape(width // 8, 2, wide // 2).transpose(2, 1, 0)
        g_down = g_down.reshape(wide // 2, width // 4)
    else:

        def over_seq(value, axis):
            return lax.psum_scatter(
                value.astype(BF), "seq", scatter_dimension=axis, tiled=True
            ).astype(F32)

        def over_side(parts):
            sends = [lax.dynamic_index_in_dim(p, 1 - side, 0, keepdims=False) for p in parts]
            kept = [lax.dynamic_index_in_dim(p, side, 0, keepdims=False) for p in parts]
            return total(kept + [lax.ppermute(total(sends).astype(BF), "dp", swap_side)])

        f_all = over_side([f_keep, f_recv])
        g_two = over_seq(f_all[:2].reshape(2, width, wide), 1)
        g_gate, g_up = g_two[0], g_two[1]
        down = f_all[2].reshape(8, width // 8, 2, wide // 2)
        g_down = over_seq(down.transpose(0, 3, 2, 1).reshape(hidden, width // 4), 0)
        s_sum = over_seq(total([s_keep, s_recv]), 1)
        t_sum = over_seq(t_out, 0)

    rows = t_sum.shape[0]
    quarter = half // 2
    t_sum = t_sum.astype(BF)
    squares = jnp.concatenate(
        [t_sum[:, : 3 * half].reshape(rows, 3, half).transpose(1, 0, 2), s_sum.astype(BF)], 0
    ).reshape(8, rows, 2, quarter)
    gains = t_sum[:, 3 * half :]
    padded = jnp.pad(gains, ((0, 0), (0, quarter - 128)))[None]

    def deliver(block, rule):
        part = lax.dynamic_index_in_dim(squares, block, 2, keepdims=False)
        return lax.ppermute(jnp.concatenate([part, padded], 0), "dp", dp_perm(rule)).astype(F32)

    done = deliver(side, lambda x, k: (k, x)) + deliver(1 - side, lambda x, k: (k, 1 - x))
    rest = lax.ppermute(gains, "dp", dp_perm(lambda x, k: (1 - k, x))).astype(F32) + lax.ppermute(
        gains, "dp", dp_perm(lambda x, k: (1 - k, 1 - x))
    ).astype(F32)
    gain_sum = done[8, :, :128] + rest

    if small:
        in_all, few_all = back_last(in_rows)
        out_all = out_rows.astype(F32)
    else:
        out_all, in_all = placed(out_parts, F32), placed(in_parts, F32)
        in_all, few_all = in_all[:, :tokens], in_all[:, tokens:]
    return (
        out_all,
        in_all,
        few_all,
        gain_sum[:, 2],
        done[0],
        done[1],
        done[2],
        done[7],
        gain_sum[:, 0],
        done[4],
        done[5],
        done[6],
        done[3],
        gain_sum[:, 1],
        g_gate,
        g_up,
        g_down,
    )


def solution(mesh):
    tok = P("dp", "seq", None)
    cut = P("seq", "dp")
    in_specs = (tok, tok, P("dp"), tok) + (P(),) * 14
    out_specs = (tok, tok, tok, P("seq"), cut, cut, cut, cut, P("seq"), cut, cut, cut, cut)
    out_specs += (P("seq"), cut, cut, cut)
    return jax.shard_map(
        functools.partial(local, mesh.shape["seq"]),
        mesh=mesh,
        in_specs=in_specs,
        out_specs=out_specs,
        check_vma=False,
    )
```

```python
import functools

import jax
import jax.numpy as jnp
from jax import lax
from jax.experimental import pallas as pl
from jax.experimental.pallas import tpu as pltpu
from jax.sharding import PartitionSpec as P

H = 12
EPSILON = 1e-06
NEGATIVE = -1e30
F32 = jnp.float32
BF = jnp.bfloat16
VM = pl.BlockSpec(memory_space=pltpu.VMEM)
SM = pl.BlockSpec(memory_space=pltpu.SMEM)
HB = pl.BlockSpec(memory_space=pltpu.HBM)
ROWS = 512
QB = 256


def dot(a, b):
    return lax.dot_general(a, b, (((1,), (0,)), ((), ())), preferred_element_type=F32)


def nt(a, b):
    return lax.dot_general(a, b, (((1,), (1,)), ((), ())), preferred_element_type=F32)


def lanes(width):
    return lax.broadcasted_iota(jnp.int32, (1, width), 1)


def inv_rms(v):
    return lax.rsqrt(jnp.mean(v * v, axis=-1, keepdims=True) + EPSILON)


def norm_back(e, v, gain):
    r = inv_rms(v)
    u = v * r
    eg = e * gain
    grad_v = (eg - u * jnp.mean(eg * u, axis=-1, keepdims=True)) * r
    return grad_v, jnp.sum(e * u, axis=0, keepdims=True)


def cost(flops, *arrays):
    total = sum(a.size * a.dtype.itemsize for a in arrays)
    return pl.CostEstimate(flops=int(flops), bytes_accessed=int(total), transcendentals=0)


def room(small, mib):
    return pltpu.CompilerParams(vmem_limit_bytes=mib << 20) if small else None


def sds(shape, dtype):
    return jax.ShapeDtypeStruct(shape, dtype)


def split3(value):
    hi = value.astype(BF).astype(F32)
    mid = (value - hi).astype(BF).astype(F32)
    lo = (value - hi - mid).astype(BF).astype(F32)
    return hi, mid, lo


def head_masks(h):
    lane = lanes(128)
    mine = ((lane < 64) if h == 0 else (lane >= 64)).astype(F32)
    base = 64 if h == 0 else 0
    marks = [(lane == base + i).astype(F32) for i in range(3)]
    return mine, marks


def add_marks(mine, marks, body, extra):
    hi, mid, lo = split3(extra)
    return (body * mine + hi * marks[0] + mid * marks[1] + lo * marks[2]).astype(BF)


def enter_kernel(
    staged, charts, tokens, patches, meta, own, oth, gain, wq_hbm, wk_hbm, wv_hbm, ck_hbm, cv_hbm,
    x_own, a1_out, k_out, v_out, mem, mk, mv, o_keep, o_send, o_nat, q_aug_out,
    mem_scr, q, wq, wk, wv, ck, cv, sems, *stage,
):
    if staged:
        a1, k, v, q_aug, out_sems, pair_sems = stage
    else:
        a1, k, v, q_aug = a1_out, k_out, v_out, q_aug_out
    core, place = meta[0], meta[1]
    half = q.shape[1]
    width = a1.shape[1]
    size = q.shape[0]
    group = max(1, min(charts, ROWS // tokens))
    cols = pl.ds(pl.multiple_of(core * half, 128), half)
    copies = [
        pltpu.make_async_copy(src.at[:, cols], dst, sems.at[n])
        for n, (src, dst) in enumerate(((wq_hbm, wq), (wk_hbm, wk), (wv_hbm, wv)))
    ] + [
        pltpu.make_async_copy(src, dst, sems.at[3 + n])
        for n, (src, dst) in enumerate(((ck_hbm, ck), (cv_hbm, cv)))
    ]
    for copy in copies:
        copy.start()

    def one(ref, parity, first, fresh):
        x = ref[pl.ds(first, group), :tokens, :].reshape(group * tokens, width)
        xf = x.astype(F32)
        a = (xf * inv_rms(xf) * gain[...]).astype(BF)
        if fresh:
            for copy in copies[:3]:
                copy.wait()
        qq = (dot(a, wq[...]) * 0.125).astype(BF)
        kk = dot(a, wk[...]).astype(BF)
        vv = dot(a, wv[...]).astype(BF)
        for i in range(group):
            chunk = lax.rem(place - (first + i) + charts, charts)
            part = slice(i * tokens, (i + 1) * tokens)
            at = pl.ds(pl.multiple_of((2 * chunk + parity) * tokens, tokens), tokens)
            a1[at, :] = a[part]
            q[at, :] = qq[part]
            k[at, :] = kk[part]
            v[at, :] = vv[part]
            few = ref[first + i, tokens:, :].astype(F32)
            spot = pl.ds(pl.multiple_of((2 * chunk + parity) * patches, patches), patches)
            mem_scr[spot, :] = few
            if ref is own:
                x_own[pl.ds(pl.multiple_of(chunk * tokens, tokens), tokens), :] = x[part]

    for ref, parity in ((own, core), (oth, 1 - core)):
        if charts == group:
            one(ref, parity, 0, ref is own)
        else:
            if ref is own:
                for copy in copies[:3]:
                    copy.wait()
            lax.fori_loop(
                0, charts // group,
                lambda g, c, r=ref, p=parity: (one(r, p, g * group, False), c)[1], 0,
            )
    whole = mem_scr[...].astype(BF)
    mem[...] = whole
    for copy in copies[3:]:
        copy.wait()
    mk[...] = dot(whole, ck[...]).astype(BF)
    mv[...] = dot(whole, cv[...]).astype(BF)
    leaving = [
        pltpu.make_async_copy(src, dst, out_sems.at[n])
        for n, (src, dst) in enumerate(((a1, a1_out), (k, k_out), (v, v_out)))
        if staged
    ]
    for copy in leaving:
        copy.start()
    row = lax.broadcasted_iota(jnp.int32, (QB, QB), 0)
    col = lax.broadcasted_iota(jnp.int32, (QB, QB), 1)

    def pair_copy(n):
        at = pl.ds(2 * n, 2)
        return pltpu.make_async_copy(q_aug.at[at], q_aug_out.at[at], pair_sems.at[n])

    def pair(n):
        wide = pl.ds(pl.multiple_of(n * 128, 128), 128)

        def one_block(i, count):
            at = pl.ds(i * QB, QB) if count is not None else pl.ds(pl.multiple_of(i * QB, QB), QB)
            qp = q[at, wide]
            outs = []
            for h in (0, 1):
                mine, marks = head_masks(h)
                mb = mine.astype(BF)
                rest = (1.0 - mine).astype(BF)
                qh = qp * mb

                def scores(j):
                    return nt(qh, k[pl.ds(pl.multiple_of(j * QB, QB), QB), wide])

                def weigh(e, j):
                    vh = v[pl.ds(pl.multiple_of(j * QB, QB), QB), wide] * mb + rest
                    return dot(e.astype(BF), vh)

                diag = jnp.where(row >= col, scores(i), NEGATIVE)
                if count is not None:
                    parts = [scores(j) for j in range(count - 1)] + [diag]
                    top = parts[0]
                    for s in parts[1:]:
                        top = jnp.maximum(top, s)
                    top = jnp.max(top, axis=1, keepdims=True)
                    acc = weigh(jnp.exp(parts[0] - top), 0)
                    for j, s in enumerate(parts[1:]):
                        acc = acc + weigh(jnp.exp(s - top), j + 1)
                else:
                    top = jnp.max(diag, axis=1, keepdims=True)
                    acc = weigh(jnp.exp(diag - top), i)

                    def step(j, state):
                        top, acc = state
                        s = scores(j)
                        new = jnp.maximum(top, jnp.max(s, axis=1, keepdims=True))
                        return new, acc * jnp.exp(top - new) + weigh(jnp.exp(s - new), j)

                    top, acc = lax.fori_loop(0, i, step, (top, acc))
                total = pltpu.roll(acc, 64, 1)
                outs.append(acc / (total * mine + (1.0 - mine)) * mine)
                lse = top + jnp.log(acc * (1.0 - mine) + mine)
                q_aug[2 * n + h, at, :] = add_marks(mine, marks, qp.astype(F32), -lse)
            o = (outs[0] + outs[1]).astype(BF)
            o_nat[at, wide] = o
            per = QB // (2 * tokens)
            for c in range(per):
                even = o[2 * c * tokens : (2 * c + 1) * tokens]
                odd = o[(2 * c + 1) * tokens : (2 * c + 2) * tokens]
                spot = pl.ds(pl.multiple_of((i * per + c) * tokens, tokens), tokens)
                flag = jnp.full(even.shape, core, jnp.int32).astype(F32)
                ef, of = even.astype(F32), odd.astype(F32)
                o_keep[spot, wide] = jnp.where(flag == 0, ef, of).astype(BF)
                o_send[spot, wide] = jnp.where(flag == 0, of, ef).astype(BF)

        if size <= 1024:
            for i in range(size // QB):
                one_block(i, i + 1)
        else:
            lax.fori_loop(0, size // QB, lambda i, c: (one_block(i, None), c)[1], 0)

    def pair_and_copy(n, carry):
        pair(n)
        if staged:
            pair_copy(n).start()
        return carry

    lax.fori_loop(0, half // 128, pair_and_copy, 0)
    info = jnp.full((16, 128), meta[2], jnp.int32)
    o_send[size // 2 :, :128] = (info // 16).astype(F32).astype(BF)
    o_send[size // 2 :, 128:256] = lax.rem(info, 16).astype(F32).astype(BF)
    o_send[size // 2 :, 256:] = jnp.zeros((16, half - 256), BF)
    for copy in leaving:
        copy.wait()
    for n in range(half // 128 if staged else 0):
        pair_copy(n).wait()


def attend_back_kernel(
    tokens, meta, q_aug, k, v, o_nat, do_own, do_oth, dq, dk, dv, k_aug, v_aug, kt, dk_acc, dv_acc
):
    core = meta[0]
    size = k.shape[0]
    krow = lax.broadcasted_iota(jnp.int32, (QB, QB), 0)
    qcol = lax.broadcasted_iota(jnp.int32, (QB, QB), 1)
    kt[...] = k[...].astype(F32).T.astype(BF)
    for h in (0, 1):
        mine, marks = head_masks(h)
        ones = (marks[0] + marks[1] + marks[2]).astype(BF)
        k_aug[h] = k[...] * mine.astype(BF) + ones
        v_aug[h] = v[...] * mine.astype(BF) + ones
    dk_acc[...] = jnp.zeros_like(dk_acc)
    dv_acc[...] = jnp.zeros_like(dv_acc)

    def one_block(i, count):
        at = pl.ds(pl.multiple_of(i * QB, QB), QB)
        per = QB // (2 * tokens)
        pieces = []
        for c in range(per):
            spot = pl.ds(pl.multiple_of((i * per + c) * tokens, tokens), tokens)
            a, b = do_own[spot, :].astype(F32), do_oth[spot, :].astype(F32)
            flag = jnp.full(a.shape, core, jnp.int32)
            pieces += [jnp.where(flag == 0, a, b), jnp.where(flag == 0, b, a)]
        do = jnp.concatenate(pieces, 0)
        prod = do * o_nat[at, :].astype(F32)
        turned = []
        for h in (0, 1):
            mine, marks = head_masks(h)
            delta = jnp.sum(prod * mine, axis=1, keepdims=True)
            doa = add_marks(mine, marks, do, -delta)
            qa = q_aug[h, at, :]

            def one(j, dqt, diagonal):
                kat = pl.ds(pl.multiple_of(j * QB, QB), QB)
                s = nt(k_aug[h, kat, :], qa)
                if diagonal:
                    s = jnp.where(qcol >= krow, s, NEGATIVE)
                p = jnp.exp(s)
                ds = (p * nt(v_aug[h, kat, :], doa)).astype(BF)
                dv_acc[h, kat, :] += dot(p.astype(BF), doa)
                dk_acc[h, kat, :] += dot(ds, qa)
                return dqt + dot(kt[64 * h : 64 * h + 64, kat], ds)

            dqt = jnp.zeros((64, QB), F32)
            if count is not None:
                for j in range(count - 1):
                    dqt = one(j, dqt, False)
            else:
                dqt = lax.fori_loop(0, i, lambda j, c: one(j, c, False), dqt)
            turned.append(one(i, dqt, True))
        dq[at, :] = (jnp.concatenate(turned, 0).T * 0.125).astype(BF)

    if size <= 1024:
        for i in range(size // QB):
            one_block(i, i + 1)
    else:
        lax.fori_loop(0, size // QB, lambda i, c: (one_block(i, None), c)[1], 0)
    m0, m1 = head_masks(0)[0], head_masks(1)[0]
    dk[...] = (dk_acc[0] * m0 + dk_acc[1] * m1).astype(BF)
    dv[...] = (dv_acc[0] * m0 + dv_acc[1] * m1).astype(BF)


def cross_pair(ref, p):
    lane = lanes(128)
    piece = ref[:, 128 * p : 128 * p + 128]
    low = (lane < 64).astype(BF)
    high = (lane >= 64).astype(BF)
    return jnp.concatenate([piece * low, piece * high], 0)


def cross_kernel(
    meta, x, o_own, o_oth, info, w_out, g_cross, c_query, mk, mv, c_out, g_ffn,
    o1, y1, a2, cq, p2, o2, y2, a3,
):
    core = meta[0]
    half = o_own.shape[1]
    mine = pl.ds(pl.multiple_of(core * half, 128), half)
    other = pl.ds(pl.multiple_of((1 - core) * half, 128), half)
    o1[:, mine] = o_own[...]
    o1[:, other] = o_oth[...]
    first = x[...].astype(F32) + dot(o1[...], w_out[...])
    y1[...] = first
    n2 = (first * inv_rms(first) * g_cross[...]).astype(BF)
    a2[...] = n2
    query = dot(n2, c_query[...]).astype(BF)
    cq[...] = query
    patches = mk.shape[0]
    lane = lanes(2 * patches)
    low = lane < patches
    sent = info[0:1, 0:1].astype(F32) * 16.0 + info[0:1, 128:129].astype(F32)
    known = jnp.full((1, 1), meta[2], jnp.int32).astype(F32)
    same = jnp.full((1, 1), meta[0] - meta[4], jnp.int32) == 0
    count = jnp.where(same, known, sent)
    valid = jnp.where(low, lane, lane - patches).astype(F32) < count
    for p in range(H // 2):
        keys = cross_pair(mk, p)
        values = cross_pair(mv, p)
        s = nt(query[:, 128 * p : 128 * p + 128], keys) * 0.125
        s = jnp.where(valid, s, NEGATIVE)
        m0 = jnp.max(jnp.where(low, s, NEGATIVE), axis=1, keepdims=True)
        m1 = jnp.max(jnp.where(low, NEGATIVE, s), axis=1, keepdims=True)
        e = jnp.exp(s - jnp.where(low, m0, m1))
        l0 = jnp.sum(jnp.where(low, e, 0.0), axis=1, keepdims=True)
        l1 = jnp.sum(jnp.where(low, 0.0, e), axis=1, keepdims=True)
        w = e / jnp.where(low, l0, l1)
        p2[p] = w
        o2[:, 128 * p : 128 * p + 128] = dot(w.astype(BF), values).astype(BF)
    second = first + dot(o2[...], c_out[...])
    y2[...] = second
    a3[...] = (second * inv_rms(second) * g_ffn[...]).astype(BF)


def ffn_kernel(
    row_blocks, meta, a3, cot, y2, g_ffn, wg, wu, wd,
    out, dy2, dy2b, gain, send, keep, acc, err, a3t, cott, dw, gu_buf, wd_buf, sems,
):
    core = meta[0]
    i, r = pl.program_id(0), pl.program_id(1)
    rows = pl.ds(pl.multiple_of(r * ROWS, ROWS), ROWS)
    first, last = i == 0, i == pl.num_programs(0) - 1

    @pl.when(first)
    def _():
        a3t[:, rows] = a3[...].astype(F32).T.astype(BF)
        cott[:, rows] = cot[...].astype(F32).T.astype(BF)
        acc[rows, :] = y2[...]
        err[rows, :] = jnp.zeros((ROWS, err.shape[1]), F32)

    gate = dot(a3[...], wg[...])
    up = dot(a3[...], wu[...])
    square = gate * gate
    th = jnp.tanh(0.7978845608028654 * gate * (1.0 + 0.044715 * square))
    more = 0.5 * (1.0 + th)
    act = gate * more
    slope = more + 0.5 * gate * (1.0 - th * th) * (
        0.7978845608028654 * (1.0 + 3 * 0.044715 * square)
    )
    hidden = (act * up).astype(BF)
    dh = nt(cot[...], wd[...])
    d_gate = (dh * up * slope).astype(BF)
    d_up = (dh * act).astype(BF)
    acc[rows, :] += dot(hidden, wd[...])
    err[rows, :] += nt(d_gate, wg[...]) + nt(d_up, wu[...])
    terms = (dot(a3t[:, rows], d_gate), dot(a3t[:, rows], d_up), dot(cott[:, rows], hidden))
    if row_blocks > 1:
        for n, term in enumerate(terms):
            dw[n] = jnp.where(r == 0, 0.0, dw[n]) + term
        terms = (dw[0], dw[1], dw[2])

    slot = lax.rem(i, 2)
    side = i // 2

    def gu_copy(dst):
        return pltpu.make_async_copy(gu_buf.at[slot], dst.at[side, pl.ds(0, 2)], sems.at[0, slot])

    def wd_copy(n, dst):
        return pltpu.make_async_copy(
            wd_buf.at[slot, n], dst.at[:, 2, pl.ds(2 * i, 2)], sems.at[1 + n, slot]
        )

    def drain(at):
        pltpu.make_async_copy(gu_buf.at[at], keep.at[0, pl.ds(0, 2)], sems.at[0, at]).wait()
        for n, dst in enumerate((send, keep)):
            pltpu.make_async_copy(
                wd_buf.at[at, n], dst.at[:, 2, pl.ds(0, 2)], sems.at[1 + n, at]
            ).wait()

    def put():
        pl.when(i >= 2)(lambda: drain(slot))
        width = terms[0].shape[1]
        for n in (0, 1):
            gu_buf[slot, n] = terms[n].astype(BF).reshape(8, terms[n].shape[0] // 8, width)
        down = terms[2].astype(BF)
        per, part, wide = down.shape[0] // 4, down.shape[0] // 8, width // 2
        for b in range(4):
            kept = jnp.where(core == b % 2, 1, 0)
            for y in range(2):
                piece = down[b * per : (b + 1) * per, y * wide : (y + 1) * wide]
                packed = jnp.concatenate([piece[:part], piece[part:]], 1)
                wd_buf[slot, kept, b // 2, y] = packed
        pl.when(slot == core)(lambda: gu_copy(keep).start())
        pl.when(slot != core)(lambda: gu_copy(send).start())
        wd_copy(0, send).start()
        wd_copy(1, keep).start()

        @pl.when(last)
        def _():
            drain(1 - slot)
            drain(slot)

    if row_blocks > 1:
        pl.when(r == row_blocks - 1)(put)
    else:
        put()

    @pl.when(last)
    def _():
        out[...] = acc[rows, :].astype(BF)
        back, gsum = norm_back(err[rows, :], y2[...], g_ffn[...])
        total = cot[...].astype(F32) + back
        dy2[...] = total
        dy2b[...] = total.astype(BF)
        gain[...] = jnp.where(r == 0, 0.0, gain[...]) + gsum


def cross_back_kernel(
    charts, patches_each, meta, dy2, dy2b, c_out, p2, mk, mv, cq, y1, g_cross, c_query, w_out,
    c_key_hbm, c_value_hbm,
    dcq, dmk, dmv, dy1, dy1b, do_keep, do_send, memg, gain, mk_acc, mv_acc, mem_scr, c_key, c_value, sems,
):
    core = meta[0]
    r = pl.program_id(0)
    half = do_keep.shape[1]
    patches = mk.shape[0]
    lane = lanes(2 * patches)
    low = lane < patches
    left = (lanes(128) < 64).astype(F32)
    do2 = nt(dy2b[...], c_out[...]).astype(BF)
    fresh = r == 0
    copies = [
        pltpu.make_async_copy(c_key_hbm, c_key, sems.at[0]),
        pltpu.make_async_copy(c_value_hbm, c_value, sems.at[1]),
    ]

    @pl.when(fresh)
    def _():
        for copy in copies:
            copy.start()

    for p in range(H // 2):
        at = slice(128 * p, 128 * p + 128)
        keys = cross_pair(mk, p)
        values = cross_pair(mv, p)
        w = p2[p]
        dp = nt(do2[:, at], values)
        prod = w * dp
        r0 = jnp.sum(jnp.where(low, prod, 0.0), axis=1, keepdims=True)
        r1 = jnp.sum(jnp.where(low, 0.0, prod), axis=1, keepdims=True)
        ds = w * (dp - jnp.where(low, r0, r1))
        dcq[:, at] = (dot(ds.astype(BF), keys) * 0.125).astype(BF)
        gk = dot(ds.T.astype(BF), cq[:, at]) * 0.125
        gv = dot(w.T.astype(BF), do2[:, at])
        gk = gk[:patches] * left + gk[patches:] * (1.0 - left)
        gv = gv[:patches] * left + gv[patches:] * (1.0 - left)
        mk_acc[:, at] = jnp.where(fresh, 0.0, mk_acc[:, at]) + gk
        mv_acc[:, at] = jnp.where(fresh, 0.0, mv_acc[:, at]) + gv
    err = nt(dcq[...], c_query[...])
    back, gsum = norm_back(err, y1[...], g_cross[...])
    total = dy2[...] + back
    dy1[...] = total
    tb = total.astype(BF)
    dy1b[...] = tb
    gain[...] = jnp.where(fresh, 0.0, gain[...]) + gsum
    do_keep[...] = nt(tb, w_out[pl.ds(pl.multiple_of(core * half, half), half), :]).astype(BF)
    rows = tb.shape[0]
    do_send[pl.ds(pl.multiple_of(r * rows, rows), rows), :] = nt(
        tb, w_out[pl.ds(pl.multiple_of((1 - core) * half, half), half), :]
    ).astype(BF)

    @pl.when(r == pl.num_programs(0) - 1)
    def _():
        gk, gv = mk_acc[...].astype(BF), mv_acc[...].astype(BF)
        for copy in copies:
            copy.wait()
        dmk[...] = gk
        dmv[...] = gv
        mem_scr[...] = nt(gk, c_key[...]) + nt(gv, c_value[...])

        def gather(parity):
            return jnp.concatenate(
                [
                    mem_scr[pl.ds(pl.multiple_of((2 * a + parity) * patches_each, 8), patches_each), :]
                    for a in range(charts)
                ],
                0,
            )

        memg[...] = gather(core)
        away = gather(1 - core).astype(BF)
        extra = away.shape[0]
        base = do_send.shape[0] - 2 * extra
        do_send[base : base + extra, :] = away[:, :half]
        do_send[base + extra :, :] = away[:, half:]


def square_kernel(meta, o2, dy2b, a2, dcq, mem, dmk, dmv, o1, dy1b, send, keep):
    core = meta[0]
    half = keep.shape[2]
    mine = pl.ds(pl.multiple_of(core * half, 128), half)
    other = pl.ds(pl.multiple_of((1 - core) * half, 128), half)
    memt = mem[...].astype(F32).T.astype(BF)
    pairs = ((o2, dy2b), (a2, dcq), (None, dmk), (None, dmv), (o1, dy1b))
    for n, (left, right) in enumerate(pairs):
        turned = memt if left is None else left[...].astype(F32).T.astype(BF)
        send[n] = dot(turned, right[:, other]).astype(BF)
        keep[n] = dot(turned, right[:, mine]).astype(BF)


def leave_kernel(
    split, charts, tokens, meta, a1, dq, dk, dv, wq, wk, wv, column, g_cross, g_ffn, *outs,
):
    half = dq.shape[1]
    size = dq.shape[0]
    width = g_ffn.shape[1]
    core, parity = meta[0], meta[4]
    cols = pl.ds(pl.multiple_of(core * half, 128), half)
    e_keep, e_send = outs[0], outs[1]
    out, scr = (outs[4], outs[5]) if split else (outs[2], outs[3])
    third = width // 3

    def rows_of(n):
        at = pl.ds(pl.multiple_of(n * third, third), third)
        turned = a1[:, at].astype(F32).T.astype(BF)
        gain = jnp.zeros((third, 1), F32)
        for m, (right, weight) in enumerate(((dq, wq), (dk, wk), (dv, wv))):
            block = dot(turned, right[...])
            gain += jnp.sum(block * weight[at, cols].astype(F32), axis=1, keepdims=True)
            out[at, m * half : (m + 1) * half] = block.astype(BF)
        gain = gain / column[at, :]
        stack = jnp.concatenate(
            [g_cross[:, at], g_ffn[:, at], jnp.zeros((126, third), F32)], 0
        ).T
        out[at, 3 * half :] = (jnp.where(lanes(128) == 2, gain, stack)).astype(BF)

    lax.fori_loop(0, 3, lambda n, c: (rows_of(n), c)[1], 0)
    if split:
        send, keep = outs[2], outs[3]
        part = width // 8
        for n in range(4):
            keep[n] = out[pl.ds(pl.multiple_of((2 * n + parity) * part, part), part), :]
            send[n] = out[pl.ds(pl.multiple_of((2 * n + 1 - parity) * part, part), part), :]
    step = scr.shape[0]
    per = step // (2 * tokens)

    def one(first):
        at = pl.ds(pl.multiple_of(first * step, step), step)
        scr[...] = (
            nt(dq[at, :], wq[:, cols]) + nt(dk[at, :], wk[:, cols]) + nt(dv[at, :], wv[:, cols])
        )
        for c in range(per):
            spot = pl.ds(pl.multiple_of((first * per + c) * tokens, tokens), tokens)
            e_keep[spot, :] = scr[pl.ds(pl.multiple_of((2 * c + core) * tokens, tokens), tokens), :]
            e_send[spot, :] = scr[
                pl.ds(pl.multiple_of((2 * c + 1 - core) * tokens, tokens), tokens), :
            ].astype(BF)

    lax.fori_loop(0, size // step, lambda g, c: (one(g), c)[1], 0)


def mix_kernel(meta, keep, recv, send1, kept1, send2, kept2):
    side, parity = meta[3], meta[4]
    rows = keep.shape[3]
    low = rows // 2

    def gu(x, w, s):
        return (keep[x, w, s].astype(F32) + recv[x, w, s].astype(F32)).astype(BF)

    def wd(x, s, part):
        return (keep[x, 2, s, part, :].astype(F32) + recv[x, 2, s, part, :].astype(F32)).astype(BF)

    for s in range(8):
        for x, to in ((1 - side, send1), (side, kept1)):
            to[s, :rows, :] = gu(x, 0, s)
            to[s, rows:, :] = wd(x, s, slice(0, low))
    for n in range(4):
        for x in range(2):
            for y, to in ((1 - parity, send2), (parity, kept2)):
                to[x, n, :rows, :] = gu(x, 1, 2 * n + y)
                to[x, n, rows:, :] = wd(x, 2 * n + y, slice(low, rows))


def input_grad_kernel(e_keep, e_recv, x, gain, dy1, out):
    err = e_keep[...] + e_recv[...].astype(F32)
    back, _ = norm_back(err, x[...].astype(F32), gain[...])
    out[...] = (dy1[...] + back).astype(BF)


def total(parts):
    result = parts[0].astype(F32)
    for part in parts[1:]:
        result = result + part.reshape(result.shape).astype(F32)
    return result


def tie(value, *deps):
    return lax.optimization_barrier((value, deps))[0]


def turn_in_kernel(meta, base, recv, send, keep):
    v, z = meta[5], meta[6]
    send[z] = base[z, 1 - v]
    send[1 - z] = recv[1 - v]
    keep[z] = base[z, v]
    keep[1 - z] = recv[v]


def gather_kernel(meta, keep, recv, out):
    v = meta[5]
    for n in range(2):
        out[n, v] = keep[n]
        out[n, 1 - v] = recv[n]


def finish_kernel(tokens, got, first, few):
    for n in range(got.shape[0]):
        first[n] = got[n, :tokens, :].astype(F32)
        few[n] = got[n, tokens:, :].astype(F32)


def place_kernel(charts, meta, *refs):
    place = meta[1]
    out = refs[-1]
    for d in range(charts):
        out[lax.rem(place - d + charts, charts)] = refs[d][...].astype(out.dtype)


def local(
    nseq, inputs, memory, patch_count, cotangent, norm_self, w_query, w_key, w_value, w_out,
    norm_cross, c_query, c_key, c_value, c_out, norm_ffn, w_gate, w_up, w_down,
):
    charts, tokens, width = inputs.shape
    patches_each = memory.shape[1]
    size = charts * 2 * tokens
    own = charts * tokens
    patches = patches_each * nseq
    half = width // 2
    small = size <= 1024
    hidden = w_gate.shape[1]
    blocks = own // ROWS
    dp = lax.axis_index("dp")
    seq = lax.axis_index("seq")
    side, core = dp // 2, lax.rem(dp, 2)
    place, parity = seq // 2, lax.rem(seq, 2)

    def shift(d):
        return [
            ((2 * x + k) * nseq + 2 * a + b, (2 * x + b) * nseq + 2 * ((a + d) % charts) + k)
            for x in range(2)
            for k in range(2)
            for a in range(charts)
            for b in range(2)
        ]

    def dp_perm(rule):
        return [(2 * x + k, 2 * rule(x, k)[0] + rule(x, k)[1]) for x in range(2) for k in range(2)]

    swap_core = dp_perm(lambda x, k: (x, 1 - k))
    swap_side = dp_perm(lambda x, k: (1 - x, k))

    def across(value):
        return lax.ppermute(value, "dp", swap_core)

    def travel(value, d):
        return lax.ppermute(value, ("dp", "seq"), shift(d))

    def pick(value, d):
        return lax.dynamic_index_in_dim(value, lax.rem(place + d, charts), 0, keepdims=False)

    gain_self, gain_cross, gain_ffn = (g.reshape(1, width) for g in (norm_self, norm_cross, norm_ffn))
    count = lax.dynamic_index_in_dim(patch_count, place, 0, keepdims=False)
    meta = jnp.stack(
        [core, place, count, side, parity, lax.rem(place, 2), place // 2]
    ).astype(jnp.int32)

    trade = [
        ((2 * x + k) * nseq + 2 * a + b, (2 * x + b) * nseq + 2 * a + k)
        for x in range(2)
        for k in range(2)
        for a in range(charts)
        for b in range(2)
    ]
    flips = {
        name: [(s, s ^ (1 << bit)) for s in range(nseq)] for bit, name in enumerate("yvz")
    }
    low_bit, high_bit = lax.rem(place, 2), place // 2

    mine = jnp.stack(
        [
            travel(jnp.concatenate([pick(inputs, d), pick(memory, d)], 0), d)
            for d in range(charts)
        ]
    )
    theirs = across(mine)
    if small:
        cot_base = lax.ppermute(cotangent, ("dp", "seq"), trade)
        cot_base = cot_base.reshape(2, 2, tokens, width)
        cot_away = lax.dynamic_index_in_dim(cot_base, 1 - high_bit, 0, keepdims=False)
        cot_got = lax.ppermute(cot_away, "seq", flips["z"])
        theirs = tie(theirs, cot_away)
    else:
        cot_parts = [travel(pick(cotangent, d), d) for d in range(charts)]
    pairs = half // 128
    pair_spec = pl.BlockSpec((size, 128), lambda p, m: (0, p))
    own_spec = pl.BlockSpec((own, 128), lambda p, m: (0, p))
    aug_spec = pl.BlockSpec((2, size, 128), lambda p, m: (p, 0, 0))
    far = pltpu.HBM if small else sds
    x_own, a1, k, v, mem, mk, mv, o_keep, o_send, o_nat, q_aug = pl.pallas_call(
        functools.partial(enter_kernel, small, charts, tokens, patches_each),
        compiler_params=room(small, 24),
        out_shape=(
            sds((own, width), BF), far((size, width), BF), far((size, half), BF),
            far((size, half), BF), sds((patches, width), BF), sds((patches, width), BF),
            sds((patches, width), BF), sds((own, half), BF), sds((own + 16, half), BF),
            far((size, half), BF), far((2 * pairs, size, 128), BF),
        ),
        in_specs=[SM] + [VM] * 3 + [pl.BlockSpec(memory_space=pltpu.HBM)] * 5,
        out_specs=([VM] + [HB] * 3 + [VM] * 6 + [HB]) if small else [VM] * 11,
        scratch_shapes=[
            pltpu.VMEM((patches, width), F32), pltpu.VMEM((size, half), BF),
            pltpu.VMEM((width, half), BF), pltpu.VMEM((width, half), BF),
            pltpu.VMEM((width, half), BF), pltpu.VMEM((width, width), BF),
            pltpu.VMEM((width, width), BF), pltpu.SemaphoreType.DMA((5,)),
        ]
        + (
            [
                pltpu.VMEM((size, width), BF), pltpu.VMEM((size, half), BF),
                pltpu.VMEM((size, half), BF), pltpu.VMEM((2 * pairs, size, 128), BF),
                pltpu.SemaphoreType.DMA((3,)), pltpu.SemaphoreType.DMA((pairs,)),
            ]
            if small
            else []
        ),
        cost_estimate=cost(2 * size * width * 3 * half, mine, theirs, w_query, w_key, w_value),
    )(
        meta, mine, theirs, gain_self,
        *(
            pltpu.with_memory_space_constraint(w, pltpu.HBM)
            for w in (w_query, w_key, w_value, c_key, c_value)
        ),
    )
    if small:
        part = sds((2, tokens, width), BF)
        cot_send, cot_keep = pl.pallas_call(
            turn_in_kernel,
            compiler_params=room(small, 6),
            out_shape=(part, part),
            in_specs=[SM, VM, VM],
            out_specs=[VM] * 2,
        )(meta, cot_base, cot_got)
        cot_got = lax.ppermute(cot_send, "seq", flips["v"])
        o_recv = tie(across(o_send), cot_send)
    else:
        o_recv = across(o_send)

    each = ROWS if small else QB
    row_spec = pl.BlockSpec((each, width), lambda r: (r, 0))
    half_spec = pl.BlockSpec((each, half), lambda r: (r, 0))
    p2_spec = pl.BlockSpec((H // 2, each, 2 * patches), lambda r: (0, r, 0))

    def fixed(shape, spaces=1):
        if spaces == 1:
            return pl.BlockSpec(shape, lambda r: (0,) * len(shape))
        return pl.BlockSpec(shape, lambda i, r: (0,) * len(shape))

    square = fixed((width, width))
    one_row = fixed((1, width))
    patch_spec = fixed((patches, width))
    rows_f = sds((own, width), F32)
    rows_b = sds((own, width), BF)
    o1, y1, a2, cq, p2, o2, y2, a3 = pl.pallas_call(
        cross_kernel,
        compiler_params=room(small, 16),
        out_shape=(
            rows_b, rows_f, rows_b, rows_b, sds((H // 2, own, 2 * patches), F32), rows_b, rows_f,
            rows_b,
        ),
        grid=(own // each,),
        in_specs=[
            SM, row_spec, half_spec, half_spec, pl.BlockSpec((16, half), lambda r: (own // 16, 0)),
            square, one_row, square, patch_spec, patch_spec, square, one_row,
        ],
        out_specs=[row_spec] * 4 + [p2_spec] + [row_spec] * 3,
        cost_estimate=cost(6 * own * width * width, w_out, c_query, c_out, rows_f, rows_f),
    )(meta, x_own, o_keep, o_recv, o_recv, w_out, gain_cross, c_query, mk, mv, c_out, gain_ffn)

    def placed(parts, dtype):
        return pl.pallas_call(
            functools.partial(place_kernel, charts),
            compiler_params=room(small, 6),
            out_shape=sds((charts,) + parts[0].shape, dtype),
            in_specs=[SM] + [VM] * charts,
            out_specs=VM,
        )(meta, *parts)

    if small:
        cot = pl.pallas_call(
            gather_kernel,
            compiler_params=room(small, 6),
            out_shape=sds((2, 2, tokens, width), BF),
            in_specs=[SM, VM, VM],
            out_specs=VM,
        )(meta, cot_keep, tie(cot_got, y2)).reshape(own, width)
    else:
        cot = placed(cot_parts, BF).reshape(own, width)
    wide = hidden // 4
    last = 3
    f_pack = sds((2, 3, 8, width // 8, wide), BF)
    anywhere = pl.BlockSpec(memory_space=pl.ANY)
    frow = pl.BlockSpec((ROWS, width), lambda i, r: (r, 0))
    lrow = pl.BlockSpec((ROWS, width), lambda i, r: (r * (i // last), 0))
    out_b, dy2, dy2b, ffn_gain, f_send, f_keep = pl.pallas_call(
        functools.partial(ffn_kernel, blocks),
        compiler_params=room(small, 30),
        out_shape=(rows_b, rows_f, rows_b, sds((1, width), F32), f_pack, f_pack),
        grid=(4, blocks),
        in_specs=[
            SM, frow, frow, frow, fixed((1, width), 2),
            pl.BlockSpec((width, wide), lambda i, r: (0, i)),
            pl.BlockSpec((width, wide), lambda i, r: (0, i)),
            pl.BlockSpec((wide, width), lambda i, r: (i, 0)),
        ],
        out_specs=[lrow, lrow, lrow, fixed((1, width), 2), anywhere, anywhere],
        scratch_shapes=[
            pltpu.VMEM((own, width), F32), pltpu.VMEM((own, width), F32),
            pltpu.VMEM((width, own), BF), pltpu.VMEM((width, own), BF),
            pltpu.VMEM((3, width, wide) if blocks > 1 else (3, 8, 128), F32),
            pltpu.VMEM((2, 2, 8, width // 8, wide), BF),
            pltpu.VMEM((2, 2, 2, 2, width // 8, wide), BF), pltpu.SemaphoreType.DMA((3, 2)),
        ],
        cost_estimate=cost(18 * own * width * hidden, w_gate, w_up, w_down, rows_f, rows_f),
    )(meta, a3, cot, y2, gain_ffn, w_gate, w_up, w_down)
    f_recv = across(f_send)

    def back_first(rows):
        return lax.ppermute(rows, ("dp", "seq"), trade)

    def back_second(rows):
        base = rows.reshape((2, 2) + rows.shape[1:])
        away = lax.dynamic_index_in_dim(base, 1 - high_bit, 0, keepdims=False)
        return base, lax.ppermute(away, "seq", flips["z"])

    def back_turn(base, got):
        return pl.pallas_call(
            turn_in_kernel,
            compiler_params=room(small, 6),
            out_shape=(sds(got.shape, BF), sds(got.shape, BF)),
            in_specs=[SM, VM, VM],
            out_specs=[VM] * 2,
        )(meta, base, got)

    def gathered(keep, got):
        return pl.pallas_call(
            gather_kernel,
            compiler_params=room(small, 6),
            out_shape=sds((2, 2) + got.shape[1:], BF),
            in_specs=[SM, VM, VM],
            out_specs=VM,
        )(meta, keep, got).reshape((charts,) + got.shape[1:])

    def back_last(got):
        return pl.pallas_call(
            functools.partial(finish_kernel, tokens),
            compiler_params=room(small, 8),
            out_shape=(
                sds((charts, tokens, width), F32), sds((charts, patches_each, width), F32),
            ),
            in_specs=[VM],
            out_specs=[VM] * 2,
        )(got)

    def halve(which, keep, recv, outer):
        parts = (keep if isinstance(keep, list) else [keep]) + [recv]
        size_now, wide_now = parts[0].size, parts[0].shape[-1]
        shape = (outer, 2, size_now // (outer * 2 * wide_now), wide_now)
        parts = [p.reshape(shape) for p in parts]
        i = meta[which]
        sends = [lax.dynamic_index_in_dim(p, 1 - i, 1, keepdims=False) for p in parts]
        kept = [lax.dynamic_index_in_dim(p, i, 1, keepdims=False) for p in parts]
        return total(sends).astype(BF), kept

    def over(name, value):
        if name == "x":
            return lax.ppermute(value, "dp", swap_side)
        return lax.ppermute(value, "seq", flips[name])

    out_rows = out_b.reshape(charts, tokens, width)
    if small:
        out_base, out_got = back_second(out_rows)
    else:
        out_parts = [travel(pick(out_rows, d), d) for d in range(charts)]
    dcq, dmk, dmv, dy1, dy1b, do_keep, do_send, memg, cross_gain = pl.pallas_call(
        functools.partial(cross_back_kernel, charts, patches_each),
        compiler_params=room(small, 18),
        out_shape=(
            rows_b, sds((patches, width), BF), sds((patches, width), BF), rows_f, rows_b,
            sds((own, half), BF), sds((own + patches, half), BF),
            sds((patches // 2, width), F32), sds((1, width), F32),
        ),
        grid=(own // each,),
        in_specs=[
            SM, row_spec, row_spec, square, p2_spec, patch_spec, patch_spec, row_spec, row_spec,
            one_row, square, square, HB, HB,
        ],
        out_specs=[
            row_spec, patch_spec, patch_spec, row_spec, row_spec, half_spec,
            fixed((own + patches, half)), fixed((patches // 2, width)), one_row,
        ],
        scratch_shapes=[pltpu.VMEM((patches, width), F32)] * 3
        + [pltpu.VMEM((width, width), BF)] * 2
        + [pltpu.SemaphoreType.DMA((2,))],
        cost_estimate=cost(6 * own * width * width, w_out, c_query, c_out, rows_f, rows_f),
    )(meta, dy2, dy2b, c_out, p2, mk, mv, cq, y1, gain_cross, c_query, w_out, c_key, c_value)
    do_recv = across(do_send)

    if small:
        f1 = sds((8, 3 * width // 16, wide), BF)
        f2 = sds((2, 4, 3 * width // 16, wide), BF)
        f1_send, f1_keep, f2_send, f2_keep = pl.pallas_call(
            mix_kernel,
            compiler_params=room(small, 16),
            out_shape=(f1, f1, f2, f2),
            in_specs=[SM] + [VM] * 2,
            out_specs=[VM] * 4,
        )(meta, f_keep, f_recv)
        f1_recv, f2_recv = over("x", f1_send), over("y", f2_send)
        dcq = tie(dcq, f1_send)
    s_send, s_keep = pl.pallas_call(
        square_kernel,
        compiler_params=room(small, 16),
        out_shape=(sds((5, width, half), BF), sds((5, width, half), BF)),
        in_specs=[SM] + [VM] * 9,
        out_specs=[VM] * 2,
        cost_estimate=cost(6 * own * width * width, o1, o2, a2, dcq, dy2b, dy1b),
    )(meta, o2, dy2b, a2, dcq, mem, dmk, dmv, o1, dy1b)
    s_recv = across(s_send)

    few = patches // 2
    memg_recv = jnp.concatenate([do_recv[own : own + few], do_recv[own + few :]], 1)
    memg_own = (memg + memg_recv.astype(F32)).astype(BF).reshape(charts, patches_each, width)
    if small:
        s_send, s_keep = halve(5, s_keep, s_recv, 10)
        s_recv = over("v", s_send)
        do_recv = tie(do_recv, s_send)

    dq, dk, dv = pl.pallas_call(
        functools.partial(attend_back_kernel, tokens),
        compiler_params=room(small, 14),
        out_shape=(sds((size, half), BF),) * 3,
        grid_spec=pltpu.PrefetchScalarGridSpec(
            num_scalar_prefetch=1,
            grid=(pairs,),
            in_specs=[aug_spec, pair_spec, pair_spec, pair_spec, own_spec, own_spec],
            out_specs=[pair_spec] * 3,
            scratch_shapes=[
                pltpu.VMEM((2, size, 128), BF), pltpu.VMEM((2, size, 128), BF),
                pltpu.VMEM((128, size), BF),
                pltpu.VMEM((2, size, 128), F32), pltpu.VMEM((2, size, 128), F32),
            ],
        ),
        cost_estimate=cost(10 * size * size * half, k, v, q_aug),
    )(meta, q_aug, k, v, o_nat, do_keep, do_recv)

    if small:
        dq = tie(dq, f1_recv, f2_recv, out_got)
    t_whole = sds((width, 3 * half + 128), BF)
    t_piece = sds((4, width // 8, 3 * half + 128), BF)
    gone = pl.pallas_call(
        functools.partial(leave_kernel, small, charts, tokens),
        compiler_params=room(small, 14),
        out_shape=(rows_f, rows_b) + ((t_piece, t_piece) if small else (t_whole,)),
        in_specs=[SM] + [VM] * 10,
        out_specs=[VM] * (4 if small else 3),
        scratch_shapes=([pltpu.VMEM((width, 3 * half + 128), BF)] if small else [])
        + [pltpu.VMEM((256, width), F32)],
    )(
        meta, a1, dq, dk, dv, w_query, w_key, w_value, norm_self.reshape(width, 1), cross_gain,
        ffn_gain,
    )
    e_keep, e_send = gone[:2]
    e_recv = across(e_send)
    if small:
        t_send, t_keep = gone[2:]
        t_recv = over("y", t_send)
        e_recv = tie(e_recv, t_send)
    else:
        t_out = gone[2]

    in_grad = pl.pallas_call(
        input_grad_kernel,
        compiler_params=room(small, 8),
        out_shape=rows_b,
        in_specs=[VM] * 5,
        out_specs=VM,
        cost_estimate=cost(20 * own * width, e_keep, e_send, x_own, dy1),
    )(e_keep, e_recv, x_own, gain_self, dy1)
    in_rows = jnp.concatenate([in_grad.reshape(charts, tokens, width), memg_own], 1)
    if small:
        in_base, in_got = back_second(in_rows)
        out_send, out_keep = back_turn(out_base, tie(out_got, in_base))
        out_got = lax.ppermute(out_send, "seq", flips["v"])
        f2_send, f2_keep = halve(3, f2_keep, tie(f2_recv, out_send), 1)
        f2_recv = over("x", f2_send)
        s_send, s_keep = halve(3, s_keep, tie(s_recv, f2_send), 20)
        s_recv = over("x", s_send)
        t_send, t_keep = halve(3, t_keep, tie(t_recv, s_send), 4)
        t_recv = over("x", t_send)
        f2_send, f2_keep = halve(5, f2_keep, tie(f2_recv, t_send), 2)
        f2_recv = over("v", f2_send)
        f1_send, f1_keep = halve(4, f1_keep, tie(f1_recv, f2_send), 4)
        f1_recv = over("y", f1_send)
        out_rows = gathered(out_keep, tie(out_got, f1_send))
        out_mid = out_rows
        out_rows = back_first(out_rows)
        in_send, in_keep = back_turn(in_base, tie(in_got, out_mid))
        in_got = lax.ppermute(in_send, "seq", flips["v"])
        s_send, s_keep = halve(4, s_keep, tie(s_recv, in_send, f2_recv), 10)
        s_recv = over("y", s_send)
        t_send, t_keep = halve(5, t_keep, tie(t_recv, s_send), 2)
        t_recv = over("v", t_send)
        f1_send, f1_keep = halve(5, f1_keep, tie(f1_recv, t_send), 2)
        f1_recv = over("v", f1_send)
        t_send, t_keep = halve(6, t_keep, tie(t_recv, f1_send, s_recv), 1)
        t_recv = over("z", t_send)
        s_send, s_keep = halve(6, s_keep, tie(s_recv, t_send), 5)
        s_recv = over("z", s_send)
        in_rows = gathered(in_keep, tie(in_got, s_send))
        in_mid = in_rows
        in_rows = back_first(in_rows)
        f2_send, f2_keep = halve(6, f2_keep, tie(f2_recv, in_mid), 1)
        f2_recv = over("z", f2_send)
        f1_send, f1_keep = halve(6, f1_keep, tie(f1_recv, f2_send), 1)
        f1_recv = over("z", f1_send)
    else:
        in_parts = [travel(pick(in_rows, d), d) for d in range(charts)]

    if small:
        f1_sum = total(f1_keep + [f1_recv]).reshape(3 * width // 16, wide)
        f2_sum = total(f2_keep + [f2_recv]).reshape(3 * width // 16, wide)
        t_part = total(t_keep + [t_recv]).reshape(width // 16, 3 * half + 128)
        t_zero = jnp.zeros_like(t_part)
        t_sum = jnp.concatenate(
            [jnp.where(side == 0, t_part, t_zero), jnp.where(side == 0, t_zero, t_part)], 0
        )
        s_part = total(s_keep + [s_recv])
        s_zero = jnp.zeros_like(s_part)
        s_sum = jnp.concatenate(
            [jnp.where(side == 0, s_part, s_zero), jnp.where(side == 0, s_zero, s_part)], 1
        )
        g_gate, g_up = f1_sum[: width // 8], f2_sum[: width // 8]
        g_down = jnp.concatenate([f1_sum[width // 8 :], f2_sum[width // 8 :]], 0)
        g_down = g_down.reshape(width // 8, 2, wide // 2).transpose(2, 1, 0)
        g_down = g_down.reshape(wide // 2, width // 4)
    else:

        def over_seq(value, axis):
            return lax.psum_scatter(
                value.astype(BF), "seq", scatter_dimension=axis, tiled=True
            ).astype(F32)

        def over_side(parts):
            sends = [lax.dynamic_index_in_dim(p, 1 - side, 0, keepdims=False) for p in parts]
            kept = [lax.dynamic_index_in_dim(p, side, 0, keepdims=False) for p in parts]
            return total(kept + [lax.ppermute(total(sends).astype(BF), "dp", swap_side)])

        f_all = over_side([f_keep, f_recv])
        g_two = over_seq(f_all[:2].reshape(2, width, wide), 1)
        g_gate, g_up = g_two[0], g_two[1]
        down = f_all[2].reshape(8, width // 8, 2, wide // 2)
        g_down = over_seq(down.transpose(0, 3, 2, 1).reshape(hidden, width // 4), 0)
        s_sum = over_seq(total([s_keep, s_recv]), 1)
        t_sum = over_seq(t_out, 0)

    rows = t_sum.shape[0]
    quarter = half // 2
    t_sum = t_sum.astype(BF)
    squares = jnp.concatenate(
        [t_sum[:, : 3 * half].reshape(rows, 3, half).transpose(1, 0, 2), s_sum.astype(BF)], 0
    ).reshape(8, rows, 2, quarter)
    gains = t_sum[:, 3 * half :]
    padded = jnp.pad(gains, ((0, 0), (0, quarter - 128)))[None]

    def deliver(block, rule):
        part = lax.dynamic_index_in_dim(squares, block, 2, keepdims=False)
        return lax.ppermute(jnp.concatenate([part, padded], 0), "dp", dp_perm(rule)).astype(F32)

    done = deliver(side, lambda x, k: (k, x)) + deliver(1 - side, lambda x, k: (k, 1 - x))
    rest = lax.ppermute(gains, "dp", dp_perm(lambda x, k: (1 - k, x))).astype(F32) + lax.ppermute(
        gains, "dp", dp_perm(lambda x, k: (1 - k, 1 - x))
    ).astype(F32)
    gain_sum = done[8, :, :128] + rest

    if small:
        in_all, few_all = back_last(in_rows)
        out_all = out_rows.astype(F32)
    else:
        out_all, in_all = placed(out_parts, F32), placed(in_parts, F32)
        in_all, few_all = in_all[:, :tokens], in_all[:, tokens:]
    return (
        out_all,
        in_all,
        few_all,
        gain_sum[:, 2],
        done[0],
        done[1],
        done[2],
        done[7],
        gain_sum[:, 0],
        done[4],
        done[5],
        done[6],
        done[3],
        gain_sum[:, 1],
        g_gate,
        g_up,
        g_down,
    )


def solution(mesh):
    tok = P("dp", "seq", None)
    cut = P("seq", "dp")
    in_specs = (tok, tok, P("dp"), tok) + (P(),) * 14
    out_specs = (tok, tok, tok, P("seq"), cut, cut, cut, cut, P("seq"), cut, cut, cut, cut)
    out_specs += (P("seq"), cut, cut, cut)
    return jax.shard_map(
        functools.partial(local, mesh.shape["seq"]),
        mesh=mesh,
        in_specs=in_specs,
        out_specs=out_specs,
        check_vma=False,
    )
```

```python
import functools

import jax
import jax.numpy as jnp
from jax import lax
from jax.experimental import pallas as pl
from jax.experimental.pallas import tpu as pltpu
from jax.sharding import PartitionSpec as P

H = 12
EPSILON = 1e-06
NEGATIVE = -1e30
F32 = jnp.float32
BF = jnp.bfloat16
VM = pl.BlockSpec(memory_space=pltpu.VMEM)
SM = pl.BlockSpec(memory_space=pltpu.SMEM)
HB = pl.BlockSpec(memory_space=pltpu.HBM)
ROWS = 512
QB = 256


def dot(a, b):
    return lax.dot_general(a, b, (((1,), (0,)), ((), ())), preferred_element_type=F32)


def nt(a, b):
    return lax.dot_general(a, b, (((1,), (1,)), ((), ())), preferred_element_type=F32)


def lanes(width):
    return lax.broadcasted_iota(jnp.int32, (1, width), 1)


def inv_rms(v):
    return lax.rsqrt(jnp.mean(v * v, axis=-1, keepdims=True) + EPSILON)


def norm_back(e, v, gain):
    r = inv_rms(v)
    u = v * r
    eg = e * gain
    grad_v = (eg - u * jnp.mean(eg * u, axis=-1, keepdims=True)) * r
    return grad_v, jnp.sum(e * u, axis=0, keepdims=True)


def cost(flops, *arrays):
    total = sum(a.size * a.dtype.itemsize for a in arrays)
    return pl.CostEstimate(flops=int(flops), bytes_accessed=int(total), transcendentals=0)


def room(small, mib):
    return pltpu.CompilerParams(vmem_limit_bytes=mib << 20) if small else None


def sds(shape, dtype):
    return jax.ShapeDtypeStruct(shape, dtype)


def split3(value):
    hi = value.astype(BF).astype(F32)
    mid = (value - hi).astype(BF).astype(F32)
    lo = (value - hi - mid).astype(BF).astype(F32)
    return hi, mid, lo


def head_masks(h):
    lane = lanes(128)
    mine = ((lane < 64) if h == 0 else (lane >= 64)).astype(F32)
    base = 64 if h == 0 else 0
    marks = [(lane == base + i).astype(F32) for i in range(3)]
    return mine, marks


def add_marks(mine, marks, body, extra):
    hi, mid, lo = split3(extra)
    return (body * mine + hi * marks[0] + mid * marks[1] + lo * marks[2]).astype(BF)


def enter_kernel(
    staged, charts, tokens, patches, meta, own, oth, gain, wq_hbm, wk_hbm, wv_hbm, ck_hbm, cv_hbm,
    x_own, a1_out, k_out, v_out, mem, mk, mv, o_keep, o_send, o_nat, q_aug_out,
    mem_scr, q, wq, wk, wv, ck, cv, sems, *stage,
):
    if staged:
        a1, k, v, q_aug, out_sems, pair_sems = stage
    else:
        a1, k, v, q_aug = a1_out, k_out, v_out, q_aug_out
    core, place = meta[0], meta[1]
    half = q.shape[1]
    width = a1.shape[1]
    size = q.shape[0]
    group = max(1, min(charts, ROWS // tokens))
    cols = pl.ds(pl.multiple_of(core * half, 128), half)
    copies = [
        pltpu.make_async_copy(src.at[:, cols], dst, sems.at[n])
        for n, (src, dst) in enumerate(((wq_hbm, wq), (wk_hbm, wk), (wv_hbm, wv)))
    ] + [
        pltpu.make_async_copy(src, dst, sems.at[3 + n])
        for n, (src, dst) in enumerate(((ck_hbm, ck), (cv_hbm, cv)))
    ]
    for copy in copies:
        copy.start()

    def one(ref, parity, first, fresh):
        x = ref[pl.ds(first, group), :tokens, :].reshape(group * tokens, width)
        xf = x.astype(F32)
        a = (xf * inv_rms(xf) * gain[...]).astype(BF)
        if fresh:
            for copy in copies[:3]:
                copy.wait()
        qq = (dot(a, wq[...]) * 0.125).astype(BF)
        kk = dot(a, wk[...]).astype(BF)
        vv = dot(a, wv[...]).astype(BF)
        for i in range(group):
            chunk = lax.rem(place - (first + i) + charts, charts)
            part = slice(i * tokens, (i + 1) * tokens)
            at = pl.ds(pl.multiple_of((2 * chunk + parity) * tokens, tokens), tokens)
            a1[at, :] = a[part]
            q[at, :] = qq[part]
            k[at, :] = kk[part]
            v[at, :] = vv[part]
            few = ref[first + i, tokens:, :].astype(F32)
            spot = pl.ds(pl.multiple_of((2 * chunk + parity) * patches, patches), patches)
            mem_scr[spot, :] = few
            if ref is own:
                x_own[pl.ds(pl.multiple_of(chunk * tokens, tokens), tokens), :] = x[part]

    for ref, parity in ((own, core), (oth, 1 - core)):
        if charts == group:
            one(ref, parity, 0, ref is own)
        else:
            if ref is own:
                for copy in copies[:3]:
                    copy.wait()
            lax.fori_loop(
                0, charts // group,
                lambda g, c, r=ref, p=parity: (one(r, p, g * group, False), c)[1], 0,
            )
    whole = mem_scr[...].astype(BF)
    mem[...] = whole
    for copy in copies[3:]:
        copy.wait()
    mk[...] = dot(whole, ck[...]).astype(BF)
    mv[...] = dot(whole, cv[...]).astype(BF)
    leaving = [
        pltpu.make_async_copy(src, dst, out_sems.at[n])
        for n, (src, dst) in enumerate(((a1, a1_out), (k, k_out), (v, v_out)))
        if staged
    ]
    for copy in leaving:
        copy.start()
    row = lax.broadcasted_iota(jnp.int32, (QB, QB), 0)
    col = lax.broadcasted_iota(jnp.int32, (QB, QB), 1)

    def pair_copy(n):
        at = pl.ds(2 * n, 2)
        return pltpu.make_async_copy(q_aug.at[at], q_aug_out.at[at], pair_sems.at[n])

    def pair(n):
        wide = pl.ds(pl.multiple_of(n * 128, 128), 128)

        def one_block(i, count):
            at = pl.ds(i * QB, QB) if count is not None else pl.ds(pl.multiple_of(i * QB, QB), QB)
            qp = q[at, wide]
            outs = []
            for h in (0, 1):
                mine, marks = head_masks(h)
                mb = mine.astype(BF)
                rest = (1.0 - mine).astype(BF)
                qh = qp * mb

                def scores(j):
                    return nt(qh, k[pl.ds(pl.multiple_of(j * QB, QB), QB), wide])

                def weigh(e, j):
                    vh = v[pl.ds(pl.multiple_of(j * QB, QB), QB), wide] * mb + rest
                    return dot(e.astype(BF), vh)

                diag = jnp.where(row >= col, scores(i), NEGATIVE)
                if count is not None:
                    parts = [scores(j) for j in range(count - 1)] + [diag]
                    top = parts[0]
                    for s in parts[1:]:
                        top = jnp.maximum(top, s)
                    top = jnp.max(top, axis=1, keepdims=True)
                    acc = weigh(jnp.exp(parts[0] - top), 0)
                    for j, s in enumerate(parts[1:]):
                        acc = acc + weigh(jnp.exp(s - top), j + 1)
                else:
                    top = jnp.max(diag, axis=1, keepdims=True)
                    acc = weigh(jnp.exp(diag - top), i)

                    def step(j, state):
                        top, acc = state
                        s = scores(j)
                        new = jnp.maximum(top, jnp.max(s, axis=1, keepdims=True))
                        return new, acc * jnp.exp(top - new) + weigh(jnp.exp(s - new), j)

                    top, acc = lax.fori_loop(0, i, step, (top, acc))
                total = pltpu.roll(acc, 64, 1)
                outs.append(acc / (total * mine + (1.0 - mine)) * mine)
                lse = top + jnp.log(acc * (1.0 - mine) + mine)
                q_aug[2 * n + h, at, :] = add_marks(mine, marks, qp.astype(F32), -lse)
            o = (outs[0] + outs[1]).astype(BF)
            o_nat[at, wide] = o
            per = QB // (2 * tokens)
            for c in range(per):
                even = o[2 * c * tokens : (2 * c + 1) * tokens]
                odd = o[(2 * c + 1) * tokens : (2 * c + 2) * tokens]
                spot = pl.ds(pl.multiple_of((i * per + c) * tokens, tokens), tokens)
                flag = jnp.full(even.shape, core, jnp.int32).astype(F32)
                ef, of = even.astype(F32), odd.astype(F32)
                o_keep[spot, wide] = jnp.where(flag == 0, ef, of).astype(BF)
                o_send[spot, wide] = jnp.where(flag == 0, of, ef).astype(BF)

        if size <= 1024:
            for i in range(size // QB):
                one_block(i, i + 1)
        else:
            lax.fori_loop(0, size // QB, lambda i, c: (one_block(i, None), c)[1], 0)

    def pair_and_copy(n, carry):
        pair(n)
        if staged:
            pair_copy(n).start()
        return carry

    lax.fori_loop(0, half // 128, pair_and_copy, 0)
    info = jnp.full((16, 128), meta[2], jnp.int32)
    o_send[size // 2 :, :128] = (info // 16).astype(F32).astype(BF)
    o_send[size // 2 :, 128:256] = lax.rem(info, 16).astype(F32).astype(BF)
    o_send[size // 2 :, 256:] = jnp.zeros((16, half - 256), BF)
    for copy in leaving:
        copy.wait()
    for n in range(half // 128 if staged else 0):
        pair_copy(n).wait()


def attend_back_kernel(
    tokens, meta, q_aug, k, v, o_nat, do_own, do_oth, dq, dk, dv, k_aug, v_aug, kt, dk_acc, dv_acc
):
    core = meta[0]
    size = k.shape[0]
    krow = lax.broadcasted_iota(jnp.int32, (QB, QB), 0)
    qcol = lax.broadcasted_iota(jnp.int32, (QB, QB), 1)
    kt[...] = k[...].astype(F32).T.astype(BF)
    for h in (0, 1):
        mine, marks = head_masks(h)
        ones = (marks[0] + marks[1] + marks[2]).astype(BF)
        k_aug[h] = k[...] * mine.astype(BF) + ones
        v_aug[h] = v[...] * mine.astype(BF) + ones
    dk_acc[...] = jnp.zeros_like(dk_acc)
    dv_acc[...] = jnp.zeros_like(dv_acc)

    def one_block(i, count):
        at = pl.ds(pl.multiple_of(i * QB, QB), QB)
        per = QB // (2 * tokens)
        pieces = []
        for c in range(per):
            spot = pl.ds(pl.multiple_of((i * per + c) * tokens, tokens), tokens)
            a, b = do_own[spot, :].astype(F32), do_oth[spot, :].astype(F32)
            flag = jnp.full(a.shape, core, jnp.int32)
            pieces += [jnp.where(flag == 0, a, b), jnp.where(flag == 0, b, a)]
        do = jnp.concatenate(pieces, 0)
        prod = do * o_nat[at, :].astype(F32)
        turned = []
        for h in (0, 1):
            mine, marks = head_masks(h)
            delta = jnp.sum(prod * mine, axis=1, keepdims=True)
            doa = add_marks(mine, marks, do, -delta)
            qa = q_aug[h, at, :]

            def one(j, dqt, diagonal):
                kat = pl.ds(pl.multiple_of(j * QB, QB), QB)
                s = nt(k_aug[h, kat, :], qa)
                if diagonal:
                    s = jnp.where(qcol >= krow, s, NEGATIVE)
                p = jnp.exp(s)
                ds = (p * nt(v_aug[h, kat, :], doa)).astype(BF)
                dv_acc[h, kat, :] += dot(p.astype(BF), doa)
                dk_acc[h, kat, :] += dot(ds, qa)
                return dqt + dot(kt[64 * h : 64 * h + 64, kat], ds)

            dqt = jnp.zeros((64, QB), F32)
            if count is not None:
                for j in range(count - 1):
                    dqt = one(j, dqt, False)
            else:
                dqt = lax.fori_loop(0, i, lambda j, c: one(j, c, False), dqt)
            turned.append(one(i, dqt, True))
        dq[at, :] = (jnp.concatenate(turned, 0).T * 0.125).astype(BF)

    if size <= 1024:
        for i in range(size // QB):
            one_block(i, i + 1)
    else:
        lax.fori_loop(0, size // QB, lambda i, c: (one_block(i, None), c)[1], 0)
    m0, m1 = head_masks(0)[0], head_masks(1)[0]
    dk[...] = (dk_acc[0] * m0 + dk_acc[1] * m1).astype(BF)
    dv[...] = (dv_acc[0] * m0 + dv_acc[1] * m1).astype(BF)


def cross_pair(ref, p):
    lane = lanes(128)
    piece = ref[:, 128 * p : 128 * p + 128]
    low = (lane < 64).astype(BF)
    high = (lane >= 64).astype(BF)
    return jnp.concatenate([piece * low, piece * high], 0)


def cross_kernel(
    meta, x, o_own, o_oth, info, w_out, g_cross, c_query, mk, mv, c_out, g_ffn,
    o1, y1, a2, cq, p2, o2, y2, a3,
):
    core = meta[0]
    half = o_own.shape[1]
    mine = pl.ds(pl.multiple_of(core * half, 128), half)
    other = pl.ds(pl.multiple_of((1 - core) * half, 128), half)
    o1[:, mine] = o_own[...]
    o1[:, other] = o_oth[...]
    first = x[...].astype(F32) + dot(o1[...], w_out[...])
    y1[...] = first
    n2 = (first * inv_rms(first) * g_cross[...]).astype(BF)
    a2[...] = n2
    query = dot(n2, c_query[...]).astype(BF)
    cq[...] = query
    patches = mk.shape[0]
    lane = lanes(2 * patches)
    low = lane < patches
    sent = info[0:1, 0:1].astype(F32) * 16.0 + info[0:1, 128:129].astype(F32)
    known = jnp.full((1, 1), meta[2], jnp.int32).astype(F32)
    same = jnp.full((1, 1), meta[0] - meta[4], jnp.int32) == 0
    count = jnp.where(same, known, sent)
    valid = jnp.where(low, lane, lane - patches).astype(F32) < count
    for p in range(H // 2):
        keys = cross_pair(mk, p)
        values = cross_pair(mv, p)
        s = nt(query[:, 128 * p : 128 * p + 128], keys) * 0.125
        s = jnp.where(valid, s, NEGATIVE)
        m0 = jnp.max(jnp.where(low, s, NEGATIVE), axis=1, keepdims=True)
        m1 = jnp.max(jnp.where(low, NEGATIVE, s), axis=1, keepdims=True)
        e = jnp.exp(s - jnp.where(low, m0, m1))
        l0 = jnp.sum(jnp.where(low, e, 0.0), axis=1, keepdims=True)
        l1 = jnp.sum(jnp.where(low, 0.0, e), axis=1, keepdims=True)
        w = e / jnp.where(low, l0, l1)
        p2[p] = w
        o2[:, 128 * p : 128 * p + 128] = dot(w.astype(BF), values).astype(BF)
    second = first + dot(o2[...], c_out[...])
    y2[...] = second
    a3[...] = (second * inv_rms(second) * g_ffn[...]).astype(BF)


def ffn_kernel(
    row_blocks, meta, a3, cot, y2, g_ffn, wg, wu, wd,
    out, dy2, dy2b, gain, send, keep, acc, err, a3t, cott, dw, gu_buf, wd_buf, sems,
):
    core = meta[0]
    i, r = pl.program_id(0), pl.program_id(1)
    rows = pl.ds(pl.multiple_of(r * ROWS, ROWS), ROWS)
    first, last = i == 0, i == pl.num_programs(0) - 1

    @pl.when(first)
    def _():
        a3t[:, rows] = a3[...].astype(F32).T.astype(BF)
        cott[:, rows] = cot[...].astype(F32).T.astype(BF)
        acc[rows, :] = y2[...]
        err[rows, :] = jnp.zeros((ROWS, err.shape[1]), F32)

    gate = dot(a3[...], wg[...])
    up = dot(a3[...], wu[...])
    square = gate * gate
    th = jnp.tanh(0.7978845608028654 * gate * (1.0 + 0.044715 * square))
    more = 0.5 * (1.0 + th)
    act = gate * more
    slope = more + 0.5 * gate * (1.0 - th * th) * (
        0.7978845608028654 * (1.0 + 3 * 0.044715 * square)
    )
    hidden = (act * up).astype(BF)
    dh = nt(cot[...], wd[...])
    d_gate = (dh * up * slope).astype(BF)
    d_up = (dh * act).astype(BF)
    acc[rows, :] += dot(hidden, wd[...])
    err[rows, :] += nt(d_gate, wg[...]) + nt(d_up, wu[...])
    terms = (dot(a3t[:, rows], d_gate), dot(a3t[:, rows], d_up), dot(cott[:, rows], hidden))
    if row_blocks > 1:
        for n, term in enumerate(terms):
            dw[n] = jnp.where(r == 0, 0.0, dw[n]) + term
        terms = (dw[0], dw[1], dw[2])

    slot = lax.rem(i, 2)
    side = i // 2

    def gu_copy(dst):
        return pltpu.make_async_copy(gu_buf.at[slot], dst.at[side, pl.ds(0, 2)], sems.at[0, slot])

    def wd_copy(n, dst):
        return pltpu.make_async_copy(
            wd_buf.at[slot, n], dst.at[:, 2, pl.ds(2 * i, 2)], sems.at[1 + n, slot]
        )

    def drain(at):
        pltpu.make_async_copy(gu_buf.at[at], keep.at[0, pl.ds(0, 2)], sems.at[0, at]).wait()
        for n, dst in enumerate((send, keep)):
            pltpu.make_async_copy(
                wd_buf.at[at, n], dst.at[:, 2, pl.ds(0, 2)], sems.at[1 + n, at]
            ).wait()

    def put():
        pl.when(i >= 2)(lambda: drain(slot))
        width = terms[0].shape[1]
        for n in (0, 1):
            gu_buf[slot, n] = terms[n].astype(BF).reshape(8, terms[n].shape[0] // 8, width)
        down = terms[2].astype(BF)
        per, part, wide = down.shape[0] // 4, down.shape[0] // 8, width // 2
        for b in range(4):
            kept = jnp.where(core == b % 2, 1, 0)
            for y in range(2):
                piece = down[b * per : (b + 1) * per, y * wide : (y + 1) * wide]
                packed = jnp.concatenate([piece[:part], piece[part:]], 1)
                wd_buf[slot, kept, b // 2, y] = packed
        pl.when(slot == core)(lambda: gu_copy(keep).start())
        pl.when(slot != core)(lambda: gu_copy(send).start())
        wd_copy(0, send).start()
        wd_copy(1, keep).start()

        @pl.when(last)
        def _():
            drain(1 - slot)
            drain(slot)

    if row_blocks > 1:
        pl.when(r == row_blocks - 1)(put)
    else:
        put()

    @pl.when(last)
    def _():
        out[...] = acc[rows, :].astype(BF)
        back, gsum = norm_back(err[rows, :], y2[...], g_ffn[...])
        total = cot[...].astype(F32) + back
        dy2[...] = total
        dy2b[...] = total.astype(BF)
        gain[...] = jnp.where(r == 0, 0.0, gain[...]) + gsum


def cross_back_kernel(
    charts, patches_each, meta, dy2, dy2b, c_out, p2, mk, mv, cq, y1, g_cross, c_query, w_out,
    c_key_hbm, c_value_hbm,
    dcq, dmk, dmv, dy1, dy1b, do_keep, do_send, memg, gain, mk_acc, mv_acc, mem_scr, c_key, c_value, sems,
):
    core = meta[0]
    r = pl.program_id(0)
    half = do_keep.shape[1]
    patches = mk.shape[0]
    lane = lanes(2 * patches)
    low = lane < patches
    left = (lanes(128) < 64).astype(F32)
    do2 = nt(dy2b[...], c_out[...]).astype(BF)
    fresh = r == 0
    copies = [
        pltpu.make_async_copy(c_key_hbm, c_key, sems.at[0]),
        pltpu.make_async_copy(c_value_hbm, c_value, sems.at[1]),
    ]

    @pl.when(fresh)
    def _():
        for copy in copies:
            copy.start()

    for p in range(H // 2):
        at = slice(128 * p, 128 * p + 128)
        keys = cross_pair(mk, p)
        values = cross_pair(mv, p)
        w = p2[p]
        dp = nt(do2[:, at], values)
        prod = w * dp
        r0 = jnp.sum(jnp.where(low, prod, 0.0), axis=1, keepdims=True)
        r1 = jnp.sum(jnp.where(low, 0.0, prod), axis=1, keepdims=True)
        ds = w * (dp - jnp.where(low, r0, r1))
        dcq[:, at] = (dot(ds.astype(BF), keys) * 0.125).astype(BF)
        gk = dot(ds.T.astype(BF), cq[:, at]) * 0.125
        gv = dot(w.T.astype(BF), do2[:, at])
        gk = gk[:patches] * left + gk[patches:] * (1.0 - left)
        gv = gv[:patches] * left + gv[patches:] * (1.0 - left)
        mk_acc[:, at] = jnp.where(fresh, 0.0, mk_acc[:, at]) + gk
        mv_acc[:, at] = jnp.where(fresh, 0.0, mv_acc[:, at]) + gv
    err = nt(dcq[...], c_query[...])
    back, gsum = norm_back(err, y1[...], g_cross[...])
    total = dy2[...] + back
    dy1[...] = total
    tb = total.astype(BF)
    dy1b[...] = tb
    gain[...] = jnp.where(fresh, 0.0, gain[...]) + gsum
    do_keep[...] = nt(tb, w_out[pl.ds(pl.multiple_of(core * half, half), half), :]).astype(BF)
    rows = tb.shape[0]
    do_send[pl.ds(pl.multiple_of(r * rows, rows), rows), :] = nt(
        tb, w_out[pl.ds(pl.multiple_of((1 - core) * half, half), half), :]
    ).astype(BF)

    @pl.when(r == pl.num_programs(0) - 1)
    def _():
        gk, gv = mk_acc[...].astype(BF), mv_acc[...].astype(BF)
        for copy in copies:
            copy.wait()
        dmk[...] = gk
        dmv[...] = gv
        mem_scr[...] = nt(gk, c_key[...]) + nt(gv, c_value[...])

        def gather(parity):
            return jnp.concatenate(
                [
                    mem_scr[pl.ds(pl.multiple_of((2 * a + parity) * patches_each, 8), patches_each), :]
                    for a in range(charts)
                ],
                0,
            )

        memg[...] = gather(core)
        away = gather(1 - core).astype(BF)
        extra = away.shape[0]
        base = do_send.shape[0] - 2 * extra
        do_send[base : base + extra, :] = away[:, :half]
        do_send[base + extra :, :] = away[:, half:]


def square_kernel(meta, o2, dy2b, a2, dcq, mem, dmk, dmv, o1, dy1b, send, keep):
    core = meta[0]
    half = keep.shape[2]
    mine = pl.ds(pl.multiple_of(core * half, 128), half)
    other = pl.ds(pl.multiple_of((1 - core) * half, 128), half)
    memt = mem[...].astype(F32).T.astype(BF)
    pairs = ((o2, dy2b), (a2, dcq), (None, dmk), (None, dmv), (o1, dy1b))
    for n, (left, right) in enumerate(pairs):
        turned = memt if left is None else left[...].astype(F32).T.astype(BF)
        send[n] = dot(turned, right[:, other]).astype(BF)
        keep[n] = dot(turned, right[:, mine]).astype(BF)


def leave_kernel(
    split, charts, tokens, meta, a1, dq, dk, dv, wq, wk, wv, column, g_cross, g_ffn, *outs,
):
    half = dq.shape[1]
    size = dq.shape[0]
    width = g_ffn.shape[1]
    core, parity = meta[0], meta[4]
    cols = pl.ds(pl.multiple_of(core * half, 128), half)
    e_keep, e_send = outs[0], outs[1]
    out, scr = (outs[4], outs[5]) if split else (outs[2], outs[3])
    third = width // 3

    def rows_of(n):
        at = pl.ds(pl.multiple_of(n * third, third), third)
        turned = a1[:, at].astype(F32).T.astype(BF)
        gain = jnp.zeros((third, 1), F32)
        for m, (right, weight) in enumerate(((dq, wq), (dk, wk), (dv, wv))):
            block = dot(turned, right[...])
            gain += jnp.sum(block * weight[at, cols].astype(F32), axis=1, keepdims=True)
            out[at, m * half : (m + 1) * half] = block.astype(BF)
        gain = gain / column[at, :]
        stack = jnp.concatenate(
            [g_cross[:, at], g_ffn[:, at], jnp.zeros((126, third), F32)], 0
        ).T
        out[at, 3 * half :] = (jnp.where(lanes(128) == 2, gain, stack)).astype(BF)

    lax.fori_loop(0, 3, lambda n, c: (rows_of(n), c)[1], 0)
    if split:
        send, keep = outs[2], outs[3]
        part = width // 8
        for n in range(4):
            keep[n] = out[pl.ds(pl.multiple_of((2 * n + parity) * part, part), part), :]
            send[n] = out[pl.ds(pl.multiple_of((2 * n + 1 - parity) * part, part), part), :]
    step = scr.shape[0]
    per = step // (2 * tokens)

    def one(first):
        at = pl.ds(pl.multiple_of(first * step, step), step)
        scr[...] = (
            nt(dq[at, :], wq[:, cols]) + nt(dk[at, :], wk[:, cols]) + nt(dv[at, :], wv[:, cols])
        )
        for c in range(per):
            spot = pl.ds(pl.multiple_of((first * per + c) * tokens, tokens), tokens)
            e_keep[spot, :] = scr[pl.ds(pl.multiple_of((2 * c + core) * tokens, tokens), tokens), :]
            e_send[spot, :] = scr[
                pl.ds(pl.multiple_of((2 * c + 1 - core) * tokens, tokens), tokens), :
            ].astype(BF)

    lax.fori_loop(0, size // step, lambda g, c: (one(g), c)[1], 0)


def mix_kernel(meta, keep, recv, send1, kept1, send2, kept2):
    side, parity = meta[3], meta[4]
    rows = keep.shape[3]
    low = rows // 2

    def gu(x, w, s):
        return (keep[x, w, s].astype(F32) + recv[x, w, s].astype(F32)).astype(BF)

    def wd(x, s, part):
        return (keep[x, 2, s, part, :].astype(F32) + recv[x, 2, s, part, :].astype(F32)).astype(BF)

    for s in range(8):
        for x, to in ((1 - side, send1), (side, kept1)):
            to[s, :rows, :] = gu(x, 0, s)
            to[s, rows:, :] = wd(x, s, slice(0, low))
    for n in range(4):
        for x in range(2):
            for y, to in ((1 - parity, send2), (parity, kept2)):
                to[x, n, :rows, :] = gu(x, 1, 2 * n + y)
                to[x, n, rows:, :] = wd(x, 2 * n + y, slice(low, rows))


def input_grad_kernel(e_keep, e_recv, x, gain, dy1, out):
    err = e_keep[...] + e_recv[...].astype(F32)
    back, _ = norm_back(err, x[...].astype(F32), gain[...])
    out[...] = (dy1[...] + back).astype(BF)


def total(parts):
    result = parts[0].astype(F32)
    for part in parts[1:]:
        result = result + part.reshape(result.shape).astype(F32)
    return result


def tie(value, *deps):
    return lax.optimization_barrier((value, deps))[0]


def turn_in_kernel(meta, base, recv, send, keep):
    v, z = meta[5], meta[6]
    send[z] = base[z, 1 - v]
    send[1 - z] = recv[1 - v]
    keep[z] = base[z, v]
    keep[1 - z] = recv[v]


def gather_kernel(meta, keep, recv, out):
    v = meta[5]
    for n in range(2):
        out[n, v] = keep[n]
        out[n, 1 - v] = recv[n]


def finish_kernel(tokens, got, first, few):
    for n in range(got.shape[0]):
        first[n] = got[n, :tokens, :].astype(F32)
        few[n] = got[n, tokens:, :].astype(F32)


def place_kernel(charts, meta, *refs):
    place = meta[1]
    out = refs[-1]
    for d in range(charts):
        out[lax.rem(place - d + charts, charts)] = refs[d][...].astype(out.dtype)


def local(
    nseq, inputs, memory, patch_count, cotangent, norm_self, w_query, w_key, w_value, w_out,
    norm_cross, c_query, c_key, c_value, c_out, norm_ffn, w_gate, w_up, w_down,
):
    charts, tokens, width = inputs.shape
    patches_each = memory.shape[1]
    size = charts * 2 * tokens
    own = charts * tokens
    patches = patches_each * nseq
    half = width // 2
    small = size <= 1024
    hidden = w_gate.shape[1]
    blocks = own // ROWS
    dp = lax.axis_index("dp")
    seq = lax.axis_index("seq")
    side, core = dp // 2, lax.rem(dp, 2)
    place, parity = seq // 2, lax.rem(seq, 2)

    def shift(d):
        return [
            ((2 * x + k) * nseq + 2 * a + b, (2 * x + b) * nseq + 2 * ((a + d) % charts) + k)
            for x in range(2)
            for k in range(2)
            for a in range(charts)
            for b in range(2)
        ]

    def dp_perm(rule):
        return [(2 * x + k, 2 * rule(x, k)[0] + rule(x, k)[1]) for x in range(2) for k in range(2)]

    swap_core = dp_perm(lambda x, k: (x, 1 - k))
    swap_side = dp_perm(lambda x, k: (1 - x, k))

    def across(value):
        return lax.ppermute(value, "dp", swap_core)

    def travel(value, d):
        return lax.ppermute(value, ("dp", "seq"), shift(d))

    def pick(value, d):
        return lax.dynamic_index_in_dim(value, lax.rem(place + d, charts), 0, keepdims=False)

    gain_self, gain_cross, gain_ffn = (g.reshape(1, width) for g in (norm_self, norm_cross, norm_ffn))
    count = lax.dynamic_index_in_dim(patch_count, place, 0, keepdims=False)
    meta = jnp.stack(
        [core, place, count, side, parity, lax.rem(place, 2), place // 2]
    ).astype(jnp.int32)

    trade = [
        ((2 * x + k) * nseq + 2 * a + b, (2 * x + b) * nseq + 2 * a + k)
        for x in range(2)
        for k in range(2)
        for a in range(charts)
        for b in range(2)
    ]
    flips = {
        name: [(s, s ^ (1 << bit)) for s in range(nseq)] for bit, name in enumerate("yvz")
    }
    low_bit, high_bit = lax.rem(place, 2), place // 2

    mine = jnp.stack(
        [
            travel(jnp.concatenate([pick(inputs, d), pick(memory, d)], 0), d)
            for d in range(charts)
        ]
    )
    theirs = across(mine)
    if small:
        cot_base = lax.ppermute(cotangent, ("dp", "seq"), trade)
        cot_base = cot_base.reshape(2, 2, tokens, width)
        cot_away = lax.dynamic_index_in_dim(cot_base, 1 - high_bit, 0, keepdims=False)
        cot_got = lax.ppermute(cot_away, "seq", flips["z"])
        theirs = tie(theirs, cot_away)
    else:
        cot_parts = [travel(pick(cotangent, d), d) for d in range(charts)]
    pairs = half // 128
    pair_spec = pl.BlockSpec((size, 128), lambda p, m: (0, p))
    own_spec = pl.BlockSpec((own, 128), lambda p, m: (0, p))
    aug_spec = pl.BlockSpec((2, size, 128), lambda p, m: (p, 0, 0))
    far = pltpu.HBM if small else sds
    x_own, a1, k, v, mem, mk, mv, o_keep, o_send, o_nat, q_aug = pl.pallas_call(
        functools.partial(enter_kernel, small, charts, tokens, patches_each),
        compiler_params=room(small, 24),
        out_shape=(
            sds((own, width), BF), far((size, width), BF), far((size, half), BF),
            far((size, half), BF), sds((patches, width), BF), sds((patches, width), BF),
            sds((patches, width), BF), sds((own, half), BF), sds((own + 16, half), BF),
            far((size, half), BF), far((2 * pairs, size, 128), BF),
        ),
        in_specs=[SM] + [VM] * 3 + [pl.BlockSpec(memory_space=pltpu.HBM)] * 5,
        out_specs=([VM] + [HB] * 3 + [VM] * 6 + [HB]) if small else [VM] * 11,
        scratch_shapes=[
            pltpu.VMEM((patches, width), F32), pltpu.VMEM((size, half), BF),
            pltpu.VMEM((width, half), BF), pltpu.VMEM((width, half), BF),
            pltpu.VMEM((width, half), BF), pltpu.VMEM((width, width), BF),
            pltpu.VMEM((width, width), BF), pltpu.SemaphoreType.DMA((5,)),
        ]
        + (
            [
                pltpu.VMEM((size, width), BF), pltpu.VMEM((size, half), BF),
                pltpu.VMEM((size, half), BF), pltpu.VMEM((2 * pairs, size, 128), BF),
                pltpu.SemaphoreType.DMA((3,)), pltpu.SemaphoreType.DMA((pairs,)),
            ]
            if small
            else []
        ),
        cost_estimate=cost(2 * size * width * 3 * half, mine, theirs, w_query, w_key, w_value),
    )(
        meta, mine, theirs, gain_self,
        *(
            pltpu.with_memory_space_constraint(w, pltpu.HBM)
            for w in (w_query, w_key, w_value, c_key, c_value)
        ),
    )
    if small:
        part = sds((2, tokens, width), BF)
        cot_send, cot_keep = pl.pallas_call(
            turn_in_kernel,
            compiler_params=room(small, 6),
            out_shape=(part, part),
            in_specs=[SM, VM, VM],
            out_specs=[VM] * 2,
        )(meta, cot_base, cot_got)
        cot_got = lax.ppermute(cot_send, "seq", flips["v"])
        o_recv = tie(across(o_send), cot_send)
    else:
        o_recv = across(o_send)

    each = ROWS if small else QB
    row_spec = pl.BlockSpec((each, width), lambda r: (r, 0))
    half_spec = pl.BlockSpec((each, half), lambda r: (r, 0))
    p2_spec = pl.BlockSpec((H // 2, each, 2 * patches), lambda r: (0, r, 0))

    def fixed(shape, spaces=1):
        if spaces == 1:
            return pl.BlockSpec(shape, lambda r: (0,) * len(shape))
        return pl.BlockSpec(shape, lambda i, r: (0,) * len(shape))

    square = fixed((width, width))
    one_row = fixed((1, width))
    patch_spec = fixed((patches, width))
    rows_f = sds((own, width), F32)
    rows_b = sds((own, width), BF)
    o1, y1, a2, cq, p2, o2, y2, a3 = pl.pallas_call(
        cross_kernel,
        compiler_params=room(small, 16),
        out_shape=(
            rows_b, rows_f, rows_b, rows_b, sds((H // 2, own, 2 * patches), F32), rows_b, rows_f,
            rows_b,
        ),
        grid=(own // each,),
        in_specs=[
            SM, row_spec, half_spec, half_spec, pl.BlockSpec((16, half), lambda r: (own // 16, 0)),
            square, one_row, square, patch_spec, patch_spec, square, one_row,
        ],
        out_specs=[row_spec] * 4 + [p2_spec] + [row_spec] * 3,
        cost_estimate=cost(6 * own * width * width, w_out, c_query, c_out, rows_f, rows_f),
    )(meta, x_own, o_keep, o_recv, o_recv, w_out, gain_cross, c_query, mk, mv, c_out, gain_ffn)

    def placed(parts, dtype):
        return pl.pallas_call(
            functools.partial(place_kernel, charts),
            compiler_params=room(small, 6),
            out_shape=sds((charts,) + parts[0].shape, dtype),
            in_specs=[SM] + [VM] * charts,
            out_specs=VM,
        )(meta, *parts)

    if small:
        cot = pl.pallas_call(
            gather_kernel,
            compiler_params=room(small, 6),
            out_shape=sds((2, 2, tokens, width), BF),
            in_specs=[SM, VM, VM],
            out_specs=VM,
        )(meta, cot_keep, tie(cot_got, y2)).reshape(own, width)
    else:
        cot = placed(cot_parts, BF).reshape(own, width)
    wide = hidden // 4
    last = 3
    f_pack = sds((2, 3, 8, width // 8, wide), BF)
    anywhere = pl.BlockSpec(memory_space=pl.ANY)
    frow = pl.BlockSpec((ROWS, width), lambda i, r: (r, 0))
    lrow = pl.BlockSpec((ROWS, width), lambda i, r: (r * (i // last), 0))
    out_b, dy2, dy2b, ffn_gain, f_send, f_keep = pl.pallas_call(
        functools.partial(ffn_kernel, blocks),
        compiler_params=room(small, 30),
        out_shape=(rows_b, rows_f, rows_b, sds((1, width), F32), f_pack, f_pack),
        grid=(4, blocks),
        in_specs=[
            SM, frow, frow, frow, fixed((1, width), 2),
            pl.BlockSpec((width, wide), lambda i, r: (0, i)),
            pl.BlockSpec((width, wide), lambda i, r: (0, i)),
            pl.BlockSpec((wide, width), lambda i, r: (i, 0)),
        ],
        out_specs=[lrow, lrow, lrow, fixed((1, width), 2), anywhere, anywhere],
        scratch_shapes=[
            pltpu.VMEM((own, width), F32), pltpu.VMEM((own, width), F32),
            pltpu.VMEM((width, own), BF), pltpu.VMEM((width, own), BF),
            pltpu.VMEM((3, width, wide) if blocks > 1 else (3, 8, 128), F32),
            pltpu.VMEM((2, 2, 8, width // 8, wide), BF),
            pltpu.VMEM((2, 2, 2, 2, width // 8, wide), BF), pltpu.SemaphoreType.DMA((3, 2)),
        ],
        cost_estimate=cost(18 * own * width * hidden, w_gate, w_up, w_down, rows_f, rows_f),
    )(meta, a3, cot, y2, gain_ffn, w_gate, w_up, w_down)
    f_recv = across(f_send)

    def back_first(rows):
        return lax.ppermute(rows, ("dp", "seq"), trade)

    def back_second(rows):
        base = rows.reshape((2, 2) + rows.shape[1:])
        away = lax.dynamic_index_in_dim(base, 1 - high_bit, 0, keepdims=False)
        return base, lax.ppermute(away, "seq", flips["z"])

    def back_turn(base, got):
        return pl.pallas_call(
            turn_in_kernel,
            compiler_params=room(small, 6),
            out_shape=(sds(got.shape, BF), sds(got.shape, BF)),
            in_specs=[SM, VM, VM],
            out_specs=[VM] * 2,
        )(meta, base, got)

    def gathered(keep, got):
        return pl.pallas_call(
            gather_kernel,
            compiler_params=room(small, 6),
            out_shape=sds((2, 2) + got.shape[1:], BF),
            in_specs=[SM, VM, VM],
            out_specs=VM,
        )(meta, keep, got).reshape((charts,) + got.shape[1:])

    def back_last(got):
        return pl.pallas_call(
            functools.partial(finish_kernel, tokens),
            compiler_params=room(small, 8),
            out_shape=(
                sds((charts, tokens, width), F32), sds((charts, patches_each, width), F32),
            ),
            in_specs=[VM],
            out_specs=[VM] * 2,
        )(got)

    def halve(which, keep, recv, outer):
        parts = (keep if isinstance(keep, list) else [keep]) + [recv]
        size_now, wide_now = parts[0].size, parts[0].shape[-1]
        shape = (outer, 2, size_now // (outer * 2 * wide_now), wide_now)
        parts = [p.reshape(shape) for p in parts]
        i = meta[which]
        sends = [lax.dynamic_index_in_dim(p, 1 - i, 1, keepdims=False) for p in parts]
        kept = [lax.dynamic_index_in_dim(p, i, 1, keepdims=False) for p in parts]
        return total(sends).astype(BF), kept

    def over(name, value):
        if name == "x":
            return lax.ppermute(value, "dp", swap_side)
        return lax.ppermute(value, "seq", flips[name])

    out_rows = out_b.reshape(charts, tokens, width)
    if small:
        out_base, out_got = back_second(out_rows)
    else:
        out_parts = [travel(pick(out_rows, d), d) for d in range(charts)]
    dcq, dmk, dmv, dy1, dy1b, do_keep, do_send, memg, cross_gain = pl.pallas_call(
        functools.partial(cross_back_kernel, charts, patches_each),
        compiler_params=room(small, 18),
        out_shape=(
            rows_b, sds((patches, width), BF), sds((patches, width), BF), rows_f, rows_b,
            sds((own, half), BF), sds((own + patches, half), BF),
            sds((patches // 2, width), F32), sds((1, width), F32),
        ),
        grid=(own // each,),
        in_specs=[
            SM, row_spec, row_spec, square, p2_spec, patch_spec, patch_spec, row_spec, row_spec,
            one_row, square, square, HB, HB,
        ],
        out_specs=[
            row_spec, patch_spec, patch_spec, row_spec, row_spec, half_spec,
            fixed((own + patches, half)), fixed((patches // 2, width)), one_row,
        ],
        scratch_shapes=[pltpu.VMEM((patches, width), F32)] * 3
        + [pltpu.VMEM((width, width), BF)] * 2
        + [pltpu.SemaphoreType.DMA((2,))],
        cost_estimate=cost(6 * own * width * width, w_out, c_query, c_out, rows_f, rows_f),
    )(meta, dy2, dy2b, c_out, p2, mk, mv, cq, y1, gain_cross, c_query, w_out, c_key, c_value)
    do_recv = across(do_send)

    if small:
        f1 = sds((8, 3 * width // 16, wide), BF)
        f2 = sds((2, 4, 3 * width // 16, wide), BF)
        f1_send, f1_keep, f2_send, f2_keep = pl.pallas_call(
            mix_kernel,
            compiler_params=room(small, 16),
            out_shape=(f1, f1, f2, f2),
            in_specs=[SM] + [VM] * 2,
            out_specs=[VM] * 4,
        )(meta, f_keep, f_recv)
        f1_recv, f2_recv = over("x", f1_send), over("y", f2_send)
        dcq = tie(dcq, f1_send)
    s_send, s_keep = pl.pallas_call(
        square_kernel,
        compiler_params=room(small, 16),
        out_shape=(sds((5, width, half), BF), sds((5, width, half), BF)),
        in_specs=[SM] + [VM] * 9,
        out_specs=[VM] * 2,
        cost_estimate=cost(6 * own * width * width, o1, o2, a2, dcq, dy2b, dy1b),
    )(meta, o2, dy2b, a2, dcq, mem, dmk, dmv, o1, dy1b)
    s_recv = across(s_send)

    few = patches // 2
    memg_recv = jnp.concatenate([do_recv[own : own + few], do_recv[own + few :]], 1)
    memg_own = (memg + memg_recv.astype(F32)).astype(BF).reshape(charts, patches_each, width)
    if small:
        s_send, s_keep = halve(5, s_keep, s_recv, 10)
        s_recv = over("v", s_send)
        do_recv = tie(do_recv, s_send)

    dq, dk, dv = pl.pallas_call(
        functools.partial(attend_back_kernel, tokens),
        compiler_params=room(small, 14),
        out_shape=(sds((size, half), BF),) * 3,
        grid_spec=pltpu.PrefetchScalarGridSpec(
            num_scalar_prefetch=1,
            grid=(pairs,),
            in_specs=[aug_spec, pair_spec, pair_spec, pair_spec, own_spec, own_spec],
            out_specs=[pair_spec] * 3,
            scratch_shapes=[
                pltpu.VMEM((2, size, 128), BF), pltpu.VMEM((2, size, 128), BF),
                pltpu.VMEM((128, size), BF),
                pltpu.VMEM((2, size, 128), F32), pltpu.VMEM((2, size, 128), F32),
            ],
        ),
        cost_estimate=cost(10 * size * size * half, k, v, q_aug),
    )(meta, q_aug, k, v, o_nat, do_keep, do_recv)

    if small:
        dq = tie(dq, f1_recv, f2_recv, out_got)
    t_whole = sds((width, 3 * half + 128), BF)
    t_piece = sds((4, width // 8, 3 * half + 128), BF)
    gone = pl.pallas_call(
        functools.partial(leave_kernel, small, charts, tokens),
        compiler_params=room(small, 14),
        out_shape=(rows_f, rows_b) + ((t_piece, t_piece) if small else (t_whole,)),
        in_specs=[SM] + [VM] * 10,
        out_specs=[VM] * (4 if small else 3),
        scratch_shapes=([pltpu.VMEM((width, 3 * half + 128), BF)] if small else [])
        + [pltpu.VMEM((256, width), F32)],
    )(
        meta, a1, dq, dk, dv, w_query, w_key, w_value, norm_self.reshape(width, 1), cross_gain,
        ffn_gain,
    )
    e_keep, e_send = gone[:2]
    e_recv = across(e_send)
    if small:
        t_send, t_keep = gone[2:]
        t_recv = over("y", t_send)
        e_recv = tie(e_recv, t_send)
    else:
        t_out = gone[2]

    in_grad = pl.pallas_call(
        input_grad_kernel,
        compiler_params=room(small, 8),
        out_shape=rows_b,
        in_specs=[VM] * 5,
        out_specs=VM,
        cost_estimate=cost(20 * own * width, e_keep, e_send, x_own, dy1),
    )(e_keep, e_recv, x_own, gain_self, dy1)
    in_rows = jnp.concatenate([in_grad.reshape(charts, tokens, width), memg_own], 1)
    if small:
        in_base, in_got = back_second(in_rows)
        out_send, out_keep = back_turn(out_base, tie(out_got, in_base))
        out_got = lax.ppermute(out_send, "seq", flips["v"])
        f2_send, f2_keep = halve(3, f2_keep, tie(f2_recv, out_send), 1)
        f2_recv = over("x", f2_send)
        s_send, s_keep = halve(3, s_keep, tie(s_recv, f2_send), 20)
        s_recv = over("x", s_send)
        t_send, t_keep = halve(3, t_keep, tie(t_recv, s_send), 4)
        t_recv = over("x", t_send)
        f2_send, f2_keep = halve(5, f2_keep, tie(f2_recv, t_send), 2)
        f2_recv = over("v", f2_send)
        f1_send, f1_keep = halve(4, f1_keep, tie(f1_recv, f2_send), 4)
        f1_recv = over("y", f1_send)
        out_rows = gathered(out_keep, tie(out_got, f1_send))
        out_mid = out_rows
        out_rows = back_first(out_rows)
        in_send, in_keep = back_turn(in_base, tie(in_got, out_mid))
        in_got = lax.ppermute(in_send, "seq", flips["v"])
        s_send, s_keep = halve(4, s_keep, tie(s_recv, in_send, f2_recv), 10)
        s_recv = over("y", s_send)
        t_send, t_keep = halve(5, t_keep, tie(t_recv, s_send), 2)
        t_recv = over("v", t_send)
        f1_send, f1_keep = halve(5, f1_keep, tie(f1_recv, t_send), 2)
        f1_recv = over("v", f1_send)
        t_send, t_keep = halve(6, t_keep, tie(t_recv, f1_send, s_recv), 1)
        t_recv = over("z", t_send)
        s_send, s_keep = halve(6, s_keep, tie(s_recv, t_send), 5)
        s_recv = over("z", s_send)
        in_rows = gathered(in_keep, tie(in_got, s_send))
        in_mid = in_rows
        in_rows = back_first(in_rows)
        f2_send, f2_keep = halve(6, f2_keep, tie(f2_recv, in_mid), 1)
        f2_recv = over("z", f2_send)
        f1_send, f1_keep = halve(6, f1_keep, tie(f1_recv, f2_send), 1)
        f1_recv = over("z", f1_send)
    else:
        in_parts = [travel(pick(in_rows, d), d) for d in range(charts)]

    if small:
        t_part = total(t_keep + [t_recv]).reshape(width // 16, 3 * half + 128)
        t_zero = jnp.zeros_like(t_part)
        t_sum = jnp.concatenate(
            [jnp.where(side == 0, t_part, t_zero), jnp.where(side == 0, t_zero, t_part)], 0
        )
        s_part = total(s_keep + [s_recv])
        s_zero = jnp.zeros_like(s_part)
        s_sum = jnp.concatenate(
            [jnp.where(side == 0, s_part, s_zero), jnp.where(side == 0, s_zero, s_part)], 1
        )
    else:

        def over_seq(value, axis):
            return lax.psum_scatter(
                value.astype(BF), "seq", scatter_dimension=axis, tiled=True
            ).astype(F32)

        def over_side(parts):
            sends = [lax.dynamic_index_in_dim(p, 1 - side, 0, keepdims=False) for p in parts]
            kept = [lax.dynamic_index_in_dim(p, side, 0, keepdims=False) for p in parts]
            return total(kept + [lax.ppermute(total(sends).astype(BF), "dp", swap_side)])

        f_all = over_side([f_keep, f_recv])
        g_two = over_seq(f_all[:2].reshape(2, width, wide), 1)
        g_gate, g_up = g_two[0], g_two[1]
        down = f_all[2].reshape(8, width // 8, 2, wide // 2)
        g_down = over_seq(down.transpose(0, 3, 2, 1).reshape(hidden, width // 4), 0)
        s_sum = over_seq(total([s_keep, s_recv]), 1)
        t_sum = over_seq(t_out, 0)

    rows = t_sum.shape[0]
    quarter = half // 2
    t_sum = t_sum.astype(BF)
    squares = jnp.concatenate(
        [t_sum[:, : 3 * half].reshape(rows, 3, half).transpose(1, 0, 2), s_sum.astype(BF)], 0
    ).reshape(8, rows, 2, quarter)
    gains = t_sum[:, 3 * half :]
    padded = jnp.pad(gains, ((0, 0), (0, quarter - 128)))[None]

    def deliver(block, rule):
        part = lax.dynamic_index_in_dim(squares, block, 2, keepdims=False)
        return lax.ppermute(jnp.concatenate([part, padded], 0), "dp", dp_perm(rule)).astype(F32)

    done = deliver(side, lambda x, k: (k, x)) + deliver(1 - side, lambda x, k: (k, 1 - x))
    if small:
        f1_recv, f2_recv = tie((f1_recv, f2_recv), done)
        f1_sum = total(f1_keep + [f1_recv]).reshape(3 * width // 16, wide)
        f2_sum = total(f2_keep + [f2_recv]).reshape(3 * width // 16, wide)
        g_gate, g_up = f1_sum[: width // 8], f2_sum[: width // 8]
        g_down = jnp.concatenate([f1_sum[width // 8 :], f2_sum[width // 8 :]], 0)
        g_down = g_down.reshape(width // 8, 2, wide // 2).transpose(2, 1, 0)
        g_down = g_down.reshape(wide // 2, width // 4)
    rest = lax.ppermute(gains, "dp", dp_perm(lambda x, k: (1 - k, x))).astype(F32) + lax.ppermute(
        gains, "dp", dp_perm(lambda x, k: (1 - k, 1 - x))
    ).astype(F32)
    gain_sum = done[8, :, :128] + rest

    if small:
        in_all, few_all = back_last(in_rows)
        out_all = out_rows.astype(F32)
    else:
        out_all, in_all = placed(out_parts, F32), placed(in_parts, F32)
        in_all, few_all = in_all[:, :tokens], in_all[:, tokens:]
    return (
        out_all,
        in_all,
        few_all,
        gain_sum[:, 2],
        done[0],
        done[1],
        done[2],
        done[7],
        gain_sum[:, 0],
        done[4],
        done[5],
        done[6],
        done[3],
        gain_sum[:, 1],
        g_gate,
        g_up,
        g_down,
    )


def solution(mesh):
    tok = P("dp", "seq", None)
    cut = P("seq", "dp")
    in_specs = (tok, tok, P("dp"), tok) + (P(),) * 14
    out_specs = (tok, tok, tok, P("seq"), cut, cut, cut, cut, P("seq"), cut, cut, cut, cut)
    out_specs += (P("seq"), cut, cut, cut)
    return jax.shard_map(
        functools.partial(local, mesh.shape["seq"]),
        mesh=mesh,
        in_specs=in_specs,
        out_specs=out_specs,
        check_vma=False,
    )
```

```python
import functools

import jax
import jax.numpy as jnp
from jax import lax
from jax.experimental import pallas as pl
from jax.experimental.pallas import tpu as pltpu
from jax.sharding import PartitionSpec as P

H = 12
EPSILON = 1e-06
NEGATIVE = -1e30
F32 = jnp.float32
BF = jnp.bfloat16
VM = pl.BlockSpec(memory_space=pltpu.VMEM)
SM = pl.BlockSpec(memory_space=pltpu.SMEM)
HB = pl.BlockSpec(memory_space=pltpu.HBM)
ROWS = 512
QB = 256


def dot(a, b):
    return lax.dot_general(a, b, (((1,), (0,)), ((), ())), preferred_element_type=F32)


def nt(a, b):
    return lax.dot_general(a, b, (((1,), (1,)), ((), ())), preferred_element_type=F32)


def lanes(width):
    return lax.broadcasted_iota(jnp.int32, (1, width), 1)


def inv_rms(v):
    return lax.rsqrt(jnp.mean(v * v, axis=-1, keepdims=True) + EPSILON)


def norm_back(e, v, gain):
    r = inv_rms(v)
    u = v * r
    eg = e * gain
    grad_v = (eg - u * jnp.mean(eg * u, axis=-1, keepdims=True)) * r
    return grad_v, jnp.sum(e * u, axis=0, keepdims=True)


def cost(flops, *arrays):
    total = sum(a.size * a.dtype.itemsize for a in arrays)
    return pl.CostEstimate(flops=int(flops), bytes_accessed=int(total), transcendentals=0)


def room(small, mib):
    return pltpu.CompilerParams(vmem_limit_bytes=mib << 20) if small else None


def sds(shape, dtype):
    return jax.ShapeDtypeStruct(shape, dtype)


def split3(value):
    hi = value.astype(BF).astype(F32)
    mid = (value - hi).astype(BF).astype(F32)
    lo = (value - hi - mid).astype(BF).astype(F32)
    return hi, mid, lo


def head_masks(h):
    lane = lanes(128)
    mine = ((lane < 64) if h == 0 else (lane >= 64)).astype(F32)
    base = 64 if h == 0 else 0
    marks = [(lane == base + i).astype(F32) for i in range(3)]
    return mine, marks


def add_marks(mine, marks, body, extra):
    hi, mid, lo = split3(extra)
    return (body * mine + hi * marks[0] + mid * marks[1] + lo * marks[2]).astype(BF)


def enter_kernel(
    staged, charts, tokens, patches, meta, own, oth, gain, wq_hbm, wk_hbm, wv_hbm, ck_hbm, cv_hbm,
    x_own, a1_out, k_out, v_out, mem, mk, mv, o_keep, o_send, o_nat, q_aug_out,
    mem_scr, q, wq, wk, wv, ck, cv, sems, *stage,
):
    if staged:
        a1, k, v, q_aug, out_sems, pair_sems = stage
    else:
        a1, k, v, q_aug = a1_out, k_out, v_out, q_aug_out
    core, place = meta[0], meta[1]
    half = q.shape[1]
    width = a1.shape[1]
    size = q.shape[0]
    group = max(1, min(charts, ROWS // tokens))
    cols = pl.ds(pl.multiple_of(core * half, 128), half)
    copies = [
        pltpu.make_async_copy(src.at[:, cols], dst, sems.at[n])
        for n, (src, dst) in enumerate(((wq_hbm, wq), (wk_hbm, wk), (wv_hbm, wv)))
    ] + [
        pltpu.make_async_copy(src, dst, sems.at[3 + n])
        for n, (src, dst) in enumerate(((ck_hbm, ck), (cv_hbm, cv)))
    ]
    for copy in copies:
        copy.start()

    def one(ref, parity, first, fresh):
        x = ref[pl.ds(first, group), :tokens, :].reshape(group * tokens, width)
        xf = x.astype(F32)
        a = (xf * inv_rms(xf) * gain[...]).astype(BF)
        if fresh:
            for copy in copies[:3]:
                copy.wait()
        qq = (dot(a, wq[...]) * 0.125).astype(BF)
        kk = dot(a, wk[...]).astype(BF)
        vv = dot(a, wv[...]).astype(BF)
        for i in range(group):
            chunk = lax.rem(place - (first + i) + charts, charts)
            part = slice(i * tokens, (i + 1) * tokens)
            at = pl.ds(pl.multiple_of((2 * chunk + parity) * tokens, tokens), tokens)
            a1[at, :] = a[part]
            q[at, :] = qq[part]
            k[at, :] = kk[part]
            v[at, :] = vv[part]
            few = ref[first + i, tokens:, :].astype(F32)
            spot = pl.ds(pl.multiple_of((2 * chunk + parity) * patches, patches), patches)
            mem_scr[spot, :] = few
            if ref is own:
                x_own[pl.ds(pl.multiple_of(chunk * tokens, tokens), tokens), :] = x[part]

    for ref, parity in ((own, core), (oth, 1 - core)):
        if charts == group:
            one(ref, parity, 0, ref is own)
        else:
            if ref is own:
                for copy in copies[:3]:
                    copy.wait()
            lax.fori_loop(
                0, charts // group,
                lambda g, c, r=ref, p=parity: (one(r, p, g * group, False), c)[1], 0,
            )
    whole = mem_scr[...].astype(BF)
    mem[...] = whole
    for copy in copies[3:]:
        copy.wait()
    mk[...] = dot(whole, ck[...]).astype(BF)
    mv[...] = dot(whole, cv[...]).astype(BF)
    leaving = [
        pltpu.make_async_copy(src, dst, out_sems.at[n])
        for n, (src, dst) in enumerate(((a1, a1_out), (k, k_out), (v, v_out)))
        if staged
    ]
    for copy in leaving:
        copy.start()
    row = lax.broadcasted_iota(jnp.int32, (QB, QB), 0)
    col = lax.broadcasted_iota(jnp.int32, (QB, QB), 1)

    def pair_copy(n):
        at = pl.ds(2 * n, 2)
        return pltpu.make_async_copy(q_aug.at[at], q_aug_out.at[at], pair_sems.at[n])

    def pair(n):
        wide = pl.ds(pl.multiple_of(n * 128, 128), 128)

        def one_block(i, count):
            at = pl.ds(i * QB, QB) if count is not None else pl.ds(pl.multiple_of(i * QB, QB), QB)
            qp = q[at, wide]
            outs = []
            for h in (0, 1):
                mine, marks = head_masks(h)
                mb = mine.astype(BF)
                rest = (1.0 - mine).astype(BF)
                qh = qp * mb

                def scores(j):
                    return nt(qh, k[pl.ds(pl.multiple_of(j * QB, QB), QB), wide])

                def weigh(e, j):
                    vh = v[pl.ds(pl.multiple_of(j * QB, QB), QB), wide] * mb + rest
                    return dot(e.astype(BF), vh)

                diag = jnp.where(row >= col, scores(i), NEGATIVE)
                if count is not None:
                    parts = [scores(j) for j in range(count - 1)] + [diag]
                    top = parts[0]
                    for s in parts[1:]:
                        top = jnp.maximum(top, s)
                    top = jnp.max(top, axis=1, keepdims=True)
                    acc = weigh(jnp.exp(parts[0] - top), 0)
                    for j, s in enumerate(parts[1:]):
                        acc = acc + weigh(jnp.exp(s - top), j + 1)
                else:
                    top = jnp.max(diag, axis=1, keepdims=True)
                    acc = weigh(jnp.exp(diag - top), i)

                    def step(j, state):
                        top, acc = state
                        s = scores(j)
                        new = jnp.maximum(top, jnp.max(s, axis=1, keepdims=True))
                        return new, acc * jnp.exp(top - new) + weigh(jnp.exp(s - new), j)

                    top, acc = lax.fori_loop(0, i, step, (top, acc))
                total = pltpu.roll(acc, 64, 1)
                outs.append(acc / (total * mine + (1.0 - mine)) * mine)
                lse = top + jnp.log(acc * (1.0 - mine) + mine)
                q_aug[2 * n + h, at, :] = add_marks(mine, marks, qp.astype(F32), -lse)
            o = (outs[0] + outs[1]).astype(BF)
            o_nat[at, wide] = o
            per = QB // (2 * tokens)
            for c in range(per):
                even = o[2 * c * tokens : (2 * c + 1) * tokens]
                odd = o[(2 * c + 1) * tokens : (2 * c + 2) * tokens]
                spot = pl.ds(pl.multiple_of((i * per + c) * tokens, tokens), tokens)
                flag = jnp.full(even.shape, core, jnp.int32).astype(F32)
                ef, of = even.astype(F32), odd.astype(F32)
                o_keep[spot, wide] = jnp.where(flag == 0, ef, of).astype(BF)
                o_send[spot, wide] = jnp.where(flag == 0, of, ef).astype(BF)

        if size <= 1024:
            for i in range(size // QB):
                one_block(i, i + 1)
        else:
            lax.fori_loop(0, size // QB, lambda i, c: (one_block(i, None), c)[1], 0)

    def pair_and_copy(n, carry):
        pair(n)
        if staged:
            pair_copy(n).start()
        return carry

    lax.fori_loop(0, half // 128, pair_and_copy, 0)
    info = jnp.full((16, 128), meta[2], jnp.int32)
    o_send[size // 2 :, :128] = (info // 16).astype(F32).astype(BF)
    o_send[size // 2 :, 128:256] = lax.rem(info, 16).astype(F32).astype(BF)
    o_send[size // 2 :, 256:] = jnp.zeros((16, half - 256), BF)
    for copy in leaving:
        copy.wait()
    for n in range(half // 128 if staged else 0):
        pair_copy(n).wait()


def attend_back_kernel(
    tokens, meta, q_aug, k, v, o_nat, do_own, do_oth, dq, dk, dv, k_aug, v_aug, kt, dk_acc, dv_acc
):
    core = meta[0]
    size = k.shape[0]
    krow = lax.broadcasted_iota(jnp.int32, (QB, QB), 0)
    qcol = lax.broadcasted_iota(jnp.int32, (QB, QB), 1)
    kt[...] = k[...].astype(F32).T.astype(BF)
    for h in (0, 1):
        mine, marks = head_masks(h)
        ones = (marks[0] + marks[1] + marks[2]).astype(BF)
        k_aug[h] = k[...] * mine.astype(BF) + ones
        v_aug[h] = v[...] * mine.astype(BF) + ones
    dk_acc[...] = jnp.zeros_like(dk_acc)
    dv_acc[...] = jnp.zeros_like(dv_acc)

    def one_block(i, count):
        at = pl.ds(pl.multiple_of(i * QB, QB), QB)
        per = QB // (2 * tokens)
        pieces = []
        for c in range(per):
            spot = pl.ds(pl.multiple_of((i * per + c) * tokens, tokens), tokens)
            a, b = do_own[spot, :].astype(F32), do_oth[spot, :].astype(F32)
            flag = jnp.full(a.shape, core, jnp.int32)
            pieces += [jnp.where(flag == 0, a, b), jnp.where(flag == 0, b, a)]
        do = jnp.concatenate(pieces, 0)
        prod = do * o_nat[at, :].astype(F32)
        turned = []
        for h in (0, 1):
            mine, marks = head_masks(h)
            delta = jnp.sum(prod * mine, axis=1, keepdims=True)
            doa = add_marks(mine, marks, do, -delta)
            qa = q_aug[h, at, :]

            def one(j, dqt, diagonal):
                kat = pl.ds(pl.multiple_of(j * QB, QB), QB)
                s = nt(k_aug[h, kat, :], qa)
                if diagonal:
                    s = jnp.where(qcol >= krow, s, NEGATIVE)
                p = jnp.exp(s)
                ds = (p * nt(v_aug[h, kat, :], doa)).astype(BF)
                dv_acc[h, kat, :] += dot(p.astype(BF), doa)
                dk_acc[h, kat, :] += dot(ds, qa)
                return dqt + dot(kt[64 * h : 64 * h + 64, kat], ds)

            dqt = jnp.zeros((64, QB), F32)
            if count is not None:
                for j in range(count - 1):
                    dqt = one(j, dqt, False)
            else:
                dqt = lax.fori_loop(0, i, lambda j, c: one(j, c, False), dqt)
            turned.append(one(i, dqt, True))
        dq[at, :] = (jnp.concatenate(turned, 0).T * 0.125).astype(BF)

    if size <= 1024:
        for i in range(size // QB):
            one_block(i, i + 1)
    else:
        lax.fori_loop(0, size // QB, lambda i, c: (one_block(i, None), c)[1], 0)
    m0, m1 = head_masks(0)[0], head_masks(1)[0]
    dk[...] = (dk_acc[0] * m0 + dk_acc[1] * m1).astype(BF)
    dv[...] = (dv_acc[0] * m0 + dv_acc[1] * m1).astype(BF)


def cross_pair(ref, p):
    lane = lanes(128)
    piece = ref[:, 128 * p : 128 * p + 128]
    low = (lane < 64).astype(BF)
    high = (lane >= 64).astype(BF)
    return jnp.concatenate([piece * low, piece * high], 0)


def cross_kernel(
    meta, x, o_own, o_oth, info, w_out, g_cross, c_query, mk, mv, c_out, g_ffn,
    o1, y1, a2, cq, p2, o2, y2, a3,
):
    core = meta[0]
    half = o_own.shape[1]
    mine = pl.ds(pl.multiple_of(core * half, 128), half)
    other = pl.ds(pl.multiple_of((1 - core) * half, 128), half)
    o1[:, mine] = o_own[...]
    o1[:, other] = o_oth[...]
    first = x[...].astype(F32) + dot(o1[...], w_out[...])
    y1[...] = first
    n2 = (first * inv_rms(first) * g_cross[...]).astype(BF)
    a2[...] = n2
    query = dot(n2, c_query[...]).astype(BF)
    cq[...] = query
    patches = mk.shape[0]
    lane = lanes(2 * patches)
    low = lane < patches
    sent = info[0:1, 0:1].astype(F32) * 16.0 + info[0:1, 128:129].astype(F32)
    known = jnp.full((1, 1), meta[2], jnp.int32).astype(F32)
    same = jnp.full((1, 1), meta[0] - meta[4], jnp.int32) == 0
    count = jnp.where(same, known, sent)
    valid = jnp.where(low, lane, lane - patches).astype(F32) < count
    for p in range(H // 2):
        keys = cross_pair(mk, p)
        values = cross_pair(mv, p)
        s = nt(query[:, 128 * p : 128 * p + 128], keys) * 0.125
        s = jnp.where(valid, s, NEGATIVE)
        m0 = jnp.max(jnp.where(low, s, NEGATIVE), axis=1, keepdims=True)
        m1 = jnp.max(jnp.where(low, NEGATIVE, s), axis=1, keepdims=True)
        e = jnp.exp(s - jnp.where(low, m0, m1))
        l0 = jnp.sum(jnp.where(low, e, 0.0), axis=1, keepdims=True)
        l1 = jnp.sum(jnp.where(low, 0.0, e), axis=1, keepdims=True)
        w = e / jnp.where(low, l0, l1)
        p2[p] = w
        o2[:, 128 * p : 128 * p + 128] = dot(w.astype(BF), values).astype(BF)
    second = first + dot(o2[...], c_out[...])
    y2[...] = second
    a3[...] = (second * inv_rms(second) * g_ffn[...]).astype(BF)


def ffn_kernel(
    row_blocks, meta, a3, cot, y2, g_ffn, wg, wu, wd,
    out, dy2, dy2b, gain, send, keep, acc, err, a3t, cott, dw, gu_buf, wd_buf, sems,
):
    core = meta[0]
    i, r = pl.program_id(0), pl.program_id(1)
    rows = pl.ds(pl.multiple_of(r * ROWS, ROWS), ROWS)
    first, last = i == 0, i == pl.num_programs(0) - 1

    @pl.when(first)
    def _():
        a3t[:, rows] = a3[...].astype(F32).T.astype(BF)
        cott[:, rows] = cot[...].astype(F32).T.astype(BF)
        acc[rows, :] = y2[...]
        err[rows, :] = jnp.zeros((ROWS, err.shape[1]), F32)

    gate = dot(a3[...], wg[...])
    up = dot(a3[...], wu[...])
    square = gate * gate
    th = jnp.tanh(0.7978845608028654 * gate * (1.0 + 0.044715 * square))
    more = 0.5 * (1.0 + th)
    act = gate * more
    slope = more + 0.5 * gate * (1.0 - th * th) * (
        0.7978845608028654 * (1.0 + 3 * 0.044715 * square)
    )
    hidden = (act * up).astype(BF)
    dh = nt(cot[...], wd[...])
    d_gate = (dh * up * slope).astype(BF)
    d_up = (dh * act).astype(BF)
    acc[rows, :] += dot(hidden, wd[...])
    err[rows, :] += nt(d_gate, wg[...]) + nt(d_up, wu[...])
    terms = (dot(a3t[:, rows], d_gate), dot(a3t[:, rows], d_up), dot(cott[:, rows], hidden))
    if row_blocks > 1:
        for n, term in enumerate(terms):
            dw[n] = jnp.where(r == 0, 0.0, dw[n]) + term
        terms = (dw[0], dw[1], dw[2])

    slot = lax.rem(i, 2)
    side = i // 2

    def gu_copy(dst):
        return pltpu.make_async_copy(gu_buf.at[slot], dst.at[side, pl.ds(0, 2)], sems.at[0, slot])

    def wd_copy(n, dst):
        return pltpu.make_async_copy(
            wd_buf.at[slot, n], dst.at[:, 2, pl.ds(2 * i, 2)], sems.at[1 + n, slot]
        )

    def drain(at):
        pltpu.make_async_copy(gu_buf.at[at], keep.at[0, pl.ds(0, 2)], sems.at[0, at]).wait()
        for n, dst in enumerate((send, keep)):
            pltpu.make_async_copy(
                wd_buf.at[at, n], dst.at[:, 2, pl.ds(0, 2)], sems.at[1 + n, at]
            ).wait()

    def put():
        pl.when(i >= 2)(lambda: drain(slot))
        width = terms[0].shape[1]
        for n in (0, 1):
            gu_buf[slot, n] = terms[n].astype(BF).reshape(8, terms[n].shape[0] // 8, width)
        down = terms[2].astype(BF)
        per, part, wide = down.shape[0] // 4, down.shape[0] // 8, width // 2
        for b in range(4):
            kept = jnp.where(core == b % 2, 1, 0)
            for y in range(2):
                piece = down[b * per : (b + 1) * per, y * wide : (y + 1) * wide]
                packed = jnp.concatenate([piece[:part], piece[part:]], 1)
                wd_buf[slot, kept, b // 2, y] = packed
        pl.when(slot == core)(lambda: gu_copy(keep).start())
        pl.when(slot != core)(lambda: gu_copy(send).start())
        wd_copy(0, send).start()
        wd_copy(1, keep).start()

        @pl.when(last)
        def _():
            drain(1 - slot)
            drain(slot)

    if row_blocks > 1:
        pl.when(r == row_blocks - 1)(put)
    else:
        put()

    @pl.when(last)
    def _():
        out[...] = acc[rows, :].astype(BF)
        back, gsum = norm_back(err[rows, :], y2[...], g_ffn[...])
        total = cot[...].astype(F32) + back
        dy2[...] = total
        dy2b[...] = total.astype(BF)
        gain[...] = jnp.where(r == 0, 0.0, gain[...]) + gsum


def cross_back_kernel(
    charts, patches_each, meta, dy2, dy2b, c_out, p2, mk, mv, cq, y1, g_cross, c_query, w_out,
    c_key_hbm, c_value_hbm,
    dcq, dmk, dmv, dy1, dy1b, do_keep, do_send, memg, gain, mk_acc, mv_acc, mem_scr, c_key, c_value, sems,
):
    core = meta[0]
    r = pl.program_id(0)
    half = do_keep.shape[1]
    patches = mk.shape[0]
    lane = lanes(2 * patches)
    low = lane < patches
    left = (lanes(128) < 64).astype(F32)
    do2 = nt(dy2b[...], c_out[...]).astype(BF)
    fresh = r == 0
    copies = [
        pltpu.make_async_copy(c_key_hbm, c_key, sems.at[0]),
        pltpu.make_async_copy(c_value_hbm, c_value, sems.at[1]),
    ]

    @pl.when(fresh)
    def _():
        for copy in copies:
            copy.start()

    for p in range(H // 2):
        at = slice(128 * p, 128 * p + 128)
        keys = cross_pair(mk, p)
        values = cross_pair(mv, p)
        w = p2[p]
        dp = nt(do2[:, at], values)
        prod = w * dp
        r0 = jnp.sum(jnp.where(low, prod, 0.0), axis=1, keepdims=True)
        r1 = jnp.sum(jnp.where(low, 0.0, prod), axis=1, keepdims=True)
        ds = w * (dp - jnp.where(low, r0, r1))
        dcq[:, at] = (dot(ds.astype(BF), keys) * 0.125).astype(BF)
        gk = dot(ds.T.astype(BF), cq[:, at]) * 0.125
        gv = dot(w.T.astype(BF), do2[:, at])
        gk = gk[:patches] * left + gk[patches:] * (1.0 - left)
        gv = gv[:patches] * left + gv[patches:] * (1.0 - left)
        mk_acc[:, at] = jnp.where(fresh, 0.0, mk_acc[:, at]) + gk
        mv_acc[:, at] = jnp.where(fresh, 0.0, mv_acc[:, at]) + gv
    err = nt(dcq[...], c_query[...])
    back, gsum = norm_back(err, y1[...], g_cross[...])
    total = dy2[...] + back
    dy1[...] = total
    tb = total.astype(BF)
    dy1b[...] = tb
    gain[...] = jnp.where(fresh, 0.0, gain[...]) + gsum
    do_keep[...] = nt(tb, w_out[pl.ds(pl.multiple_of(core * half, half), half), :]).astype(BF)
    rows = tb.shape[0]
    do_send[pl.ds(pl.multiple_of(r * rows, rows), rows), :] = nt(
        tb, w_out[pl.ds(pl.multiple_of((1 - core) * half, half), half), :]
    ).astype(BF)

    @pl.when(r == pl.num_programs(0) - 1)
    def _():
        gk, gv = mk_acc[...].astype(BF), mv_acc[...].astype(BF)
        for copy in copies:
            copy.wait()
        dmk[...] = gk
        dmv[...] = gv
        mem_scr[...] = nt(gk, c_key[...]) + nt(gv, c_value[...])

        def gather(parity):
            return jnp.concatenate(
                [
                    mem_scr[pl.ds(pl.multiple_of((2 * a + parity) * patches_each, 8), patches_each), :]
                    for a in range(charts)
                ],
                0,
            )

        memg[...] = gather(core)
        away = gather(1 - core).astype(BF)
        extra = away.shape[0]
        base = do_send.shape[0] - 2 * extra
        do_send[base : base + extra, :] = away[:, :half]
        do_send[base + extra :, :] = away[:, half:]


def square_kernel(meta, o2, dy2b, a2, dcq, mem, dmk, dmv, o1, dy1b, send, keep):
    core = meta[0]
    half = keep.shape[2]
    mine = pl.ds(pl.multiple_of(core * half, 128), half)
    other = pl.ds(pl.multiple_of((1 - core) * half, 128), half)
    memt = mem[...].astype(F32).T.astype(BF)
    pairs = ((o2, dy2b), (a2, dcq), (None, dmk), (None, dmv), (o1, dy1b))
    for n, (left, right) in enumerate(pairs):
        turned = memt if left is None else left[...].astype(F32).T.astype(BF)
        send[n] = dot(turned, right[:, other]).astype(BF)
        keep[n] = dot(turned, right[:, mine]).astype(BF)


def leave_kernel(
    split, charts, tokens, meta, a1, dq, dk, dv, wq, wk, wv, column, g_cross, g_ffn, *outs,
):
    half = dq.shape[1]
    size = dq.shape[0]
    width = g_ffn.shape[1]
    core, parity = meta[0], meta[4]
    cols = pl.ds(pl.multiple_of(core * half, 128), half)
    e_keep, e_send = outs[0], outs[1]
    out, scr = (outs[4], outs[5]) if split else (outs[2], outs[3])
    third = width // 3

    def rows_of(n):
        at = pl.ds(pl.multiple_of(n * third, third), third)
        turned = a1[:, at].astype(F32).T.astype(BF)
        gain = jnp.zeros((third, 1), F32)
        for m, (right, weight) in enumerate(((dq, wq), (dk, wk), (dv, wv))):
            block = dot(turned, right[...])
            gain += jnp.sum(block * weight[at, cols].astype(F32), axis=1, keepdims=True)
            out[at, m * half : (m + 1) * half] = block.astype(BF)
        gain = gain / column[at, :]
        stack = jnp.concatenate(
            [g_cross[:, at], g_ffn[:, at], jnp.zeros((126, third), F32)], 0
        ).T
        out[at, 3 * half :] = (jnp.where(lanes(128) == 2, gain, stack)).astype(BF)

    lax.fori_loop(0, 3, lambda n, c: (rows_of(n), c)[1], 0)
    if split:
        send, keep = outs[2], outs[3]
        part = width // 8
        for n in range(4):
            keep[n] = out[pl.ds(pl.multiple_of((2 * n + parity) * part, part), part), :]
            send[n] = out[pl.ds(pl.multiple_of((2 * n + 1 - parity) * part, part), part), :]
    step = scr.shape[0]
    per = step // (2 * tokens)

    def one(first):
        at = pl.ds(pl.multiple_of(first * step, step), step)
        scr[...] = (
            nt(dq[at, :], wq[:, cols]) + nt(dk[at, :], wk[:, cols]) + nt(dv[at, :], wv[:, cols])
        )
        for c in range(per):
            spot = pl.ds(pl.multiple_of((first * per + c) * tokens, tokens), tokens)
            e_keep[spot, :] = scr[pl.ds(pl.multiple_of((2 * c + core) * tokens, tokens), tokens), :]
            e_send[spot, :] = scr[
                pl.ds(pl.multiple_of((2 * c + 1 - core) * tokens, tokens), tokens), :
            ].astype(BF)

    lax.fori_loop(0, size // step, lambda g, c: (one(g), c)[1], 0)


def mix_kernel(meta, keep, recv, send1, kept1, send2, kept2):
    side, parity = meta[3], meta[4]
    rows = keep.shape[3]
    low = rows // 2

    def gu(x, w, s):
        return (keep[x, w, s].astype(F32) + recv[x, w, s].astype(F32)).astype(BF)

    def wd(x, s, part):
        return (keep[x, 2, s, part, :].astype(F32) + recv[x, 2, s, part, :].astype(F32)).astype(BF)

    for s in range(8):
        for x, to in ((1 - side, send1), (side, kept1)):
            to[s, :rows, :] = gu(x, 0, s)
            to[s, rows:, :] = wd(x, s, slice(0, low))
    for n in range(4):
        for x in range(2):
            for y, to in ((1 - parity, send2), (parity, kept2)):
                to[x, n, :rows, :] = gu(x, 1, 2 * n + y)
                to[x, n, rows:, :] = wd(x, 2 * n + y, slice(low, rows))


def input_grad_kernel(e_keep, e_recv, x, gain, dy1, out):
    err = e_keep[...] + e_recv[...].astype(F32)
    back, _ = norm_back(err, x[...].astype(F32), gain[...])
    out[...] = (dy1[...] + back).astype(BF)


def total(parts):
    result = parts[0].astype(F32)
    for part in parts[1:]:
        result = result + part.reshape(result.shape).astype(F32)
    return result


def tie(value, *deps):
    return lax.optimization_barrier((value, deps))[0]


def turn_in_kernel(meta, base, recv, send, keep):
    v, z = meta[5], meta[6]
    send[z] = base[z, 1 - v]
    send[1 - z] = recv[1 - v]
    keep[z] = base[z, v]
    keep[1 - z] = recv[v]


def gather_kernel(meta, keep, recv, out):
    v = meta[5]
    for n in range(2):
        out[n, v] = keep[n]
        out[n, 1 - v] = recv[n]


def finish_kernel(tokens, got, first, few):
    for n in range(got.shape[0]):
        first[n] = got[n, :tokens, :].astype(F32)
        few[n] = got[n, tokens:, :].astype(F32)


def place_kernel(charts, meta, *refs):
    place = meta[1]
    out = refs[-1]
    for d in range(charts):
        out[lax.rem(place - d + charts, charts)] = refs[d][...].astype(out.dtype)


def local(
    nseq, inputs, memory, patch_count, cotangent, norm_self, w_query, w_key, w_value, w_out,
    norm_cross, c_query, c_key, c_value, c_out, norm_ffn, w_gate, w_up, w_down,
):
    charts, tokens, width = inputs.shape
    patches_each = memory.shape[1]
    size = charts * 2 * tokens
    own = charts * tokens
    patches = patches_each * nseq
    half = width // 2
    small = size <= 1024
    hidden = w_gate.shape[1]
    blocks = own // ROWS
    dp = lax.axis_index("dp")
    seq = lax.axis_index("seq")
    side, core = dp // 2, lax.rem(dp, 2)
    place, parity = seq // 2, lax.rem(seq, 2)

    def shift(d):
        return [
            ((2 * x + k) * nseq + 2 * a + b, (2 * x + b) * nseq + 2 * ((a + d) % charts) + k)
            for x in range(2)
            for k in range(2)
            for a in range(charts)
            for b in range(2)
        ]

    def dp_perm(rule):
        return [(2 * x + k, 2 * rule(x, k)[0] + rule(x, k)[1]) for x in range(2) for k in range(2)]

    swap_core = dp_perm(lambda x, k: (x, 1 - k))
    swap_side = dp_perm(lambda x, k: (1 - x, k))

    def across(value):
        return lax.ppermute(value, "dp", swap_core)

    def travel(value, d):
        return lax.ppermute(value, ("dp", "seq"), shift(d))

    def pick(value, d):
        return lax.dynamic_index_in_dim(value, lax.rem(place + d, charts), 0, keepdims=False)

    gain_self, gain_cross, gain_ffn = (g.reshape(1, width) for g in (norm_self, norm_cross, norm_ffn))
    count = lax.dynamic_index_in_dim(patch_count, place, 0, keepdims=False)
    meta = jnp.stack(
        [core, place, count, side, parity, lax.rem(place, 2), place // 2]
    ).astype(jnp.int32)

    trade = [
        ((2 * x + k) * nseq + 2 * a + b, (2 * x + b) * nseq + 2 * a + k)
        for x in range(2)
        for k in range(2)
        for a in range(charts)
        for b in range(2)
    ]
    flips = {
        name: [(s, s ^ (1 << bit)) for s in range(nseq)] for bit, name in enumerate("yvz")
    }
    low_bit, high_bit = lax.rem(place, 2), place // 2

    mine = jnp.stack(
        [
            travel(jnp.concatenate([pick(inputs, d), pick(memory, d)], 0), d)
            for d in range(charts)
        ]
    )
    theirs = across(mine)
    if small:
        cot_base = lax.ppermute(cotangent, ("dp", "seq"), trade)
        cot_base = cot_base.reshape(2, 2, tokens, width)
        cot_away = lax.dynamic_index_in_dim(cot_base, 1 - high_bit, 0, keepdims=False)
        cot_got = lax.ppermute(cot_away, "seq", flips["z"])
        theirs = tie(theirs, cot_away)
    else:
        cot_parts = [travel(pick(cotangent, d), d) for d in range(charts)]
    pairs = half // 128
    pair_spec = pl.BlockSpec((size, 128), lambda p, m: (0, p))
    own_spec = pl.BlockSpec((own, 128), lambda p, m: (0, p))
    aug_spec = pl.BlockSpec((2, size, 128), lambda p, m: (p, 0, 0))
    far = pltpu.HBM if small else sds
    x_own, a1, k, v, mem, mk, mv, o_keep, o_send, o_nat, q_aug = pl.pallas_call(
        functools.partial(enter_kernel, small, charts, tokens, patches_each),
        compiler_params=room(small, 24),
        out_shape=(
            sds((own, width), BF), far((size, width), BF), far((size, half), BF),
            far((size, half), BF), sds((patches, width), BF), sds((patches, width), BF),
            sds((patches, width), BF), sds((own, half), BF), sds((own + 16, half), BF),
            far((size, half), BF), far((2 * pairs, size, 128), BF),
        ),
        in_specs=[SM] + [VM] * 3 + [pl.BlockSpec(memory_space=pltpu.HBM)] * 5,
        out_specs=([VM] + [HB] * 3 + [VM] * 6 + [HB]) if small else [VM] * 11,
        scratch_shapes=[
            pltpu.VMEM((patches, width), F32), pltpu.VMEM((size, half), BF),
            pltpu.VMEM((width, half), BF), pltpu.VMEM((width, half), BF),
            pltpu.VMEM((width, half), BF), pltpu.VMEM((width, width), BF),
            pltpu.VMEM((width, width), BF), pltpu.SemaphoreType.DMA((5,)),
        ]
        + (
            [
                pltpu.VMEM((size, width), BF), pltpu.VMEM((size, half), BF),
                pltpu.VMEM((size, half), BF), pltpu.VMEM((2 * pairs, size, 128), BF),
                pltpu.SemaphoreType.DMA((3,)), pltpu.SemaphoreType.DMA((pairs,)),
            ]
            if small
            else []
        ),
        cost_estimate=cost(2 * size * width * 3 * half, mine, theirs, w_query, w_key, w_value),
    )(
        meta, mine, theirs, gain_self,
        *(
            pltpu.with_memory_space_constraint(w, pltpu.HBM)
            for w in (w_query, w_key, w_value, c_key, c_value)
        ),
    )
    if small:
        part = sds((2, tokens, width), BF)
        cot_send, cot_keep = pl.pallas_call(
            turn_in_kernel,
            compiler_params=room(small, 6),
            out_shape=(part, part),
            in_specs=[SM, VM, VM],
            out_specs=[VM] * 2,
        )(meta, cot_base, cot_got)
        cot_got = lax.ppermute(cot_send, "seq", flips["v"])
        o_recv = tie(across(o_send), cot_send)
    else:
        o_recv = across(o_send)

    each = ROWS if small else QB
    row_spec = pl.BlockSpec((each, width), lambda r: (r, 0))
    half_spec = pl.BlockSpec((each, half), lambda r: (r, 0))
    p2_spec = pl.BlockSpec((H // 2, each, 2 * patches), lambda r: (0, r, 0))

    def fixed(shape, spaces=1):
        if spaces == 1:
            return pl.BlockSpec(shape, lambda r: (0,) * len(shape))
        return pl.BlockSpec(shape, lambda i, r: (0,) * len(shape))

    square = fixed((width, width))
    one_row = fixed((1, width))
    patch_spec = fixed((patches, width))
    rows_f = sds((own, width), F32)
    rows_b = sds((own, width), BF)
    o1, y1, a2, cq, p2, o2, y2, a3 = pl.pallas_call(
        cross_kernel,
        compiler_params=room(small, 16),
        out_shape=(
            rows_b, rows_f, rows_b, rows_b, sds((H // 2, own, 2 * patches), F32), rows_b, rows_f,
            rows_b,
        ),
        grid=(own // each,),
        in_specs=[
            SM, row_spec, half_spec, half_spec, pl.BlockSpec((16, half), lambda r: (own // 16, 0)),
            square, one_row, square, patch_spec, patch_spec, square, one_row,
        ],
        out_specs=[row_spec] * 4 + [p2_spec] + [row_spec] * 3,
        cost_estimate=cost(6 * own * width * width, w_out, c_query, c_out, rows_f, rows_f),
    )(meta, x_own, o_keep, o_recv, o_recv, w_out, gain_cross, c_query, mk, mv, c_out, gain_ffn)

    def placed(parts, dtype):
        return pl.pallas_call(
            functools.partial(place_kernel, charts),
            compiler_params=room(small, 6),
            out_shape=sds((charts,) + parts[0].shape, dtype),
            in_specs=[SM] + [VM] * charts,
            out_specs=VM,
        )(meta, *parts)

    if small:
        cot = pl.pallas_call(
            gather_kernel,
            compiler_params=room(small, 6),
            out_shape=sds((2, 2, tokens, width), BF),
            in_specs=[SM, VM, VM],
            out_specs=VM,
        )(meta, cot_keep, tie(cot_got, y2)).reshape(own, width)
    else:
        cot = placed(cot_parts, BF).reshape(own, width)
    wide = hidden // 4
    last = 3
    f_pack = sds((2, 3, 8, width // 8, wide), BF)
    anywhere = pl.BlockSpec(memory_space=pl.ANY)
    frow = pl.BlockSpec((ROWS, width), lambda i, r: (r, 0))
    lrow = pl.BlockSpec((ROWS, width), lambda i, r: (r * (i // last), 0))
    out_b, dy2, dy2b, ffn_gain, f_send, f_keep = pl.pallas_call(
        functools.partial(ffn_kernel, blocks),
        compiler_params=room(small, 30),
        out_shape=(rows_b, rows_f, rows_b, sds((1, width), F32), f_pack, f_pack),
        grid=(4, blocks),
        in_specs=[
            SM, frow, frow, frow, fixed((1, width), 2),
            pl.BlockSpec((width, wide), lambda i, r: (0, i)),
            pl.BlockSpec((width, wide), lambda i, r: (0, i)),
            pl.BlockSpec((wide, width), lambda i, r: (i, 0)),
        ],
        out_specs=[lrow, lrow, lrow, fixed((1, width), 2), anywhere, anywhere],
        scratch_shapes=[
            pltpu.VMEM((own, width), F32), pltpu.VMEM((own, width), F32),
            pltpu.VMEM((width, own), BF), pltpu.VMEM((width, own), BF),
            pltpu.VMEM((3, width, wide) if blocks > 1 else (3, 8, 128), F32),
            pltpu.VMEM((2, 2, 8, width // 8, wide), BF),
            pltpu.VMEM((2, 2, 2, 2, width // 8, wide), BF), pltpu.SemaphoreType.DMA((3, 2)),
        ],
        cost_estimate=cost(18 * own * width * hidden, w_gate, w_up, w_down, rows_f, rows_f),
    )(meta, a3, cot, y2, gain_ffn, w_gate, w_up, w_down)
    f_recv = across(f_send)

    def back_first(rows):
        return lax.ppermute(rows, ("dp", "seq"), trade)

    def back_second(rows):
        base = rows.reshape((2, 2) + rows.shape[1:])
        away = lax.dynamic_index_in_dim(base, 1 - high_bit, 0, keepdims=False)
        return base, lax.ppermute(away, "seq", flips["z"])

    def back_turn(base, got):
        return pl.pallas_call(
            turn_in_kernel,
            compiler_params=room(small, 6),
            out_shape=(sds(got.shape, BF), sds(got.shape, BF)),
            in_specs=[SM, VM, VM],
            out_specs=[VM] * 2,
        )(meta, base, got)

    def gathered(keep, got):
        return pl.pallas_call(
            gather_kernel,
            compiler_params=room(small, 6),
            out_shape=sds((2, 2) + got.shape[1:], BF),
            in_specs=[SM, VM, VM],
            out_specs=VM,
        )(meta, keep, got).reshape((charts,) + got.shape[1:])

    def back_last(got):
        return pl.pallas_call(
            functools.partial(finish_kernel, tokens),
            compiler_params=room(small, 8),
            out_shape=(
                sds((charts, tokens, width), F32), sds((charts, patches_each, width), F32),
            ),
            in_specs=[VM],
            out_specs=[VM] * 2,
        )(got)

    def halve(which, keep, recv, outer):
        parts = (keep if isinstance(keep, list) else [keep]) + [recv]
        size_now, wide_now = parts[0].size, parts[0].shape[-1]
        shape = (outer, 2, size_now // (outer * 2 * wide_now), wide_now)
        parts = [p.reshape(shape) for p in parts]
        i = meta[which]
        sends = [lax.dynamic_index_in_dim(p, 1 - i, 1, keepdims=False) for p in parts]
        kept = [lax.dynamic_index_in_dim(p, i, 1, keepdims=False) for p in parts]
        return total(sends).astype(BF), kept

    def over(name, value):
        if name == "x":
            return lax.ppermute(value, "dp", swap_side)
        return lax.ppermute(value, "seq", flips[name])

    out_rows = out_b.reshape(charts, tokens, width)
    if small:
        out_base, out_got = back_second(out_rows)
    else:
        out_parts = [travel(pick(out_rows, d), d) for d in range(charts)]
    dcq, dmk, dmv, dy1, dy1b, do_keep, do_send, memg, cross_gain = pl.pallas_call(
        functools.partial(cross_back_kernel, charts, patches_each),
        compiler_params=room(small, 18),
        out_shape=(
            rows_b, sds((patches, width), BF), sds((patches, width), BF), rows_f, rows_b,
            sds((own, half), BF), sds((own + patches, half), BF),
            sds((patches // 2, width), F32), sds((1, width), F32),
        ),
        grid=(own // each,),
        in_specs=[
            SM, row_spec, row_spec, square, p2_spec, patch_spec, patch_spec, row_spec, row_spec,
            one_row, square, square, HB, HB,
        ],
        out_specs=[
            row_spec, patch_spec, patch_spec, row_spec, row_spec, half_spec,
            fixed((own + patches, half)), fixed((patches // 2, width)), one_row,
        ],
        scratch_shapes=[pltpu.VMEM((patches, width), F32)] * 3
        + [pltpu.VMEM((width, width), BF)] * 2
        + [pltpu.SemaphoreType.DMA((2,))],
        cost_estimate=cost(6 * own * width * width, w_out, c_query, c_out, rows_f, rows_f),
    )(meta, dy2, dy2b, c_out, p2, mk, mv, cq, y1, gain_cross, c_query, w_out, c_key, c_value)
    do_recv = across(do_send)

    if small:
        f1 = sds((8, 3 * width // 16, wide), BF)
        f2 = sds((2, 4, 3 * width // 16, wide), BF)
        f1_send, f1_keep, f2_send, f2_keep = pl.pallas_call(
            mix_kernel,
            compiler_params=room(small, 16),
            out_shape=(f1, f1, f2, f2),
            in_specs=[SM] + [VM] * 2,
            out_specs=[VM] * 4,
        )(meta, f_keep, f_recv)
        f1_recv, f2_recv = over("x", f1_send), over("y", f2_send)
        dcq = tie(dcq, f1_send)
    s_send, s_keep = pl.pallas_call(
        square_kernel,
        compiler_params=room(small, 16),
        out_shape=(sds((5, width, half), BF), sds((5, width, half), BF)),
        in_specs=[SM] + [VM] * 9,
        out_specs=[VM] * 2,
        cost_estimate=cost(6 * own * width * width, o1, o2, a2, dcq, dy2b, dy1b),
    )(meta, o2, dy2b, a2, dcq, mem, dmk, dmv, o1, dy1b)
    s_recv = across(s_send)

    few = patches // 2
    memg_recv = jnp.concatenate([do_recv[own : own + few], do_recv[own + few :]], 1)
    memg_own = (memg + memg_recv.astype(F32)).astype(BF).reshape(charts, patches_each, width)
    if small:
        s_send, s_keep = halve(5, s_keep, s_recv, 10)
        s_recv = over("v", s_send)
        do_recv = tie(do_recv, s_send)

    dq, dk, dv = pl.pallas_call(
        functools.partial(attend_back_kernel, tokens),
        compiler_params=room(small, 14),
        out_shape=(sds((size, half), BF),) * 3,
        grid_spec=pltpu.PrefetchScalarGridSpec(
            num_scalar_prefetch=1,
            grid=(pairs,),
            in_specs=[aug_spec, pair_spec, pair_spec, pair_spec, own_spec, own_spec],
            out_specs=[pair_spec] * 3,
            scratch_shapes=[
                pltpu.VMEM((2, size, 128), BF), pltpu.VMEM((2, size, 128), BF),
                pltpu.VMEM((128, size), BF),
                pltpu.VMEM((2, size, 128), F32), pltpu.VMEM((2, size, 128), F32),
            ],
        ),
        cost_estimate=cost(10 * size * size * half, k, v, q_aug),
    )(meta, q_aug, k, v, o_nat, do_keep, do_recv)

    if small:
        dq = tie(dq, f1_recv, f2_recv, out_got)
    t_whole = sds((width, 3 * half + 128), BF)
    t_piece = sds((4, width // 8, 3 * half + 128), BF)
    gone = pl.pallas_call(
        functools.partial(leave_kernel, small, charts, tokens),
        compiler_params=room(small, 14),
        out_shape=(rows_f, rows_b) + ((t_piece, t_piece) if small else (t_whole,)),
        in_specs=[SM] + [VM] * 10,
        out_specs=[VM] * (4 if small else 3),
        scratch_shapes=([pltpu.VMEM((width, 3 * half + 128), BF)] if small else [])
        + [pltpu.VMEM((256, width), F32)],
    )(
        meta, a1, dq, dk, dv, w_query, w_key, w_value, norm_self.reshape(width, 1), cross_gain,
        ffn_gain,
    )
    e_keep, e_send = gone[:2]
    e_recv = across(e_send)
    if small:
        t_send, t_keep = gone[2:]
        t_recv = over("y", t_send)
        e_recv = tie(e_recv, t_send)
    else:
        t_out = gone[2]

    in_grad = pl.pallas_call(
        input_grad_kernel,
        compiler_params=room(small, 8),
        out_shape=rows_b,
        in_specs=[VM] * 5,
        out_specs=VM,
        cost_estimate=cost(20 * own * width, e_keep, e_send, x_own, dy1),
    )(e_keep, e_recv, x_own, gain_self, dy1)
    in_rows = jnp.concatenate([in_grad.reshape(charts, tokens, width), memg_own], 1)
    if small:
        in_base, in_got = back_second(in_rows)
        out_send, out_keep = back_turn(out_base, tie(out_got, in_base))
        out_got = lax.ppermute(out_send, "seq", flips["v"])
        f2_send, f2_keep = halve(3, f2_keep, tie(f2_recv, out_send), 1)
        f2_recv = over("x", f2_send)
        s_send, s_keep = halve(3, s_keep, tie(s_recv, f2_send), 20)
        s_recv = over("x", s_send)
        t_send, t_keep = halve(3, t_keep, tie(t_recv, s_send), 4)
        t_recv = over("x", t_send)
        f2_send, f2_keep = halve(5, f2_keep, tie(f2_recv, t_send), 2)
        f2_recv = over("v", f2_send)
        f1_send, f1_keep = halve(4, f1_keep, tie(f1_recv, f2_send), 4)
        f1_recv = over("y", f1_send)
        in_send, in_keep = back_turn(in_base, tie(in_got, f1_send))
        in_got = lax.ppermute(in_send, "seq", flips["v"])
        s_send, s_keep = halve(4, s_keep, tie(s_recv, in_send, f2_recv), 10)
        s_recv = over("y", s_send)
        out_rows = gathered(out_keep, tie(out_got, s_send))
        out_mid = out_rows
        out_rows = back_first(out_rows)
        t_send, t_keep = halve(5, t_keep, tie(t_recv, out_mid), 2)
        t_recv = over("v", t_send)
        f1_send, f1_keep = halve(5, f1_keep, tie(f1_recv, t_send), 2)
        f1_recv = over("v", f1_send)
        t_send, t_keep = halve(6, t_keep, tie(t_recv, f1_send, s_recv), 1)
        t_recv = over("z", t_send)
        s_send, s_keep = halve(6, s_keep, tie(s_recv, t_send), 5)
        s_recv = over("z", s_send)
        in_rows = gathered(in_keep, tie(in_got, s_send))
        in_mid = in_rows
        in_rows = back_first(in_rows)
        f1_send, f1_keep = halve(6, f1_keep, tie(f1_recv, in_mid), 1)
        f1_recv = over("z", f1_send)
        f2_send, f2_keep = halve(6, f2_keep, tie(f2_recv, f1_send), 1)
        f2_recv = over("z", f2_send)
    else:
        in_parts = [travel(pick(in_rows, d), d) for d in range(charts)]

    if small:
        t_part = total(t_keep + [t_recv]).reshape(width // 16, 3 * half + 128)
        t_zero = jnp.zeros_like(t_part)
        t_sum = jnp.concatenate(
            [jnp.where(side == 0, t_part, t_zero), jnp.where(side == 0, t_zero, t_part)], 0
        )
        s_part = total(s_keep + [s_recv])
        s_zero = jnp.zeros_like(s_part)
        s_sum = jnp.concatenate(
            [jnp.where(side == 0, s_part, s_zero), jnp.where(side == 0, s_zero, s_part)], 1
        )
    else:

        def over_seq(value, axis):
            return lax.psum_scatter(
                value.astype(BF), "seq", scatter_dimension=axis, tiled=True
            ).astype(F32)

        def over_side(parts):
            sends = [lax.dynamic_index_in_dim(p, 1 - side, 0, keepdims=False) for p in parts]
            kept = [lax.dynamic_index_in_dim(p, side, 0, keepdims=False) for p in parts]
            return total(kept + [lax.ppermute(total(sends).astype(BF), "dp", swap_side)])

        f_all = over_side([f_keep, f_recv])
        g_two = over_seq(f_all[:2].reshape(2, width, wide), 1)
        g_gate, g_up = g_two[0], g_two[1]
        down = f_all[2].reshape(8, width // 8, 2, wide // 2)
        g_down = over_seq(down.transpose(0, 3, 2, 1).reshape(hidden, width // 4), 0)
        s_sum = over_seq(total([s_keep, s_recv]), 1)
        t_sum = over_seq(t_out, 0)

    rows = t_sum.shape[0]
    quarter = half // 2
    t_sum = t_sum.astype(BF)
    squares = jnp.concatenate(
        [t_sum[:, : 3 * half].reshape(rows, 3, half).transpose(1, 0, 2), s_sum.astype(BF)], 0
    ).reshape(8, rows, 2, quarter)
    gains = t_sum[:, 3 * half :]
    padded = jnp.pad(gains, ((0, 0), (0, quarter - 128)))[None]

    def deliver(block, rule):
        part = lax.dynamic_index_in_dim(squares, block, 2, keepdims=False)
        return lax.ppermute(jnp.concatenate([part, padded], 0), "dp", dp_perm(rule)).astype(F32)

    done = deliver(side, lambda x, k: (k, x)) + deliver(1 - side, lambda x, k: (k, 1 - x))
    if small:
        f1_recv, f2_recv = tie((f1_recv, f2_recv), done)
        f1_sum = total(f1_keep + [f1_recv]).reshape(3 * width // 16, wide)
        f2_sum = total(f2_keep + [f2_recv]).reshape(3 * width // 16, wide)
        g_gate, g_up = f1_sum[: width // 8], f2_sum[: width // 8]
        g_down = jnp.concatenate([f1_sum[width // 8 :], f2_sum[width // 8 :]], 0)
        g_down = g_down.reshape(width // 8, 2, wide // 2).transpose(2, 1, 0)
        g_down = g_down.reshape(wide // 2, width // 4)
    rest = lax.ppermute(gains, "dp", dp_perm(lambda x, k: (1 - k, x))).astype(F32) + lax.ppermute(
        gains, "dp", dp_perm(lambda x, k: (1 - k, 1 - x))
    ).astype(F32)
    gain_sum = done[8, :, :128] + rest

    if small:
        in_all, few_all = back_last(in_rows)
        out_all = out_rows.astype(F32)
    else:
        out_all, in_all = placed(out_parts, F32), placed(in_parts, F32)
        in_all, few_all = in_all[:, :tokens], in_all[:, tokens:]
    return (
        out_all,
        in_all,
        few_all,
        gain_sum[:, 2],
        done[0],
        done[1],
        done[2],
        done[7],
        gain_sum[:, 0],
        done[4],
        done[5],
        done[6],
        done[3],
        gain_sum[:, 1],
        g_gate,
        g_up,
        g_down,
    )


def solution(mesh):
    tok = P("dp", "seq", None)
    cut = P("seq", "dp")
    in_specs = (tok, tok, P("dp"), tok) + (P(),) * 14
    out_specs = (tok, tok, tok, P("seq"), cut, cut, cut, cut, P("seq"), cut, cut, cut, cut)
    out_specs += (P("seq"), cut, cut, cut)
    return jax.shard_map(
        functools.partial(local, mesh.shape["seq"]),
        mesh=mesh,
        in_specs=in_specs,
        out_specs=out_specs,
        check_vma=False,
    )
```
